32 devices in a mesh: shard: 4 (over z), ctx: 4 (over y, x), tensor: 2 (over core).
Axes of the slice: x: 2, y: 2, z: 4, core: 2. Of those that a mesh axis runs over, the one named last changes fastest.
Arguments:
- inputs: bfloat16 [2, 1280, 1472], P(None, ('shard', 'ctx')), may hold values from -6 to 6
- cotangent: bfloat16 [2, 1280, 1472], P(None, ('shard', 'ctx')), may hold values from -6 to 6
- norm1_gain: bfloat16 [1472], P('shard'), may hold values from 0.099609375 to 1.8984375
- w_query: bfloat16 [1472, 384], P('shard', 'tensor'), may hold values from -0.0390625 to 0.0390625
- w_key: bfloat16 [1472, 384], P('shard', 'tensor'), may hold values from -0.15625 to 0.15625
- w_value: bfloat16 [1472, 384], P('shard', 'tensor'), may hold values from -0.15625 to 0.15625
- w_out: bfloat16 [384, 1472], P('tensor', 'shard'), may hold values from -1.25 to 1.25
- norm2_gain: bfloat16 [1472], P('shard'), may hold values from 0.099609375 to 1.8984375
- w_gate: bfloat16 [1472, 3584], P('shard', 'tensor'), may hold values from -0.15625 to 0.15625
- w_up: bfloat16 [1472, 3584], P('shard', 'tensor'), may hold values from -0.15625 to 0.15625
- w_down: bfloat16 [3584, 1472], P('tensor', 'shard'), may hold values from -0.1875 to 0.1875
- bias_table: float32 [32, 6], replicated, may hold values from -4 to 4
Outputs:
- output: bfloat16 [2, 1280, 1472], P(None, ('shard', 'ctx'))
- input_grad: bfloat16 [2, 1280, 1472], P(None, ('shard', 'ctx'))
- norm1_gain_grad: float32 [1472], P('shard')
- w_query_grad: float32 [1472, 384], P('shard', 'tensor')
- w_key_grad: float32 [1472, 384], P('shard', 'tensor')
- w_value_grad: float32 [1472, 384], P('shard', 'tensor')
- w_out_grad: float32 [384, 1472], P('tensor', 'shard')
- norm2_gain_grad: float32 [1472], P('shard')
- w_gate_grad: float32 [1472, 3584], P('shard', 'tensor')
- w_up_grad: float32 [1472, 3584], P('shard', 'tensor')
- w_down_grad: float32 [3584, 1472], P('tensor', 'shard')
The draws below stay inside these ranges and needn't reach their ends.
All inputs are finite; a program needn't handle non-finite values.
Results may differ from the reference program's by a relative error of at most 0.024.
Values may be sent and summed in bfloat16 or wider, within the bound.
No kernel may reach another device: no remote copies, remote signals or barrier semaphores. Data moves between devices by JAX's collectives and lax.ppermute only.
A program may use at most 128 MiB of HBM per device.

```python
from functools import partial
import jax
import jax.numpy as jnp
from jax import lax

D = 1472
HEADS = 6
DK = 64
FF = 3584
BUCKETS = 32
SEG = 16
MICRO = 2
TOKENS_MB = 1280


def shard_levels(stream_key, dims, split, low, top_value):
    level = 1.0
    for position, blocks in split:
        heights = jax.random.uniform(jax.random.fold_in(jax.random.fold_in(stream_key, 6), position), (blocks,), jnp.float32, low / len(split), top_value / len(split))
        level = level * jnp.repeat(jnp.exp(heights), dims[position] // blocks).reshape((-1,) + (1,) * (len(dims) - 1 - position))
    return level


def normal_values(own_key, extent, width, limit, pieces=(), kind=jnp.bfloat16):
    entries = jax.random.normal(own_key, extent, jnp.float32) * width
    if len(pieces) > 0:
        entries = shard_levels(own_key, extent, pieces, -0.22, 0.18) * entries
    return jnp.clip(entries, min=-limit, max=limit).astype(kind)


def setup_inputs(seed: int = 0) -> dict:
    key_list = jax.random.split(jax.random.key(seed), 13)
    return {
        "inputs": normal_values(key_list[0], (MICRO, TOKENS_MB, D), 1.0, 6.0, ((1, 16),)),
        "cotangent": normal_values(key_list[1], (MICRO, TOKENS_MB, D), 1.0, 6.0, ((1, 16),)),
        "norm1_gain": jnp.clip(1.0 + 0.18 * jax.random.normal(key_list[2], (D,), jnp.float32), 0.099609375, 1.8984375).astype(jnp.bfloat16),
        "w_query": normal_values(key_list[3], (D, HEADS * DK), (16 * D) ** -0.5, 0.0390625, ((0, 4), (1, 2))),
        "w_key": normal_values(key_list[4], (D, HEADS * DK), D ** -0.5, 0.15625, ((0, 4), (1, 2))),
        "w_value": normal_values(key_list[5], (D, HEADS * DK), D ** -0.5, 0.15625, ((0, 4), (1, 2))),
        "w_out": normal_values(key_list[6], (HEADS * DK, D), (HEADS * DK // 16) ** -0.5, 1.25, ((0, 2), (1, 4))),
        "norm2_gain": jnp.clip(1.0 + 0.18 * jax.random.normal(key_list[7], (D,), jnp.float32), 0.099609375, 1.8984375).astype(jnp.bfloat16),
        "w_gate": normal_values(key_list[8], (D, FF), D ** -0.5, 0.15625, ((0, 4), (1, 2))),
        "w_up": normal_values(key_list[9], (D, FF), D ** -0.5, 0.15625, ((0, 4), (1, 2))),
        "w_down": normal_values(key_list[10], (FF, D), (FF // 4) ** -0.5, 0.1875, ((0, 2), (1, 4))),
        "bias_table": normal_values(key_list[11], (BUCKETS, HEADS), 1.0, 4.0, (), jnp.float32),
    }


norm_eps = 1e-06
distance_marks = (8, 12, 16, 23, 32, 46, 64, 91)
masked_score = -1e+30

@jax.custom_vjp
def low(v):
    return lax.optimization_barrier(v.astype(jnp.bfloat16)).astype(jnp.float32)

@jax.custom_vjp
def low_back(v):
    return v

def low_keep(v):
    return (low(v), None)

def low_pass(kept, grad):
    return (grad,)

def back_keep(v):
    return (v, None)

def back_low(kept, grad):
    return (low(grad),)
low.defvjp(low_keep, low_pass)
low_back.defvjp(back_keep, back_low)

def matmul_high(left, right):
    return jnp.dot(left, right, precision=lax.Precision.HIGHEST, preferred_element_type=jnp.float32)

def path_info(token, seg_len):
    segment = jnp.where(token < 8 * seg_len, 0, jnp.where(token < 12 * seg_len, (token - 8 * seg_len) // seg_len + 1, (token - 12 * seg_len) // seg_len + 5))
    parent = jnp.where(segment == 0, -1, jnp.where(segment <= 4, 0, (segment - 5) // 2 + 1))
    place = token - jnp.where(segment == 0, 0, jnp.where(segment <= 4, (segment - 1) * seg_len, (segment - 2) * seg_len))
    return (segment, parent, place)

def bucket_of(relative):
    magnitude = jnp.abs(relative)
    marked = sum(((magnitude >= mark).astype(jnp.int32) for mark in distance_marks))
    return jnp.where(relative > 0, 16, 0) + jnp.where(magnitude < 8, magnitude, 7 + marked)

def score_bias(query_token, key_token, table, seg_len):
    query_seg, query_parent, query_place = path_info(query_token, seg_len)
    key_seg, key_parent, key_place = path_info(key_token, seg_len)
    allowed = (key_seg[None, :] == 0) | (key_seg[None, :] == query_seg[:, None]) | (key_seg[None, :] == query_parent[:, None])
    bucket = bucket_of(key_place[None, :] - query_place[:, None]).astype(jnp.int32)
    looked = jnp.stack([jnp.take(table[:, head], bucket, axis=0) for head in range(table.shape[1])])
    return jnp.where(allowed[None], looked, masked_score)

def rms_scale(values_in, gain):
    return values_in * lax.rsqrt(lax.optimization_barrier(jnp.mean(values_in * values_in, axis=-1, keepdims=True)) + norm_eps) * gain

def tree_layer(table, params, tree_in):
    gain_one, w_query, w_key, w_value, w_out, gain_two, w_gate, w_up, w_down = params
    length = tree_in.shape[0]
    block_len = 5 * SEG
    normed_one = low(rms_scale(tree_in, gain_one))
    queries = low_back(low(matmul_high(normed_one, w_query)))
    keys = low_back(low(matmul_high(normed_one, w_key)))
    values = low_back(low(matmul_high(normed_one, w_value)))
    key_heads = keys.reshape(length, HEADS, DK)
    value_heads = values.reshape(length, HEADS, DK)
    query_sets = queries.reshape(length // block_len, block_len, HEADS, DK)
    starts = jnp.arange(length // block_len, dtype=jnp.int32) * block_len
    key_token = jnp.arange(length, dtype=jnp.int32)

    def attend_block(block):
        query_block, start = block
        query_token = start + jnp.arange(block_len, dtype=jnp.int32)
        scores = jnp.einsum('qhd,khd->hqk', query_block, key_heads, precision=lax.Precision.HIGHEST)
        scores = low_back(scores + score_bias(query_token, key_token, table, SEG))
        attention = low(jax.nn.softmax(scores, axis=-1))
        return jnp.einsum('hqk,khd->qhd', attention, value_heads, precision=lax.Precision.HIGHEST)
    mixed = lax.map(jax.checkpoint(attend_block), (query_sets, starts)).reshape(length, HEADS * DK)
    mixed = low_back(low(mixed))
    middle = tree_in + low_back(matmul_high(mixed, w_out))
    normed_two = low(rms_scale(middle, gain_two))
    gate_pre = low_back(matmul_high(normed_two, w_gate))
    up_pre = low_back(matmul_high(normed_two, w_up))
    hidden = low(jax.nn.gelu(gate_pre, approximate=True) * up_pre)
    return middle + low_back(matmul_high(hidden, w_down))

def reference(inputs, cotangent, norm1_gain, w_query, w_key, w_value, w_out, norm2_gain, w_gate, w_up, w_down, bias_table):
    params = tuple((weight.astype(jnp.float32) for weight in (norm1_gain, w_query, w_key, w_value, w_out, norm2_gain, w_gate, w_up, w_down)))
    table = bias_table.astype(jnp.float32)

    def forward(inputs_f, gain_one, wq_f, wk_f, wv_f, wo_f, gain_two, wg_f, wu_f, wd_f):
        layer_params = (gain_one, wq_f, wk_f, wv_f, wo_f, gain_two, wg_f, wu_f, wd_f)
        tree_blocks = inputs_f.reshape(-1, 20 * SEG, D)
        layer_fn = jax.checkpoint(partial(tree_layer, table, layer_params))
        return lax.map(layer_fn, tree_blocks).reshape(inputs_f.shape)
    outputs, pull = jax.vjp(forward, inputs.astype(jnp.float32), *params)
    grads = pull(cotangent.astype(jnp.float32))
    return (outputs.astype(jnp.bfloat16), grads[0].astype(jnp.bfloat16), grads[1], grads[2], grads[3], grads[4], grads[5], grads[6], grads[7], grads[8], grads[9])
```

```python
import jax
import jax.numpy as jnp
from jax import lax
from jax.sharding import PartitionSpec as P

DK = 64
norm_eps = 1e-06
distance_marks = (8, 12, 16, 23, 32, 46, 64, 91)
masked_score = -1e30
low = jnp.bfloat16
wide = jnp.float32


def path_info(token, seg_len):
    segment = jnp.where(
        token < 8 * seg_len,
        0,
        jnp.where(
            token < 12 * seg_len,
            (token - 8 * seg_len) // seg_len + 1,
            (token - 12 * seg_len) // seg_len + 5,
        ),
    )
    parent = jnp.where(segment == 0, -1, jnp.where(segment <= 4, 0, (segment - 5) // 2 + 1))
    place = token - jnp.where(
        segment == 0, 0, jnp.where(segment <= 4, (segment - 1) * seg_len, (segment - 2) * seg_len)
    )
    return (segment, parent, place)


def score_bias(token, table, seg_len):
    seg, parent, place = path_info(token, seg_len)
    allowed = (
        (seg[None, :] == 0) | (seg[None, :] == seg[:, None]) | (seg[None, :] == parent[:, None])
    )
    relative = place[None, :] - place[:, None]
    magnitude = jnp.abs(relative)
    marked = sum(((magnitude >= mark).astype(jnp.int32) for mark in distance_marks))
    bucket = jnp.where(relative > 0, 16, 0) + jnp.where(magnitude < 8, magnitude, 7 + marked)
    heads = []
    for head in range(table.shape[1]):
        looked = jnp.full(bucket.shape, table[0, head])
        for place_in in range(1, table.shape[0]):
            looked = jnp.where(bucket == place_in, table[place_in, head], looked)
        heads.append(jnp.where(allowed, looked, masked_score))
    return jnp.stack(heads)


def dot(left, right, left_dim, right_dim):
    return lax.dot_general(
        left, right, (((left_dim,), (right_dim,)), ((), ())), preferred_element_type=wide
    )


def step(x, axis):
    n = lax.axis_size(axis)
    return lax.ppermute(x, axis, [(i, (i + 1) % n) for i in range(n)])


def swap(x, axis, k):
    n = lax.axis_size(axis)
    return lax.ppermute(x, axis, [(i, i ^ k) for i in range(n)])


def pick(stack, index):
    return lax.dynamic_index_in_dim(stack, index, 0, keepdims=False)


def put(stack, part, index):
    return lax.dynamic_update_slice_in_dim(stack, part[None], index, 0)


def ring_gather(x, axis):
    n, me = lax.axis_size(axis), lax.axis_index(axis)
    out = put(jnp.zeros((n,) + x.shape, x.dtype), x, me)
    for k in range(1, n):
        x = step(x, axis)
        out = put(out, x, lax.rem(me - k + n, n))
    return out


def ring_scatter(parts, axis):
    n, me = lax.axis_size(axis), lax.axis_index(axis)
    acc = pick(parts, lax.rem(me + n - 1, n))
    for k in range(2, n + 1):
        got = step(acc.astype(low), axis)
        acc = got.astype(wide) + pick(parts, lax.rem(me + 2 * n - k, n)).astype(wide)
    return acc


def xor_gather(x, axis):
    n = lax.axis_size(axis)
    return [x] + [swap(x, axis, k) for k in range(1, n)]


def xor_scatter(parts, axis):
    n = lax.axis_size(axis)
    acc = parts[0].astype(wide)
    for k in range(1, n):
        acc = acc + swap(parts[k].astype(low), axis, k).astype(wide)
    return acc


def absolute(blocks, axis):
    n, me = lax.axis_size(axis), lax.axis_index(axis)
    out = jnp.zeros((n,) + blocks[0].shape, blocks[0].dtype)
    for k in range(n):
        out = put(out, blocks[k], me ^ k)
    return out


def norm_back(values_in, scale, gain, normed_grad):
    weighted = normed_grad * gain
    value_grad = scale * weighted - values_in * scale**3 * jnp.mean(
        weighted * values_in, axis=-1, keepdims=True
    )
    gain_grad = jnp.sum(normed_grad * values_in * scale, axis=(0, 1))
    return (value_grad, gain_grad)


def gelu_tanh(value_in):
    return jax.nn.gelu(value_in, approximate=True)


def tree_rows(x, half):
    mine, other = pick(x, half), pick(x, 1 - half)
    mine_all = xor_gather(mine, "ctx")
    other_rest = swap(jnp.stack(mine_all[1:]), "tensor", 1)
    return jnp.stack([jnp.stack(mine_all), jnp.concatenate([other[None], other_rest])])


def tree_sum(partial, half):
    both = swap(partial[1].astype(low), "tensor", 1).astype(wide) + partial[0].astype(wide)
    return xor_scatter([both[k] for k in range(both.shape[0])], "ctx")


def on_device(
    inputs,
    cotangent,
    norm1_gain,
    w_query,
    w_key,
    w_value,
    w_out,
    norm2_gain,
    w_gate,
    w_up,
    w_down,
    bias_table,
):
    micro, rows, width = inputs.shape
    shards, ctx = lax.axis_size("shard"), lax.axis_size("ctx")
    own_width = w_query.shape[0]
    inner = w_query.shape[1]
    heads = inner // DK
    me_ctx, half = lax.axis_index("ctx"), lax.axis_index("tensor")
    columns = w_gate.shape[1] // ctx

    tree_in = tree_rows(inputs, half)
    tree_cot = tree_rows(cotangent, half)
    gains = ring_gather(jnp.stack([norm1_gain, norm2_gain]), "shard")
    gains = gains.transpose(1, 0, 2).reshape(2, width).astype(wide)

    four = jnp.stack([w_query, w_key, w_value, w_out.T])
    one = ring_gather(pick(four, me_ctx), "shard")
    four_all = absolute(xor_gather(one, "ctx"), "ctx").reshape(4, width, inner)
    q_w, k_w, v_w, o_w = (four_all[i] for i in range(4))

    start = me_ctx * columns
    three = jnp.stack(
        [
            lax.dynamic_slice_in_dim(w_gate, start, columns, 1),
            lax.dynamic_slice_in_dim(w_up, start, columns, 1),
            lax.dynamic_slice_in_dim(w_down, start, columns, 0).T,
        ]
    )
    three_all = [ring_gather(three[i], "shard").reshape(width, columns) for i in range(3)]
    g_w, u_w, d_w = three_all

    token = (
        (me_ctx ^ jnp.arange(ctx, dtype=jnp.int32))[:, None] * rows
        + jnp.arange(rows, dtype=jnp.int32)[None]
    ).reshape(-1)
    table = lax.dynamic_slice_in_dim(bias_table, half * heads, heads, 1)
    bias = score_bias(token, table, rows // 5)

    length = ctx * rows
    start_in = tree_in.astype(wide).reshape(micro, length, width)
    scale_one = lax.rsqrt(jnp.mean(start_in * start_in, axis=-1, keepdims=True) + norm_eps)
    normed_one = (start_in * scale_one * gains[0]).astype(low).reshape(micro * length, width)
    queries = dot(normed_one, q_w, 1, 0).astype(low)
    keys = dot(normed_one, k_w, 1, 0).astype(low)
    values = dot(normed_one, v_w, 1, 0).astype(low)
    query_heads = queries.reshape(micro, length, heads, DK)
    key_heads = keys.reshape(micro, length, heads, DK)
    value_heads = values.reshape(micro, length, heads, DK)
    scores = (
        jnp.einsum("mqhd,mkhd->mhqk", query_heads, key_heads, preferred_element_type=wide) + bias
    )
    row_max = jnp.max(scores, axis=-1, keepdims=True)
    raised = jnp.exp(scores - row_max)
    soft_all = raised / jnp.sum(raised, axis=-1, keepdims=True)
    mixed_all = jnp.einsum(
        "mhqk,mkhd->mqhd", soft_all.astype(low), value_heads, preferred_element_type=wide
    ).astype(low)
    mixed_all = mixed_all.reshape(micro * length, inner)
    attended = dot(mixed_all, o_w, 1, 1).astype(low).reshape(micro, length, width)
    theirs = swap(attended[::-1], "tensor", 1)
    middle_all = start_in + (attended.astype(wide) + theirs.astype(wide))
    scale_two_all = lax.rsqrt(jnp.mean(middle_all * middle_all, axis=-1, keepdims=True) + norm_eps)
    normed_two = (middle_all * scale_two_all * gains[1]).astype(low).reshape(micro * length, width)

    gate_pre = dot(normed_two, g_w, 1, 0)
    up_pre = dot(normed_two, u_w, 1, 0)
    activated, gelu_pull = jax.vjp(gelu_tanh, gate_pre)
    hidden = (activated * up_pre).astype(low)
    down_in = tree_cot.reshape(micro * length, width)
    hidden_grad = dot(down_in, d_w, 1, 1 - 1)
    gate_grad = gelu_pull(hidden_grad * up_pre)[0].astype(low)
    up_grad = (hidden_grad * activated).astype(low)
    two_partial = dot(gate_grad, g_w, 1, 1) + dot(up_grad, u_w, 1, 1)
    two_mine = tree_sum(two_partial.reshape(micro, ctx, rows, width).astype(low), half).astype(low)
    two_grad = jnp.stack([two_mine, swap(two_mine, "tensor", 1)]).astype(wide)

    feed = dot(hidden, d_w, 1, 1).astype(low).reshape(micro, ctx, rows, width)
    feed_mine = tree_sum(feed, half)

    def own(x):
        return x.reshape((micro, ctx, rows) + x.shape[2:])[:, 0]

    middle = own(middle_all)
    produced_mine = (middle[0] + feed_mine).astype(low)
    produced_other = swap(produced_mine, "tensor", 1)

    wgrads = jnp.stack(
        [
            dot(normed_two, gate_grad, 0, 0).astype(low),
            dot(normed_two, up_grad, 0, 0).astype(low),
            dot(down_in, hidden, 0, 0).astype(low),
        ]
    ).reshape(3, shards, own_width, columns)
    wide_grads = []
    for i in range(3):
        own_columns = ring_scatter(wgrads[i], "shard").astype(low)
        every = absolute(xor_gather(own_columns, "ctx"), "ctx")
        if i < 2:
            every = every.transpose(1, 0, 2).reshape(own_width, ctx * columns)
        else:
            every = every.transpose(0, 2, 1).reshape(ctx * columns, own_width)
        wide_grads.append(every.astype(wide))

    grad_out = own(tree_cot.reshape(micro, length, width)).astype(wide)
    middle_part, gain_two_grad = norm_back(middle, own(scale_two_all), gains[1], two_grad)
    middle_grad = grad_out + middle_part
    out_in = middle_grad.astype(low).reshape(micro * rows, width)
    mixed = own(mixed_all.reshape(micro, length, inner)).reshape(micro * rows, inner)
    out_wgrad = dot(out_in, mixed, 0, 0)
    mixed_grad = dot(out_in, o_w, 1, 0).astype(low).reshape(micro, rows, heads, DK)
    soft = soft_all.reshape(micro, heads, ctx, rows, length)[:, :, 0]
    values_full = jnp.einsum(
        "mhqk,mqhd->mkhd", soft.astype(low), mixed_grad, preferred_element_type=wide
    )
    weight_grad = jnp.einsum("mqhd,mkhd->mhqk", mixed_grad, value_heads, preferred_element_type=wide)
    scores_grad = soft * (weight_grad - jnp.sum(weight_grad * soft, axis=-1, keepdims=True))
    scores_grad = scores_grad.astype(low)
    queries_grad = jnp.einsum("mhqk,mkhd->mqhd", scores_grad, key_heads, preferred_element_type=wide)
    queries_grad = queries_grad.reshape(micro * rows, inner).astype(low)
    own_queries = own(query_heads.reshape(micro, length, inner)).reshape(micro, rows, heads, DK)
    keys_full = jnp.einsum("mhqk,mqhd->mkhd", scores_grad, own_queries, preferred_element_type=wide)
    both_full = jnp.concatenate(
        [keys_full.reshape(micro, length, inner), values_full.reshape(micro, length, inner)], -1
    ).astype(low)
    both_full = both_full.reshape(micro, ctx, rows, 2 * inner)
    both_own = xor_scatter([both_full[:, k] for k in range(ctx)], "ctx").astype(low)
    keys_grad = both_own[..., :inner].reshape(micro * rows, inner)
    values_grad = both_own[..., inner:].reshape(micro * rows, inner)
    normed_own = own(normed_one.reshape(micro, length, width)).reshape(micro * rows, width)
    first = dot(queries_grad, q_w, 1, 1) + dot(keys_grad, k_w, 1, 1) + dot(values_grad, v_w, 1, 1)
    first = first.astype(low).reshape(micro, rows, width)
    normed_one_grad = first.astype(wide) + swap(first[::-1], "tensor", 1).astype(wide)
    x_own = own(start_in)
    input_part, gain_one_grad = norm_back(x_own, own(scale_one), gains[0], normed_one_grad)
    input_grad = (middle_grad + input_part).astype(low)

    four_grads = jnp.stack(
        [
            dot(normed_own, queries_grad, 0, 0).astype(low),
            dot(normed_own, keys_grad, 0, 0).astype(low),
            dot(normed_own, values_grad, 0, 0).astype(low),
            out_wgrad.astype(low),
        ]
    )
    mine = xor_scatter([pick(four_grads, me_ctx ^ k) for k in range(ctx)], "ctx").astype(low)
    mine = ring_scatter(mine.reshape(shards, own_width, inner), "shard").astype(low)
    four_own = absolute(xor_gather(mine, "ctx"), "ctx").astype(wide)
    gain_sum = xor_scatter([jnp.stack([gain_one_grad, gain_two_grad]).astype(low)] * ctx, "ctx")
    gain_parts = gain_sum.reshape(2, shards, own_width).transpose(1, 0, 2)
    gain_own = ring_scatter(gain_parts, "shard")

    def ordered(mine_part, other_part):
        return jnp.where(half == 0, jnp.stack([mine_part, other_part]), jnp.stack([other_part, mine_part]))

    return (
        ordered(produced_mine, produced_other),
        ordered(input_grad[0], input_grad[1]),
        gain_own[0],
        four_own[0],
        four_own[1],
        four_own[2],
        four_own[3].T,
        gain_own[1],
        wide_grads[0],
        wide_grads[1],
        wide_grads[2],
    )


def solution(mesh):
    placed = (
        P(None, ("shard", "ctx"), None),
        P(None, ("shard", "ctx"), None),
        P("shard"),
        P("shard", "tensor"),
        P("shard", "tensor"),
        P("shard", "tensor"),
        P("tensor", "shard"),
        P("shard"),
        P("shard", "tensor"),
        P("shard", "tensor"),
        P("tensor", "shard"),
        P(),
    )
    return jax.shard_map(
        on_device,
        mesh=mesh,
        in_specs=placed,
        out_specs=placed[:2]
        + (
            P("shard"),
            P("shard", "tensor"),
            P("shard", "tensor"),
            P("shard", "tensor"),
            P("tensor", "shard"),
            P("shard"),
            P("shard", "tensor"),
            P("shard", "tensor"),
            P("tensor", "shard"),
        ),
        check_vma=False,
    )
```

```python
import functools

import jax
import jax.numpy as jnp
from jax import lax
from jax.experimental import pallas as pl
from jax.experimental.pallas import tpu as pltpu
from jax.sharding import PartitionSpec as P

DK = 64
norm_eps = 1e-06
distance_marks = (8, 12, 16, 23, 32, 46, 64, 91)
masked_score = -1e30
low = jnp.bfloat16
wide = jnp.float32
LANES = 128


def dot_nn(left, right):
    return lax.dot_general(left, right, (((1,), (0,)), ((), ())), preferred_element_type=wide)


def dot_nt(left, right):
    return lax.dot_general(left, right, (((1,), (1,)), ((), ())), preferred_element_type=wide)


def dot_tn(left, right):
    return lax.dot_general(left, right, (((0,), (0,)), ((), ())), preferred_element_type=wide)


def wrap(value, n):
    return lax.rem(value + 2 * n, n)


def run(body, name, outs, operands, scratch=(), scalars=1, flops=0):
    moved = sum(a.size * a.dtype.itemsize for a in operands)
    moved += sum(functools.reduce(lambda a, b: a * b, s, 1) * jnp.dtype(d).itemsize for s, d in outs)
    return pl.pallas_call(
        body,
        name=name,
        out_shape=[jax.ShapeDtypeStruct(s, d) for s, d in outs],
        in_specs=[pl.BlockSpec(memory_space=pltpu.SMEM)] * scalars
        + [pl.BlockSpec(memory_space=pltpu.VMEM)] * (len(operands) - scalars),
        out_specs=[pl.BlockSpec(memory_space=pltpu.VMEM)] * len(outs),
        scratch_shapes=list(scratch),
        compiler_params=pltpu.CompilerParams(vmem_limit_bytes=40 * 2**20),
        cost_estimate=pl.CostEstimate(flops=flops, bytes_accessed=moved, transcendentals=0),
    )(*operands)


def step(x, axis, k=1):
    n = lax.axis_size(axis)
    return lax.ppermute(x, axis, [(i, (i + k) % n) for i in range(n)])


def swap(x, axis, k=1):
    n = lax.axis_size(axis)
    return lax.ppermute(x, axis, [(i, i ^ k) for i in range(n)])


def ring_gather(x, axis):
    out = [x]
    for _ in range(1, lax.axis_size(axis)):
        out.append(step(out[-1], axis))
    return out


def ring_scatter(parts, axis):
    acc = parts[0]
    for part in parts[1:]:
        acc = (step(acc, axis).astype(wide) + part.astype(wide)).astype(low)
    return acc


def xor_gather(x, axis):
    return [x] + [swap(x, axis, k) for k in range(1, lax.axis_size(axis))]


def pack_attention(n_ctx, idx, w_q, w_k, w_v, w_o, g1, g2, own_t, buf):
    c = idx[1]
    inner, r = w_o.shape
    for i, ref in enumerate((w_q, w_k, w_v)):
        own_t[i * inner : (i + 1) * inner, :] = ref[...].T
    for v in range(n_ctx):

        @pl.when(c == v)
        def _(v=v):
            if v < 3:
                buf[0:inner, 0:r] = own_t[v * inner : (v + 1) * inner, :]
            else:
                buf[0:inner, 0:r] = w_o[...]

    buf[inner : inner + 1, 0:r] = g1[...]
    buf[inner + 1 : inner + 2, 0:r] = g2[...]


def pack_wide(n_ctx, widths, rp, idx, w_g, w_u, w_d, *refs):
    bufs, stage = refs[:-1], refs[-1]
    r = w_g.shape[0]
    columns = sum(widths)
    for v in range(n_ctx):

        @pl.when(idx[1] == v)
        def _(v=v):
            at = v * columns
            for n, buf in zip(widths, bufs, strict=True):
                stage[:, 0:n] = w_g[:, at : at + n]
                stage[:, n : 2 * n] = w_u[:, at : at + n]
                for q in range(2 * n // LANES):
                    buf[rp * q : rp * q + r, :] = stage[:, LANES * q : LANES * (q + 1)]
                base = rp * (2 * n // LANES)
                for q in range(pl.cdiv(r, LANES)):
                    wide_q = min(LANES, r - LANES * q)
                    buf[base + n * q : base + n * (q + 1), 0:wide_q] = w_d[
                        at : at + n, LANES * q : LANES * q + wide_q
                    ]
                at += n


def bias_body(rows, seg_len, marks, idx, table, out):
    c = idx[1]
    heads, length, _ = out.shape

    def info(position):
        block = sum(((position >= rows * b).astype(jnp.int32) for b in range(1, length // rows)))
        token = (block ^ c) * rows + position - block * rows
        seg = sum(((token >= q * seg_len).astype(jnp.int32) for q in range(8, 20)))
        parent = jnp.where(seg == 0, -1, jnp.where(seg <= 4, 0, (seg - 3) >> 1))
        shift = jnp.where(seg == 0, 0, jnp.where(seg <= 4, seg - 1, seg - 2))
        return seg, parent, token - shift * seg_len

    key_seg, _, key_place = info(lax.broadcasted_iota(jnp.int32, (16, length), 1))

    def rows_of(i, _):
        at = pl.multiple_of(i * 16, 16)
        seg, parent, place = info(lax.broadcasted_iota(jnp.int32, (16, length), 0) + at)
        allowed = (key_seg == 0) | (key_seg == seg) | (key_seg == parent)
        relative = key_place - place
        magnitude = jnp.abs(relative)
        marked = sum(((magnitude >= mark).astype(jnp.int32) for mark in marks))
        bucket = jnp.where(relative > 0, 16, 0) + jnp.where(magnitude < 8, magnitude, 7 + marked)
        looked = [jnp.full(bucket.shape, table[0, h], wide) for h in range(heads)]
        for b in range(1, table.shape[0]):
            hit = bucket == b
            looked = [jnp.where(hit, table[b, h], looked[h]) for h in range(heads)]
        for h in range(heads):
            out[h, pl.ds(at, 16), :] = jnp.where(allowed, looked[h], masked_score)
        return 0

    lax.fori_loop(0, length // 16, rows_of, 0)


def norm_one(n_ctx, n_shard, idx, x_in, *refs):
    s, half = idx[0], idx[2]
    mine, rest = refs[: n_ctx - 1], refs[n_ctx - 1]
    g1, g2 = refs[n_ctx], refs[n_ctx + 1]
    bufs = refs[n_ctx + 2 : n_ctx + 1 + n_shard]
    normed, x_mine, x_own, gains = refs[n_ctx + 1 + n_shard :]
    r = normed.shape[2]
    inner = bufs[0].shape[0] - 16
    _, rows, width = x_in.shape
    gains[s, 0:1, :] = g1[...].astype(wide)
    gains[s, 1:2, :] = g2[...].astype(wide)
    for k, buf in enumerate(bufs):
        both = buf[inner : inner + 2, 0:r].astype(wide)
        gains[wrap(s - 1 - k, n_shard), 0:2, :] = both
    for m in range(2):
        for k in range(n_ctx):
            if k == 0:
                x = x_in[half if m == 0 else 1 - half]
            else:
                x = mine[k - 1][...] if m == 0 else rest[k - 1]
            x = x.astype(wide)
            y = x * lax.rsqrt(jnp.mean(x * x, axis=-1, keepdims=True) + norm_eps)
            at = (m * n_ctx + k) * rows
            for j in range(n_shard):
                piece = slice(r * j, r * (j + 1))
                normed[j, at : at + rows, :] = (y[:, piece] * gains[j, 0:1, :]).astype(low)
                if m == 0:
                    x_mine[j, at : at + rows, :] = x[:, piece].astype(low)
                    if k == 0:
                        x_own[j] = x[:, piece]


def chunk_cot(n_ctx, n_shard, idx, x_in, *refs):
    half = idx[2]
    mine, rest = refs[: n_ctx - 1], refs[n_ctx - 1]
    out, own = refs[n_ctx:]
    r = out.shape[2]
    _, rows, _ = x_in.shape
    for m in range(2):
        for k in range(n_ctx):
            if k == 0:
                x = x_in[half if m == 0 else 1 - half]
            else:
                x = mine[k - 1][...] if m == 0 else rest[k - 1]
            at = (m * n_ctx + k) * rows
            for j in range(n_shard):
                out[j, at : at + rows, :] = x[:, r * j : r * (j + 1)]
                if m == 0 and k == 0:
                    own[j] = x[:, r * j : r * (j + 1)]


def attend(n_ctx, n_shard, rows, heads, idx, normed, own_t, w_o, bias, *refs):
    s, c = idx[0], idx[1]
    first, later = refs[:n_ctx], refs[n_ctx : 2 * n_ctx]
    att_mine, att_other, soft, qkv, mixed_own, every, mixed = refs[2 * n_ctx :]
    inner, r = w_o.shape
    length = n_ctx * rows
    every[s, 0 : 3 * inner, :] = own_t[...]
    every[s, 3 * inner : 4 * inner, :] = w_o[...]
    for v in range(n_ctx):

        @pl.when(c == v)
        def _(v=v):
            for k in range(n_ctx):
                at = slice((v ^ k) * inner, ((v ^ k) + 1) * inner)
                every[wrap(s - 1, n_shard), at, :] = first[k][0:inner, 0:r]
                for z in range(2, n_shard):
                    every[wrap(s - z, n_shard), at, :] = later[k][z - 2, 0:inner, 0:r]

    for m in range(2):
        low_row = m * length
        acc = dot_nt(normed[0, low_row : low_row + length, :], every[0, 0 : 3 * inner, :])
        for j in range(1, n_shard):
            acc += dot_nt(normed[j, low_row : low_row + length, :], every[j, 0 : 3 * inner, :])
        qkv[low_row : low_row + length, :] = acc.astype(low)
        for h in range(heads):
            at = DK * h
            keys = qkv[low_row : low_row + length, inner + at : inner + at + DK]
            values = qkv[low_row : low_row + length, 2 * inner + at : 2 * inner + at + DK]
            for b in range(n_ctx):
                top = low_row + b * rows
                scores = dot_nt(qkv[top : top + rows, at : at + DK], keys)
                scores += bias[h, b * rows : (b + 1) * rows, :]
                raised = jnp.exp(scores - jnp.max(scores, axis=-1, keepdims=True))
                share = raised / jnp.sum(raised, axis=-1, keepdims=True)
                if b == 0:
                    soft[m, h] = share
                got = dot_nn(share.astype(low), values).astype(low)
                mixed[top : top + rows, at : at + DK] = got
                if b == 0:
                    mixed_own[m * rows : (m + 1) * rows, at : at + DK] = got
        out = att_mine if m == 0 else att_other
        for j in range(n_shard):
            out[j] = dot_nn(
                mixed[low_row : low_row + length, :], every[j, 3 * inner : 4 * inner, :]
            ).astype(low)


def middle_norm(n_ctx, n_shard, width, x_mine, att, got, gains, normed, middle_own):
    length = x_mine.shape[1]
    rows = length // n_ctx
    for b in range(n_ctx):
        at = slice(b * rows, (b + 1) * rows)
        mids, total = [], 0.0
        for j in range(n_shard):
            mid = x_mine[j, at, :].astype(wide) + (
                att[j, at, :].astype(wide) + got[j, at, :].astype(wide)
            )
            total += jnp.sum(mid * mid, axis=-1, keepdims=True)
            mids.append(mid)
        scale = lax.rsqrt(total / width + norm_eps)
        for j in range(n_shard):
            normed[j, at, :] = (mids[j] * scale * gains[j, 1:2, :]).astype(low)
            if b == 0:
                middle_own[j] = mids[j]


def feed_forward(n_ctx, n_shard, n, rp, first, idx, nt_mine, nt_other, cot, *refs):
    s = idx[0]
    bufs, refs = refs[:n_shard], refs[n_shard:]
    before = None
    if not first:
        before, refs = refs[:4], refs[4:]
    grads, refs = refs[:n_shard], refs[n_shard:]
    feed, two, refs = refs[0:2], refs[2:4], refs[4:]
    w_in, w_down, hidden, pair = refs
    _, length, r = nt_mine.shape
    rows = length // n_ctx
    tiles, base = 2 * n // LANES, rp * (2 * n // LANES)
    down_tiles = [(q, min(LANES, r - LANES * q)) for q in range(pl.cdiv(r, LANES))]
    for k in range(n_shard):
        for q in range(tiles):
            w_in[k, :, LANES * q : LANES * (q + 1)] = bufs[k][rp * q : rp * q + r, :]
        for q, size in down_tiles:
            w_down[k, :, LANES * q : LANES * q + size] = bufs[k][
                base + n * q : base + n * (q + 1), 0:size
            ]
    c0, c1 = 0.7978845608028654, 0.044715
    span = 2 * rows
    for m, nt in ((0, nt_mine), (1, nt_other)):

        def block(b, _, m=m, nt=nt):
            at = pl.ds(pl.multiple_of(b * span, span), span)
            all_at = pl.ds(pl.multiple_of(m * length + b * span, span), span)
            both, back = 0.0, 0.0
            for k in range(n_shard):
                j = wrap(s - k, n_shard)
                both += dot_nn(nt[j, at, :], w_in[k])
                back += dot_nt(cot[j, all_at, :], w_down[k])
            gate, up = both[:, :n], both[:, n:]
            square = gate * gate
            bent = jnp.tanh(c0 * (gate + c1 * gate * square))
            half_one = 0.5 * (1.0 + bent)
            active = gate * half_one
            slope = half_one + 0.5 * gate * (1.0 - bent * bent) * (c0 * (1.0 + 3.0 * c1 * square))
            hid = (active * up).astype(low)
            hidden[all_at, :] = hid
            pair[all_at, 0:n] = (back * up * slope).astype(low)
            pair[all_at, n : 2 * n] = (back * active).astype(low)
            both_grad = pair[all_at, :]
            for k in range(n_shard):
                j = wrap(s - k, n_shard)
                made = dot_nn(hid, w_down[k])
                back_in = dot_nt(both_grad, w_in[k])
                for i in range(2):
                    piece = slice(i * rows, (i + 1) * rows)
                    out, out_two = made[piece], back_in[piece]
                    if before is not None:
                        out = out + before[m][2 * b + i, j].astype(wide)
                        out_two = out_two + before[2 + m][2 * b + i, j].astype(wide)
                    feed[m][2 * b + i, j] = out.astype(low)
                    two[m][2 * b + i, j] = out_two.astype(low)
            return 0

        lax.fori_loop(0, n_ctx // 2, block, 0)
    for p in range(n_shard):
        j = wrap(s - 1 - p, n_shard)
        got = dot_tn(nt_mine[j], pair[0:length, :]) + dot_tn(nt_other[j], pair[length:, :])
        for q in range(tiles):
            grads[p][rp * q : rp * q + r, :] = got[:, LANES * q : LANES * (q + 1)].astype(low)
        got = dot_tn(hidden[...], cot[j])
        for q, size in down_tiles:
            grads[p][base + n * q : base + n * (q + 1), 0:size] = got[
                :, LANES * q : LANES * q + size
            ].astype(low)


def norm_two_back(n_shard, width, n_parts, *refs):
    parts, refs = refs[:n_parts], refs[n_parts:]
    middle, cot, gains, out_in, grad, gain_grad = refs
    mids = [middle[j] for j in range(n_shard)]
    twos = [sum((p[j].astype(wide) for p in parts)) for j in range(n_shard)]
    mean = sum((jnp.sum(a * a, axis=-1, keepdims=True) for a in mids)) / width
    scale = lax.rsqrt(mean + norm_eps)
    us = [twos[j] * gains[j, 1:2, :] for j in range(n_shard)]
    inner = sum((jnp.sum(a * b, axis=-1, keepdims=True) for a, b in zip(us, mids, strict=True)))
    inner = inner / width * (scale * scale * scale)
    for j in range(n_shard):
        back = cot[j].astype(wide) + scale * us[j] - mids[j] * inner
        grad[j] = back
        out_in[j] = back.astype(low)
        gain_grad[j] = jnp.sum(twos[j] * mids[j] * scale, axis=0, keepdims=True)


def attend_back(n_ctx, n_shard, heads, idx, o_mine, o_other, soft, qkv, mixed, every, normed, *refs):
    s, c = idx[0], idx[1]
    kv, (q_grad, stack, kv_all, mixed_grad) = refs[:n_ctx], refs[n_ctx:]
    _, rows, r = o_mine.shape
    length = n_ctx * rows
    inner = heads * DK
    for m, o_in in ((0, o_mine), (1, o_other)):
        top, own = m * length, m * rows
        acc = 0.0
        for j in range(n_shard):
            acc += dot_nt(o_in[j], every[j, 3 * inner : 4 * inner, :])
        mixed_grad[own : own + rows, :] = acc.astype(low)
        for h in range(heads):
            at = DK * h
            share = soft[m, h]
            grad = mixed_grad[own : own + rows, at : at + DK]
            keys = qkv[top : top + length, inner + at : inner + at + DK]
            values = qkv[top : top + length, 2 * inner + at : 2 * inner + at + DK]
            queries = qkv[top : top + rows, at : at + DK]
            weight = dot_nt(grad, values)
            ds = share * (weight - jnp.sum(weight * share, axis=-1, keepdims=True))
            ds = ds.astype(low)
            q_grad[own : own + rows, at : at + DK] = dot_nn(ds, keys).astype(low)
            kv_all[top : top + length, at : at + DK] = dot_tn(ds, queries).astype(low)
            kv_all[top : top + length, inner + at : inner + at + DK] = dot_tn(
                share.astype(low), grad
            ).astype(low)
        for k in range(n_ctx):
            kv[k][own : own + rows, :] = kv_all[top + k * rows : top + (k + 1) * rows, :]
    for p in range(n_shard):
        j = wrap(s - 1 - p, n_shard)
        for_q = dot_tn(q_grad[0:rows, :], normed[j, 0:rows, :])
        for_q += dot_tn(q_grad[rows:, :], normed[j, length : length + rows, :])
        for_kv = dot_tn(kv_all[...], normed[j])
        for_o = dot_tn(mixed[0:rows, :], o_mine[j]) + dot_tn(mixed[rows:, :], o_other[j])
        stack[c, p] = for_q.astype(low)
        stack[c ^ 1, p] = for_kv[0:inner].astype(low)
        stack[c ^ 2, p] = for_kv[inner:].astype(low)
        stack[c ^ 3, p] = for_o.astype(low)


def first_grad(n_shard, n_parts, *refs):
    parts, (q_grad, every, out_mine, out_other, three) = refs[:n_parts], refs[n_parts:]
    rows2, inner = q_grad.shape
    rows = rows2 // 2
    three[:, 0:inner] = q_grad[...]
    three[:, inner:] = sum((p[...].astype(wide) for p in parts)).astype(low)
    for j in range(n_shard):
        got = dot_nn(three[...], every[j, 0 : 3 * inner, :]).astype(low)
        out_mine[j] = got[0:rows]
        out_other[j] = got[rows:]


def norm_one_back(n_shard, width, mine, got, x_own, grad, gains, out, gain_grad):
    r = x_own.shape[2]
    xs = [x_own[j] for j in range(n_shard)]
    ones = [mine[j].astype(wide) + got[j].astype(wide) for j in range(n_shard)]
    mean = sum((jnp.sum(a * a, axis=-1, keepdims=True) for a in xs)) / width
    scale = lax.rsqrt(mean + norm_eps)
    us = [ones[j] * gains[j, 0:1, :] for j in range(n_shard)]
    inner = sum((jnp.sum(a * b, axis=-1, keepdims=True) for a, b in zip(us, xs, strict=True)))
    inner = inner / width * (scale * scale * scale)
    for j in range(n_shard):
        back = grad[j] + scale * us[j] - xs[j] * inner
        out[:, r * j : r * (j + 1)] = back.astype(low)
        gain_grad[j] = jnp.sum(ones[j] * xs[j] * scale, axis=0, keepdims=True)


def produce(n_shard, n_parts, *refs):
    parts, (middle, out) = refs[:n_parts], refs[n_parts:]
    r = middle.shape[2]
    for j in range(n_shard):
        fed = sum((p[j].astype(wide) for p in parts))
        out[:, r * j : r * (j + 1)] = (middle[j] + fed).astype(low)


def finish_wide(n_ctx, widths, rp, idx, *refs):
    pieces, (out_g, out_u, out_d, stage) = refs[: len(widths) * n_ctx], refs[len(widths) * n_ctx :]
    r = out_g.shape[0]
    columns = sum(widths)
    for i, n in enumerate(widths):
        base = rp * (2 * n // LANES)
        for k in range(n_ctx):
            piece = pieces[i * n_ctx + k]
            for q in range(2 * n // LANES):
                stage[:, LANES * q : LANES * (q + 1)] = piece[rp * q : rp * q + r, :].astype(wide)
            for v in range(n_ctx):

                @pl.when(idx[1] == v)
                def _(v=v, n=n, i=i, k=k, piece=piece, base=base):
                    at = (v ^ k) * columns + sum(widths[:i])
                    out_g[:, at : at + n] = stage[:, 0:n]
                    out_u[:, at : at + n] = stage[:, n : 2 * n]
                    for q in range(pl.cdiv(r, LANES)):
                        size = min(LANES, r - LANES * q)
                        out_d[at : at + n, LANES * q : LANES * q + size] = piece[
                            base + n * q : base + n * (q + 1), 0:size
                        ].astype(wide)


def finish_attention(n_ctx, idx, *refs):
    pieces, outs = refs[:n_ctx], refs[n_ctx:]
    for v in range(n_ctx):

        @pl.when(idx[1] == v)
        def _(v=v):
            for k in range(n_ctx):
                got = pieces[k][...].astype(wide)
                outs[v ^ k][...] = got if (v ^ k) == 3 else got.T


def on_device(
    inputs,
    cotangent,
    norm1_gain,
    w_query,
    w_key,
    w_value,
    w_out,
    norm2_gain,
    w_gate,
    w_up,
    w_down,
    bias_table,
):
    _, rows, width = inputs.shape
    shards, ctx = lax.axis_size("shard"), lax.axis_size("ctx")
    r, inner = w_query.shape
    heads = inner // DK
    length = ctx * rows
    columns = w_gate.shape[1] // ctx
    first_width = pl.cdiv(columns, 2 * LANES) * LANES
    widths = (first_width, columns - first_width)
    rp = pl.cdiv(r, 16) * 16
    lanes_r = pl.cdiv(r, LANES) * LANES
    s, c, half = lax.axis_index("shard"), lax.axis_index("ctx"), lax.axis_index("tensor")
    idx = jnp.stack([s, c, half]).astype(jnp.int32)
    token_flops = 2 * 2 * length * width

    own_x = lax.dynamic_index_in_dim(inputs, half, 0, keepdims=False)
    mine_x = xor_gather(own_x, "ctx")[1:]
    own_t, own_buf = run(
        functools.partial(pack_attention, ctx),
        "pack_attention",
        [((3 * inner, r), low), ((inner + 16, lanes_r), low)],
        [idx, w_query, w_key, w_value, w_out, norm1_gain[None], norm2_gain[None]],
    )
    ring = ring_gather(own_buf, "shard")
    gathered_first = xor_gather(ring[1], "ctx")
    gathered_later = xor_gather(jnp.stack(ring[2:]), "ctx")
    rest_x = swap(jnp.stack(mine_x), "tensor")
    packed = run(
        functools.partial(pack_wide, ctx, widths, rp),
        "pack_wide",
        [((rp * (2 * n // LANES) + n * (lanes_r // LANES), LANES), low) for n in widths],
        [idx, w_gate, w_up, w_down],
        scratch=[pltpu.VMEM((r, 2 * max(widths)), low)],
    )
    wide_rings = [ring_gather(buf, "shard") for buf in packed]

    table = lax.dynamic_slice_in_dim(bias_table, half * heads, heads, 1)
    (bias,) = run(
        functools.partial(bias_body, rows, rows // 5, distance_marks),
        "bias",
        [((heads, length, length), wide)],
        [idx, table],
        scalars=2,
    )
    normed_one, x_mine, x_own, gains = run(
        functools.partial(norm_one, ctx, shards),
        "norm_one",
        [
            ((shards, 2 * length, r), low),
            ((shards, length, r), low),
            ((shards, rows, r), wide),
            ((shards, 2, r), wide),
        ],
        [idx, inputs, *mine_x, rest_x, norm1_gain[None], norm2_gain[None], *ring[1:]],
    )
    own_cot = lax.dynamic_index_in_dim(cotangent, half, 0, keepdims=False)
    mine_cot = xor_gather(own_cot, "ctx")[1:]
    rest_cot = swap(jnp.stack(mine_cot), "tensor")
    cot, cot_own = run(
        functools.partial(chunk_cot, ctx, shards),
        "chunk_cot",
        [((shards, 2 * length, r), low), ((shards, rows, r), low)],
        [idx, cotangent, *mine_cot, rest_cot],
    )
    att_mine, att_other, soft, qkv, mixed_own, every = run(
        functools.partial(attend, ctx, shards, rows, heads),
        "attend",
        [
            ((shards, length, r), low),
            ((shards, length, r), low),
            ((2, heads, rows, length), wide),
            ((2 * length, 3 * inner), low),
            ((2 * rows, inner), low),
            ((shards, 4 * inner, r), low),
        ],
        [idx, normed_one, own_t, w_out, bias, *gathered_first, *gathered_later],
        scratch=[pltpu.VMEM((2 * length, inner), low)],
        flops=token_flops * 4 * inner,
    )
    att_got = swap(att_other, "tensor")
    nt_mine, middle_own = run(
        functools.partial(middle_norm, ctx, shards, width),
        "middle_norm",
        [((shards, length, r), low), ((shards, rows, r), wide)],
        [x_mine, att_mine, att_got, gains],
        scalars=0,
    )
    nt_other = swap(nt_mine, "tensor")

    before = []
    wide_grads = []
    for i, n in enumerate(widths):
        tokens_out = ((ctx, shards, rows, r), low)
        got = run(
            functools.partial(feed_forward, ctx, shards, n, rp, i == 0),
            "feed_forward",
            [(packed[i].shape, low)] * shards + [tokens_out] * 4,
            [idx, nt_mine, nt_other, cot, *wide_rings[i], *before],
            scratch=[
                pltpu.VMEM((shards, r, 2 * n), low),
                pltpu.VMEM((shards, n, r), low),
                pltpu.VMEM((2 * length, n), low),
                pltpu.VMEM((2 * length, 2 * n), low),
            ],
            flops=token_flops * 9 * n,
        )
        wide_grads.append(got[:shards])
        before = list(got[shards:])
    feed_mine, feed_other, two_mine, two_other = before

    def tree_sum(mine, other):
        theirs = swap(other, "tensor")
        both = [(mine[k].astype(wide) + theirs[k].astype(wide)).astype(low) for k in range(ctx)]
        return [both[0]] + [swap(both[k], "ctx", k) for k in range(1, ctx)]

    two_parts = tree_sum(two_mine, two_other)
    out_in, middle_grad, gain_two = run(
        functools.partial(norm_two_back, shards, width, ctx),
        "norm_two_back",
        [((shards, rows, r), low), ((shards, rows, r), wide), ((shards, 1, r), wide)],
        [*two_parts, middle_own, cot_own, gains],
        scalars=0,
    )
    out_in_other = swap(out_in, "tensor")
    got = run(
        functools.partial(attend_back, ctx, shards, heads),
        "attend_back",
        [((2 * rows, 2 * inner), low)] * ctx
        + [((2 * rows, inner), low), ((4, shards, inner, r), low)],
        [idx, out_in, out_in_other, soft, qkv, mixed_own, every, normed_one],
        scratch=[pltpu.VMEM((2 * length, 2 * inner), low), pltpu.VMEM((2 * rows, inner), low)],
        flops=token_flops * 3 * inner,
    )
    kv_parts, q_grad, stack = got[:ctx], got[ctx], got[ctx + 1]
    kv_parts = [kv_parts[0]] + [swap(kv_parts[k], "ctx", k) for k in range(1, ctx)]
    first_mine, first_other = run(
        functools.partial(first_grad, shards, ctx),
        "first_grad",
        [((shards, rows, r), low)] * 2,
        [*kv_parts, q_grad, every],
        scalars=0,
        scratch=[pltpu.VMEM((2 * rows, 3 * inner), low)],
    )
    first_got = swap(first_other, "tensor")
    input_mine, gain_one = run(
        functools.partial(norm_one_back, shards, width),
        "norm_one_back",
        [((rows, width), low), ((shards, 1, r), wide)],
        [first_mine, first_got, x_own, middle_grad, gains],
        scalars=0,
    )
    input_other = swap(input_mine, "tensor")

    feed_parts = tree_sum(feed_mine, feed_other)
    (produced_mine,) = run(
        functools.partial(produce, shards, ctx),
        "produce",
        [((rows, width), low)],
        [*feed_parts, middle_own],
        scalars=0,
    )
    produced_other = swap(produced_mine, "tensor")

    pieces = []
    for grads in wide_grads:
        pieces += xor_gather(ring_scatter(grads, "shard"), "ctx")
    out_g, out_u, out_d = run(
        functools.partial(finish_wide, ctx, widths, rp),
        "finish_wide",
        [(w_gate.shape, wide), (w_up.shape, wide), (w_down.shape, wide)],
        [idx, *pieces],
        scratch=[pltpu.VMEM((r, 2 * max(widths)), wide)],
    )
    four = stack[0].astype(wide)
    for k in range(1, ctx):
        four = four + swap(stack[k], "ctx", k).astype(wide)
    four = four.astype(low)
    four = xor_gather(ring_scatter([four[p] for p in range(shards)], "shard"), "ctx")
    out_q, out_k, out_v, out_o = run(
        functools.partial(finish_attention, ctx),
        "finish_attention",
        [((r, inner), wide)] * 3 + [((inner, r), wide)],
        [idx, *four],
    )
    gain = jnp.concatenate([gain_one, gain_two], 1)
    gain = gain + swap(gain, "tensor")
    gain = sum(xor_gather(gain, "ctx"))
    own_gain = lax.dynamic_index_in_dim(gain, s, 0, keepdims=False)
    for k in range(1, shards):
        part = lax.dynamic_index_in_dim(gain, wrap(s + k, shards), 0, keepdims=False)
        own_gain = own_gain + step(part, "shard", k)

    def ordered(mine, other):
        return jnp.where(half == 0, jnp.stack([mine, other]), jnp.stack([other, mine]))

    return (
        ordered(produced_mine, produced_other),
        ordered(input_mine, input_other),
        own_gain[0],
        out_q,
        out_k,
        out_v,
        out_o,
        own_gain[1],
        out_g,
        out_u,
        out_d,
    )


def solution(mesh):
    placed = (
        P(None, ("shard", "ctx"), None),
        P(None, ("shard", "ctx"), None),
        P("shard"),
        P("shard", "tensor"),
        P("shard", "tensor"),
        P("shard", "tensor"),
        P("tensor", "shard"),
        P("shard"),
        P("shard", "tensor"),
        P("shard", "tensor"),
        P("tensor", "shard"),
        P(),
    )
    return jax.shard_map(
        on_device, mesh=mesh, in_specs=placed, out_specs=placed[:2] + placed[2:11], check_vma=False
    )
```

```python
import functools

import jax
import jax.numpy as jnp
from jax import lax
from jax.experimental import pallas as pl
from jax.experimental.pallas import tpu as pltpu
from jax.sharding import PartitionSpec as P

DK = 64
norm_eps = 1e-06
distance_marks = (8, 12, 16, 23, 32, 46, 64, 91)
masked_score = -1e30
low = jnp.bfloat16
wide = jnp.float32
LANES = 128
COST = 1e8


def dot_nn(left, right):
    return lax.dot_general(left, right, (((1,), (0,)), ((), ())), preferred_element_type=wide)


def dot_nt(left, right):
    return lax.dot_general(left, right, (((1,), (1,)), ((), ())), preferred_element_type=wide)


def dot_tn(left, right):
    return lax.dot_general(left, right, (((0,), (0,)), ((), ())), preferred_element_type=wide)


def wrap(value, n):
    return lax.rem(value + 2 * n, n)


def run(body, name, outs, operands, scratch=(), scalars=1, cost=1, far=0, vmem=40):
    return pl.pallas_call(
        body,
        name=name,
        out_shape=[jax.ShapeDtypeStruct(s, d) for s, d in outs],
        in_specs=[pl.BlockSpec(memory_space=pltpu.SMEM)] * scalars
        + [pl.BlockSpec(memory_space=pl.ANY)] * far
        + [pl.BlockSpec(memory_space=pltpu.VMEM)] * (len(operands) - scalars - far),
        out_specs=[pl.BlockSpec(memory_space=pltpu.VMEM)] * len(outs),
        scratch_shapes=list(scratch),
        compiler_params=pltpu.CompilerParams(vmem_limit_bytes=vmem * 2**20),
        cost_estimate=pl.CostEstimate(flops=int(cost * COST), bytes_accessed=0, transcendentals=0),
    )(*operands)


def step(x, axis, k=1):
    n = lax.axis_size(axis)
    return lax.ppermute(x, axis, [(i, (i + k) % n) for i in range(n)])


def swap(x, axis, k=1):
    n = lax.axis_size(axis)
    return lax.ppermute(x, axis, [(i, i ^ k) for i in range(n)])


def after(x, *others):
    return lax.optimization_barrier((x, *others))[0]


def gather_ctx(x):
    n = lax.axis_size("ctx")
    if n != 4:
        return [swap(x, "ctx", k) for k in range(1, n)]
    half = x.shape[0] // 2
    one, two = swap(x, "ctx", 1), swap(x, "ctx", 2)
    return [one, two, swap(one[:half], "ctx", 2), swap(two[half:], "ctx", 1)]


def xor_gather(x, axis):
    return [x] + [swap(x, axis, k) for k in range(1, lax.axis_size(axis))]


def pack_attention(n_ctx, idx, w_q, w_k, w_v, w_o, gain, buf, held, sem):
    inner, r = w_o.shape
    for v, ref in enumerate((w_q, w_k, w_v, w_o)):

        @pl.when(idx[1] == v)
        def _(ref=ref):
            copy = pltpu.make_async_copy(ref, held, sem)
            copy.start()
            copy.wait()

    buf[0:inner, 0:r] = held[...]

    buf[inner : inner + 2, 0:r] = gain[...]


def wide_tiles(r, widths):
    rp = pl.cdiv(r, 16) * 16
    row, parts = 0, []
    for n in widths:
        full, left = divmod(3 * n, LANES)
        pieces = [(row + rp * q, r, 0, LANES * q, LANES, 0) for q in range(full)]
        row += rp * full
        if left:
            assert 2 * left == LANES
            pieces.append((row, r // 2, 0, LANES * full, left, 0))
            pieces.append((row, r // 2, r // 2, LANES * full, left, left))
            row += pl.cdiv(r // 2, 8) * 8
        parts.append(pieces)
    return parts, pl.cdiv(row, 32) * 32


def pack_wide(n_ctx, widths, window, idx, w_g, w_u, w_d, buf, stage, held, sems):
    r = w_g.shape[0]
    columns = sum(widths)
    parts, _ = wide_tiles(r, widths)
    for v in range(n_ctx):

        @pl.when(idx[1] == v)
        def _(v=v):
            start = min(v * columns // LANES * LANES, w_g.shape[1] - window)
            copies = [
                pltpu.make_async_copy(ref.at[:, start : start + window], held.at[i], sems.at[i])
                for i, ref in enumerate((w_g, w_u, w_d))
            ]
            for copy in copies:
                copy.start()
            for copy in copies:
                copy.wait()
            at = v * columns - start
            for n, pieces in zip(widths, parts, strict=True):
                for i in range(3):
                    stage[:, i * n : (i + 1) * n] = held[i, :, at : at + n]
                for row, size, top, lane, lanes, to in pieces:
                    buf[row : row + size, to : to + lanes] = stage[
                        top : top + size, lane : lane + lanes
                    ]
                at += n


def bias_body(rows, seg_len, marks, idx, table, out):
    c = idx[1]
    heads, length, _ = out.shape

    def info(position):
        block = sum(((position >= rows * b).astype(jnp.int32) for b in range(1, length // rows)))
        token = (block ^ c) * rows + position - block * rows
        seg = sum(((token >= q * seg_len).astype(jnp.int32) for q in range(8, 20)))
        parent = jnp.where(seg == 0, -1, jnp.where(seg <= 4, 0, (seg - 3) >> 1))
        shift = jnp.where(seg == 0, 0, jnp.where(seg <= 4, seg - 1, seg - 2))
        return seg, parent, token - shift * seg_len

    key_seg, _, key_place = info(lax.broadcasted_iota(jnp.int32, (16, length), 1))

    def rows_of(i, _):
        at = pl.multiple_of(i * 16, 16)
        seg, parent, place = info(lax.broadcasted_iota(jnp.int32, (16, length), 0) + at)
        allowed = (key_seg == 0) | (key_seg == seg) | (key_seg == parent)
        relative = key_place - place
        magnitude = jnp.abs(relative)
        marked = sum(((magnitude >= mark).astype(jnp.int32) for mark in marks))
        bucket = jnp.where(relative > 0, 16, 0) + jnp.where(magnitude < 8, magnitude, 7 + marked)
        looked = [jnp.full(bucket.shape, table[0, h], wide) for h in range(heads)]
        for b in range(1, table.shape[0]):
            hit = bucket == b
            looked = [jnp.where(hit, table[b, h], looked[h]) for h in range(heads)]
        for h in range(heads):
            out[h, pl.ds(at, 16), :] = jnp.where(allowed, looked[h], masked_score)
        return 0

    lax.fori_loop(0, length // 16, rows_of, 0)


def norm_one(n_ctx, n_shard, idx, x_in, *refs):
    s, half = idx[0], idx[2]
    mine, rest = refs[: n_ctx - 1], refs[n_ctx - 1]
    bufs = refs[n_ctx : n_ctx + n_shard]
    normed, x_mine, x_own, gains = refs[n_ctx + n_shard :]
    r = normed.shape[2]
    _, rows, width = x_in.shape
    for k, buf in enumerate(bufs):
        at = buf.shape[0] - 16
        gains[wrap(s - k, n_shard), 0:2, :] = buf[at : at + 2, 0:r].astype(wide)
    for m in range(2):
        for k in range(n_ctx):
            if k == 0:
                x = x_in[half if m == 0 else 1 - half]
            else:
                x = mine[k - 1][...] if m == 0 else rest[k - 1]
            x = x.astype(wide)
            y = x * lax.rsqrt(jnp.mean(x * x, axis=-1, keepdims=True) + norm_eps)
            at = (m * n_ctx + k) * rows
            for j in range(n_shard):
                piece = slice(r * j, r * (j + 1))
                normed[j, at : at + rows, :] = (y[:, piece] * gains[j, 0:1, :]).astype(low)
                if m == 0:
                    x_mine[j, at : at + rows, :] = x[:, piece].astype(low)
                    if k == 0:
                        x_own[j] = x[:, piece]


def chunk_cot(n_ctx, n_shard, idx, x_in, *refs):
    half = idx[2]
    mine, rest = refs[: n_ctx - 1], refs[n_ctx - 1]
    out, own = refs[n_ctx:]
    r = out.shape[2]
    _, rows, _ = x_in.shape
    for m in range(2):
        for k in range(n_ctx):
            if k == 0:
                x = x_in[half if m == 0 else 1 - half]
            else:
                x = mine[k - 1][...] if m == 0 else rest[k - 1]
            at = (m * n_ctx + k) * rows
            for j in range(n_shard):
                out[j, at : at + rows, :] = x[:, r * j : r * (j + 1)]
                if m == 0 and k == 0:
                    own[j] = x[:, r * j : r * (j + 1)]


def attend(n_ctx, n_shard, rows, heads, place, idx, normed, w_q, w_k, w_v, w_o, bias, *refs):
    s, c = idx[0], idx[1]
    groups = 1 + max((g for pieces in place.values() for g, _, _ in pieces))
    got = [refs[g * n_ctx : (g + 1) * n_ctx] for g in range(groups)]
    att_mine, att_other, soft, qkv, mixed_own, every, mixed = refs[groups * n_ctx :]
    inner, r = w_o.shape
    length = n_ctx * rows
    for i, ref in enumerate((w_q, w_k, w_v, w_o)):
        every[s, i * inner : (i + 1) * inner, :] = ref[...]
    for v in range(n_ctx):

        @pl.when(c == v)
        def _(v=v):
            for k in range(n_ctx):
                for z, pieces in place.items():
                    at, last = (v ^ k) * inner, ((v ^ k) + 1) * inner
                    for g, row, size in pieces:
                        size = min(size, last - at)
                        every[wrap(s - z, n_shard), at : at + size, :] = got[g][k][
                            row : row + size, 0:r
                        ]
                        at += size

    for m in range(2):
        low_row = m * length
        acc = dot_nt(normed[0, low_row : low_row + length, :], every[0, 0 : 3 * inner, :])
        for j in range(1, n_shard):
            acc += dot_nt(normed[j, low_row : low_row + length, :], every[j, 0 : 3 * inner, :])
        qkv[low_row : low_row + length, :] = acc.astype(low)
        for h in range(heads):
            at = DK * h
            keys = qkv[low_row : low_row + length, inner + at : inner + at + DK]
            values = qkv[low_row : low_row + length, 2 * inner + at : 2 * inner + at + DK]
            for b in range(n_ctx):
                top = low_row + b * rows
                scores = dot_nt(qkv[top : top + rows, at : at + DK], keys)
                scores += bias[h, b * rows : (b + 1) * rows, :]
                raised = jnp.exp(scores - jnp.max(scores, axis=-1, keepdims=True))
                share = raised / jnp.sum(raised, axis=-1, keepdims=True)
                if b == 0:
                    soft[m, h] = share
                got = dot_nn(share.astype(low), values).astype(low)
                mixed[top : top + rows, at : at + DK] = got
                if b == 0:
                    mixed_own[m * rows : (m + 1) * rows, at : at + DK] = got
        out = att_mine if m == 0 else att_other
        for j in range(n_shard):
            out[j] = dot_nn(
                mixed[low_row : low_row + length, :], every[j, 3 * inner : 4 * inner, :]
            ).astype(low)


def middle_norm(n_ctx, n_shard, width, x_mine, att, got, gains, normed, middle_own):
    length = x_mine.shape[1]
    rows = length // n_ctx
    for b in range(n_ctx):
        at = slice(b * rows, (b + 1) * rows)
        mids, total = [], 0.0
        for j in range(n_shard):
            mid = x_mine[j, at, :].astype(wide) + (
                att[j, at, :].astype(wide) + got[j, at, :].astype(wide)
            )
            total += jnp.sum(mid * mid, axis=-1, keepdims=True)
            mids.append(mid)
        scale = lax.rsqrt(total / width + norm_eps)
        for j in range(n_shard):
            normed[j, at, :] = (mids[j] * scale * gains[j, 1:2, :]).astype(low)
            if b == 0:
                middle_own[j] = mids[j]


def feed_forward(n_ctx, n_shard, widths, idx, nt_mine, nt_other, cot, buf, *refs):
    sent, feed, two = refs[0], refs[1:3], refs[3:5]
    n_parts = len(widths)
    weights, hidden, pair = (refs[5 + i * n_parts : 5 + (i + 1) * n_parts] for i in range(3))
    _, length, r = nt_mine.shape
    rows = length // n_ctx
    parts, _ = wide_tiles(r, widths)
    for j in range(n_shard):
        for e, pieces in enumerate(parts):
            for row, size, top, lane, lanes, at in pieces:
                weights[e][j, top : top + size, lane : lane + lanes] = buf[
                    j, row : row + size, at : at + lanes
                ]
    w_in = [[weights[e].at[j, :, 0 : 2 * n] for j in range(n_shard)] for e, n in enumerate(widths)]
    w_down = [
        [weights[e].at[j, :, 2 * n : 3 * n] for j in range(n_shard)] for e, n in enumerate(widths)
    ]
    c0, c1 = 0.7978845608028654, 0.044715
    span = 2 * rows
    for m, nt in ((0, nt_mine), (1, nt_other)):

        def block(b, _, m=m, nt=nt):
            at = pl.ds(pl.multiple_of(b * span, span), span)
            all_at = pl.ds(pl.multiple_of(m * length + b * span, span), span)
            for e, n in enumerate(widths):
                both, back = 0.0, 0.0
                for j in range(n_shard):
                    both += dot_nn(nt[j, at, :], w_in[e][j][...])
                    back += dot_nn(cot[j, all_at, :], w_down[e][j][...])
                gate, up = both[:, :n], both[:, n:]
                square = gate * gate
                bent = jnp.tanh(c0 * (gate + c1 * gate * square))
                half_one = 0.5 * (1.0 + bent)
                active = gate * half_one
                slope = half_one + 0.5 * gate * (1.0 - bent * bent) * (
                    c0 * (1.0 + 3.0 * c1 * square)
                )
                hidden[e][all_at, :] = (active * up).astype(low)
                pair[e][all_at, 0:n] = (back * up * slope).astype(low)
                pair[e][all_at, n : 2 * n] = (back * active).astype(low)
            for j in range(n_shard):
                made, back_in = 0.0, 0.0
                for e in range(n_parts):
                    made += dot_nt(hidden[e][all_at, :], w_down[e][j][...])
                    back_in += dot_nt(pair[e][all_at, :], w_in[e][j][...])
                for i in range(2):
                    piece = slice(i * rows, (i + 1) * rows)
                    feed[m][2 * b + i, j] = made[piece].astype(low)
                    two[m][2 * b + i, j] = back_in[piece].astype(low)
            return 0

        lax.fori_loop(0, n_ctx // 2, block, 0)
    for j in range(n_shard):
        for e, n in enumerate(widths):
            for_in = dot_tn(nt_mine[j], pair[e][0:length, :])
            for_in += dot_tn(nt_other[j], pair[e][length:, :])
            for_in = for_in.astype(low)
            for_down = dot_tn(cot[j], hidden[e][...]).astype(low)
            for row, size, top, lane, lanes, at in parts[e]:
                inside = max(0, min(lanes, 2 * n - lane))
                if inside:
                    sent[j, row : row + size, at : at + inside] = for_in[
                        top : top + size, lane : lane + inside
                    ]
                if inside < lanes:
                    begin = lane + inside - 2 * n
                    sent[j, row : row + size, at + inside : at + lanes] = for_down[
                        top : top + size, begin : begin + lanes - inside
                    ]


def norm_two_back(n_shard, width, n_parts, *refs):
    parts, refs = refs[:n_parts], refs[n_parts:]
    middle, cot, gains, out_in, grad, gain_grad = refs
    mids = [middle[j] for j in range(n_shard)]
    twos = [sum((p[j].astype(wide) for p in parts)) for j in range(n_shard)]
    mean = sum((jnp.sum(a * a, axis=-1, keepdims=True) for a in mids)) / width
    scale = lax.rsqrt(mean + norm_eps)
    us = [twos[j] * gains[j, 1:2, :] for j in range(n_shard)]
    inner = sum((jnp.sum(a * b, axis=-1, keepdims=True) for a, b in zip(us, mids, strict=True)))
    inner = inner / width * (scale * scale * scale)
    for j in range(n_shard):
        back = cot[j].astype(wide) + scale * us[j] - mids[j] * inner
        grad[j] = back
        out_in[j] = back.astype(low)
        gain_grad[j] = jnp.sum(twos[j] * mids[j] * scale, axis=0, keepdims=True)


def attend_back(n_ctx, n_shard, heads, idx, o_mine, o_other, soft, qkv, mixed, every, normed, *refs):
    s, c = idx[0], idx[1]
    kv, (q_grad, stack, kv_all, mixed_grad) = refs[:n_ctx], refs[n_ctx:]
    _, rows, r = o_mine.shape
    length = n_ctx * rows
    inner = heads * DK
    for m, o_in in ((0, o_mine), (1, o_other)):
        top, own = m * length, m * rows
        acc = 0.0
        for j in range(n_shard):
            acc += dot_nt(o_in[j], every[j, 3 * inner : 4 * inner, :])
        mixed_grad[own : own + rows, :] = acc.astype(low)
        for h in range(heads):
            at = DK * h
            share = soft[m, h]
            grad = mixed_grad[own : own + rows, at : at + DK]
            keys = qkv[top : top + length, inner + at : inner + at + DK]
            values = qkv[top : top + length, 2 * inner + at : 2 * inner + at + DK]
            queries = qkv[top : top + rows, at : at + DK]
            weight = dot_nt(grad, values)
            ds = share * (weight - jnp.sum(weight * share, axis=-1, keepdims=True))
            ds = ds.astype(low)
            q_grad[own : own + rows, at : at + DK] = dot_nn(ds, keys).astype(low)
            kv_all[top : top + length, at : at + DK] = dot_tn(ds, queries).astype(low)
            kv_all[top : top + length, inner + at : inner + at + DK] = dot_tn(
                share.astype(low), grad
            ).astype(low)
        for k in range(n_ctx):
            kv[k][own : own + rows, :] = kv_all[top + k * rows : top + (k + 1) * rows, :]
    for p in range(n_shard):
        j = wrap(s + p, n_shard)
        for_q = dot_tn(q_grad[0:rows, :], normed[j, 0:rows, :])
        for_q += dot_tn(q_grad[rows:, :], normed[j, length : length + rows, :])
        for_kv = dot_tn(kv_all[...], normed[j])
        for_o = dot_tn(mixed[0:rows, :], o_mine[j]) + dot_tn(mixed[rows:, :], o_other[j])
        stack[c, p] = for_q.astype(low)
        stack[c ^ 1, p] = for_kv[0:inner].astype(low)
        stack[c ^ 2, p] = for_kv[inner:].astype(low)
        stack[c ^ 3, p] = for_o.astype(low)


def first_grad(n_shard, n_parts, *refs):
    parts, (q_grad, every, out_mine, out_other, three) = refs[:n_parts], refs[n_parts:]
    rows2, inner = q_grad.shape
    rows = rows2 // 2
    three[:, 0:inner] = q_grad[...]
    three[:, inner:] = sum((p[...].astype(wide) for p in parts)).astype(low)
    for j in range(n_shard):
        got = dot_nn(three[...], every[j, 0 : 3 * inner, :]).astype(low)
        out_mine[j] = got[0:rows]
        out_other[j] = got[rows:]


def norm_one_back(n_shard, width, mine, got, x_own, grad, gains, out, gain_grad):
    r = x_own.shape[2]
    xs = [x_own[j] for j in range(n_shard)]
    ones = [mine[j].astype(wide) + got[j].astype(wide) for j in range(n_shard)]
    mean = sum((jnp.sum(a * a, axis=-1, keepdims=True) for a in xs)) / width
    scale = lax.rsqrt(mean + norm_eps)
    us = [ones[j] * gains[j, 0:1, :] for j in range(n_shard)]
    inner = sum((jnp.sum(a * b, axis=-1, keepdims=True) for a, b in zip(us, xs, strict=True)))
    inner = inner / width * (scale * scale * scale)
    for j in range(n_shard):
        back = grad[j] + scale * us[j] - xs[j] * inner
        out[:, r * j : r * (j + 1)] = back.astype(low)
        gain_grad[j] = jnp.sum(ones[j] * xs[j] * scale, axis=0, keepdims=True)


def produce(n_shard, n_parts, *refs):
    parts, (middle, out) = refs[:n_parts], refs[n_parts:]
    r = middle.shape[2]
    for j in range(n_shard):
        fed = sum((p[j].astype(wide) for p in parts))
        out[:, r * j : r * (j + 1)] = (middle[j] + fed).astype(low)


def finish_wide(n_ctx, widths, idx, own, *refs):
    n_got = len(refs) - 4
    got, (out_g, out_u, out_d, stage) = refs[:n_got], refs[n_got:]
    r = out_g.shape[0]
    columns = sum(widths)
    parts, rows = wide_tiles(r, widths)
    sources = [[own], [got[0]], [got[1]], list(got[2:])] if n_ctx == 4 else [[own]] + [[g] for g in got]
    for k, source in enumerate(sources):
        size_each = rows // len(source)
        for i, n in enumerate(widths):
            for row, size, top, lane, lanes, at in parts[i]:
                done = 0
                while done < size:
                    which, here = divmod(row + done, size_each)
                    count = min(size - done, size_each - here)
                    stage[top + done : top + done + count, lane : lane + lanes] = source[which][
                        here : here + count, at : at + lanes
                    ].astype(wide)
                    done += count
            for v in range(n_ctx):

                @pl.when(idx[1] == v)
                def _(v=v, n=n, i=i, k=k):
                    at = (v ^ k) * columns + sum(widths[:i])
                    for j, out in enumerate((out_g, out_u, out_d)):
                        out[:, at : at + n] = stage[:, j * n : (j + 1) * n]


def finish_attention(n_ctx, idx, *refs):
    pieces, outs = refs[:n_ctx], refs[n_ctx:]
    for v in range(n_ctx):

        @pl.when(idx[1] == v)
        def _(v=v):
            for k in range(n_ctx):
                outs[v ^ k][...] = pieces[k][...].astype(wide)


def on_device(
    inputs,
    cotangent,
    norm1_gain,
    w_query,
    w_key,
    w_value,
    w_out,
    norm2_gain,
    w_gate,
    w_up,
    w_down,
    bias_table,
):
    _, rows, width = inputs.shape
    shards, ctx = lax.axis_size("shard"), lax.axis_size("ctx")
    inner, r = w_out.shape
    heads = inner // DK
    length = ctx * rows
    columns = w_gate.shape[1] // ctx
    first_width = pl.cdiv(columns, 2 * LANES) * LANES
    widths = (first_width, columns - first_width)
    lanes_r = pl.cdiv(r, LANES) * LANES
    s, c, half = lax.axis_index("shard"), lax.axis_index("ctx"), lax.axis_index("tensor")
    idx = jnp.stack([s, c, half]).astype(jnp.int32)
    attention_weights = (w_query.T, w_key.T, w_value.T, w_out)


    wide_rows = wide_tiles(r, widths)[1]
    window = min(pl.cdiv(columns, LANES) * LANES, w_gate.shape[1])
    (packed,) = run(
        functools.partial(pack_wide, ctx, widths, window),
        "pack_wide",
        [((wide_rows, LANES), low)],
        [idx, w_gate, w_up, w_down.T],
        scratch=[
            pltpu.VMEM((r, 3 * max(widths)), low),
            pltpu.VMEM((3, r, window), low),
            pltpu.SemaphoreType.DMA((3,)),
        ],
        cost=2,
        far=3,
    )
    chunks = lax.all_gather(packed, "shard", axis=0, tiled=False)
    own_x = lax.dynamic_index_in_dim(inputs, half, 0, keepdims=False)
    (own_buf,) = run(
        functools.partial(pack_attention, ctx),
        "pack_attention",
        [((inner + 16, lanes_r), low)],
        [after(idx, packed), *attention_weights, jnp.stack([norm1_gain, norm2_gain])],
        scratch=[pltpu.VMEM((inner, r), low), pltpu.SemaphoreType.DMA],
        far=4,
    )
    from_shard = [step(own_buf, "shard", k) for k in range(1, shards)]
    mine_x = [swap(own_x, "ctx", k) for k in range(1, ctx)]
    table = lax.dynamic_slice_in_dim(bias_table, half * heads, heads, 1)
    (bias,) = run(
        functools.partial(bias_body, rows, rows // 5, distance_marks),
        "bias",
        [((heads, length, length), wide)],
        [after(idx, own_buf), table],
        scalars=2,
        cost=5,
    )
    now = after(idx, *from_shard, *mine_x, bias)

    group = jnp.concatenate(from_shard)
    buf_rows = inner + 16
    place = {z: [(0, (z - 1) * buf_rows, inner)] for z in range(1, shards)}
    gathered = [group] + [swap(after(group, now), "ctx", k) for k in range(1, ctx)]
    rest_x = swap(after(jnp.stack(mine_x), now), "tensor")
    normed_one, x_mine, x_own, gains = run(
        functools.partial(norm_one, ctx, shards),
        "norm_one",
        [
            ((shards, 2 * length, r), low),
            ((shards, length, r), low),
            ((shards, rows, r), wide),
            ((shards, 2, r), wide),
        ],
        [now, inputs, *mine_x, rest_x, own_buf, *from_shard],
        cost=3,
    )
    now = after(now, *gathered[1:], normed_one)

    own_cot = lax.dynamic_index_in_dim(cotangent, half, 0, keepdims=False)
    mine_cot = [swap(after(own_cot, now), "ctx", k) for k in range(1, ctx)]
    att_mine, att_other, soft, qkv, mixed_own, every = run(
        functools.partial(attend, ctx, shards, rows, heads, place),
        "attend",
        [
            ((shards, length, r), low),
            ((shards, length, r), low),
            ((2, heads, rows, length), wide),
            ((2 * length, 3 * inner), low),
            ((2 * rows, inner), low),
            ((shards, 4 * inner, r), low),
        ],
        [now, normed_one, *attention_weights, bias, *gathered],
        scratch=[pltpu.VMEM((2 * length, inner), low)],
        cost=14,
    )
    now = after(now, *mine_cot, att_other)

    att_got = swap(after(att_other, now), "tensor")
    rest_cot = swap(after(jnp.stack(mine_cot), now), "tensor")
    nt_mine, middle_own = run(
        functools.partial(middle_norm, ctx, shards, width),
        "middle_norm",
        [((shards, length, r), low), ((shards, rows, r), wide)],
        [x_mine, att_mine, att_got, gains],
        scalars=0,
    )
    nt_other = swap(nt_mine, "tensor")
    cot, cot_own = run(
        functools.partial(chunk_cot, ctx, shards),
        "chunk_cot",
        [((shards, 2 * length, r), low), ((shards, rows, r), low)],
        [now, cotangent, *mine_cot, rest_cot],
        cost=1,
    )
    now = after(now, nt_other, cot)

    def add(a, b):
        return (a.astype(wide) + b.astype(wide)).astype(low)

    tokens_out = ((ctx, shards, rows, r), low)
    wide_grads, feed_mine, feed_other, two_mine, two_other = run(
        functools.partial(feed_forward, ctx, shards, widths),
        "feed_forward",
        [((shards, wide_rows, LANES), low)] + [tokens_out] * 4,
        [now, nt_mine, nt_other, cot, chunks],
        scratch=[pltpu.VMEM((shards, r, 3 * n), low) for n in widths]
        + [pltpu.VMEM((2 * length, n), low) for n in widths]
        + [pltpu.VMEM((2 * length, 2 * n), low) for n in widths],
        cost=20,
        vmem=48,
    )
    wide_own = lax.psum_scatter(wide_grads, "shard", scatter_dimension=0, tiled=False)
    now = after(now, two_other)

    two_got = swap(after(two_other, now), "tensor")
    two_both = [add(two_mine[k], two_got[k]) for k in range(ctx)]
    feed_got = swap(after(feed_other, two_got), "tensor")
    feed_both = [add(feed_mine[k], feed_got[k]) for k in range(ctx)]
    now = after(now, *two_both, *feed_both)

    two_parts = [two_both[0]] + [swap(after(two_both[k], now), "ctx", k) for k in range(1, ctx)]
    out_in, middle_grad, gain_two = run(
        functools.partial(norm_two_back, shards, width, ctx),
        "norm_two_back",
        [((shards, rows, r), low), ((shards, rows, r), wide), ((shards, 1, r), wide)],
        [*two_parts, middle_own, cot_own, gains],
        scalars=0,
    )
    out_in_other = swap(out_in, "tensor")
    now = after(now, out_in_other)

    feed_parts = [feed_both[0]] + [swap(after(feed_both[k], now), "ctx", k) for k in range(1, ctx)]
    got = run(
        functools.partial(attend_back, ctx, shards, heads),
        "attend_back",
        [((2 * rows, 2 * inner), low)] * ctx
        + [((2 * rows, inner), low), ((4, shards, inner, r), low)],
        [now, out_in, out_in_other, soft, qkv, mixed_own, every, normed_one],
        scratch=[pltpu.VMEM((2 * length, 2 * inner), low), pltpu.VMEM((2 * rows, inner), low)],
        cost=6,
    )
    kv_parts, q_grad, stack = got[:ctx], got[ctx], got[ctx + 1]
    now = after(now, *feed_parts[1:], q_grad)

    kv_parts = [kv_parts[0]] + [swap(after(kv_parts[k], now), "ctx", k) for k in range(1, ctx)]
    four_got = [swap(after(stack[k], now), "ctx", k) for k in range(1, 3)]
    (produced_mine,) = run(
        functools.partial(produce, shards, ctx),
        "produce",
        [((rows, width), low)],
        [*feed_parts, middle_own],
        scalars=0,
    )
    produced_other = swap(after(produced_mine, now), "tensor")
    now = after(now, *kv_parts, *four_got, produced_other)

    four_got += [swap(after(stack[k], now), "ctx", k) for k in range(3, ctx)]
    first_mine, first_other = run(
        functools.partial(first_grad, shards, ctx),
        "first_grad",
        [((shards, rows, r), low)] * 2,
        [*kv_parts, q_grad, every],
        scalars=0,
        scratch=[pltpu.VMEM((2 * rows, 3 * inner), low)],
    )
    first_got = swap(after(first_other, now), "tensor")
    input_mine, gain_one = run(
        functools.partial(norm_one_back, shards, width),
        "norm_one_back",
        [((rows, width), low), ((shards, 1, r), wide)],
        [first_mine, first_got, x_own, middle_grad, gains],
        scalars=0,
    )
    input_other = swap(input_mine, "tensor")
    gain = jnp.concatenate([gain_one, gain_two], 1)
    gain = gain + swap(gain, "tensor")
    now = after(now, *four_got, input_other, gain)

    four = stack[0].astype(wide)
    for got in four_got:
        four = four + got.astype(wide)
    four = four.astype(low)
    four_shard = [four[0]] + [step(after(four[d], now), "shard", d) for d in range(1, shards)]
    gain_got = [swap(after(gain, now), "ctx", k) for k in range(1, ctx)]
    now = after(now, *four_shard, *gain_got)

    four_own = sum((part.astype(wide) for part in four_shard)).astype(low)
    four_all = [four_own] + [swap(after(four_own, now), "ctx", k) for k in range(1, ctx)]
    gain = gain + sum(gain_got)
    own_gain = lax.dynamic_index_in_dim(gain, s, 0, keepdims=False)
    for k in range(1, shards):
        part = lax.dynamic_index_in_dim(gain, wrap(s + k, shards), 0, keepdims=False)
        own_gain = own_gain + step(after(part, now), "shard", k)
    out_q, out_k, out_v, out_o = run(
        functools.partial(finish_attention, ctx),
        "finish_attention",
        [((inner, r), wide)] * 4,
        [now, *four_all],
    )
    now = after(now, out_q, own_gain)

    wide_own = after(wide_own, now)
    wide_all = gather_ctx(wide_own)
    out_g, out_u, out_d = run(
        functools.partial(finish_wide, ctx, widths),
        "finish_wide",
        [(w_gate.shape, wide)] * 3,
        [now, wide_own, *wide_all],
        scratch=[pltpu.VMEM((r, 3 * max(widths)), wide)],
        cost=5,
    )

    def ordered(mine, other):
        return jnp.where(half == 0, jnp.stack([mine, other]), jnp.stack([other, mine]))

    return (
        ordered(produced_mine, produced_other),
        ordered(input_mine, input_other),
        own_gain[0],
        out_q.T,
        out_k.T,
        out_v.T,
        out_o,
        own_gain[1],
        out_g,
        out_u,
        out_d.T,
    )


def solution(mesh):
    placed = (
        P(None, ("shard", "ctx"), None),
        P(None, ("shard", "ctx"), None),
        P("shard"),
        P("shard", "tensor"),
        P("shard", "tensor"),
        P("shard", "tensor"),
        P("tensor", "shard"),
        P("shard"),
        P("shard", "tensor"),
        P("shard", "tensor"),
        P("tensor", "shard"),
        P(),
    )
    return jax.shard_map(
        on_device, mesh=mesh, in_specs=placed, out_specs=placed[:2] + placed[2:11], check_vma=False
    )
```

```python
import functools

import jax
import jax.numpy as jnp
from jax import lax
from jax.experimental import pallas as pl
from jax.experimental.pallas import tpu as pltpu
from jax.sharding import PartitionSpec as P

DK = 64
norm_eps = 1e-06
distance_marks = (8, 12, 16, 23, 32, 46, 64, 91)
masked_score = -1e30
low = jnp.bfloat16
wide = jnp.float32
LANES = 128
COST = 1e8


def dot_nn(left, right):
    return lax.dot_general(left, right, (((1,), (0,)), ((), ())), preferred_element_type=wide)


def dot_nt(left, right):
    return lax.dot_general(left, right, (((1,), (1,)), ((), ())), preferred_element_type=wide)


def dot_tn(left, right):
    return lax.dot_general(left, right, (((0,), (0,)), ((), ())), preferred_element_type=wide)


def wrap(value, n):
    return lax.rem(value + 2 * n, n)


def run(body, name, outs, operands, scratch=(), scalars=1, cost=1, far=0, far_out=False, into=0, vmem=16):
    return pl.pallas_call(
        body,
        name=name,
        out_shape=[jax.ShapeDtypeStruct(s, d) for s, d in outs],
        in_specs=[pl.BlockSpec(memory_space=pltpu.SMEM)] * scalars
        + [pl.BlockSpec(memory_space=pltpu.HBM)] * far
        + [pl.BlockSpec(memory_space=pltpu.VMEM)] * (len(operands) - scalars - far - into)
        + [pl.BlockSpec(memory_space=pltpu.HBM)] * into,
        out_specs=[pl.BlockSpec(memory_space=pltpu.HBM if far_out else pltpu.VMEM)] * len(outs),
        scratch_shapes=list(scratch),
        input_output_aliases={len(operands) - into + i: i for i in range(into)},
        compiler_params=pltpu.CompilerParams(vmem_limit_bytes=vmem * 2**20),
        cost_estimate=pl.CostEstimate(flops=int(cost * COST), bytes_accessed=0, transcendentals=0),
    )(*operands)


def step(x, axis, k=1):
    n = lax.axis_size(axis)
    return lax.ppermute(x, axis, [(i, (i + k) % n) for i in range(n)])


def swap(x, axis, k=1):
    n = lax.axis_size(axis)
    return lax.ppermute(x, axis, [(i, i ^ k) for i in range(n)])


def after(x, *others):
    return lax.optimization_barrier((x, *others))[0]


def pack_attention(n_ctx, idx, w_q, w_k, w_v, w_o, gain, buf, held, sem):
    inner, r = w_o.shape
    for v, ref in enumerate((w_q, w_k, w_v, w_o)):

        @pl.when(idx[1] == v)
        def _(ref=ref):
            copy = pltpu.make_async_copy(ref, held, sem)
            copy.start()
            copy.wait()

    buf[0:inner, 0:r] = held[...]

    buf[inner : inner + 2, 0:r] = gain[...]


def wide_tiles(r, widths):
    rp = pl.cdiv(r, 16) * 16
    row, parts = 0, []
    for n in widths:
        full, left = divmod(3 * n, LANES)
        pieces = [(row + rp * q, r, 0, LANES * q, LANES, 0) for q in range(full)]
        row += rp * full
        if left:
            assert 2 * left == LANES
            pieces.append((row, r // 2, 0, LANES * full, left, 0))
            pieces.append((row, r // 2, r // 2, LANES * full, left, left))
            row += pl.cdiv(r // 2, 8) * 8
        parts.append(pieces)
    return parts, pl.cdiv(row, 32) * 32


def pack_wide(n_ctx, widths, window, idx, w_g, w_u, w_d, buf, stage, held, sems):
    r = w_g.shape[0]
    columns = sum(widths)
    parts, _ = wide_tiles(r, widths)
    for v in range(n_ctx):

        @pl.when(idx[1] == v)
        def _(v=v):
            start = min(v * columns // LANES * LANES, w_g.shape[1] - window)
            copies = [
                pltpu.make_async_copy(ref.at[:, start : start + window], held.at[i], sems.at[i])
                for i, ref in enumerate((w_g, w_u, w_d))
            ]
            for copy in copies:
                copy.start()
            for copy in copies:
                copy.wait()
            at = v * columns - start
            for n, pieces in zip(widths, parts, strict=True):
                for i in range(3):
                    stage[:, i * n : (i + 1) * n] = held[i, :, at : at + n]
                for row, size, top, lane, lanes, to in pieces:
                    buf[row : row + size, to : to + lanes] = stage[
                        top : top + size, lane : lane + lanes
                    ]
                at += n


def bias_body(rows, seg_len, marks, idx, table, out):
    c = idx[1]
    heads, length, _ = out.shape

    def info(position):
        block = sum(((position >= rows * b).astype(jnp.int32) for b in range(1, length // rows)))
        token = (block ^ c) * rows + position - block * rows
        seg = sum(((token >= q * seg_len).astype(jnp.int32) for q in range(8, 20)))
        parent = jnp.where(seg == 0, -1, jnp.where(seg <= 4, 0, (seg - 3) >> 1))
        shift = jnp.where(seg == 0, 0, jnp.where(seg <= 4, seg - 1, seg - 2))
        return seg, parent, token - shift * seg_len

    key_seg, _, key_place = info(lax.broadcasted_iota(jnp.int32, (16, length), 1))

    def rows_of(i, _):
        at = pl.multiple_of(i * 16, 16)
        seg, parent, place = info(lax.broadcasted_iota(jnp.int32, (16, length), 0) + at)
        allowed = (key_seg == 0) | (key_seg == seg) | (key_seg == parent)
        relative = key_place - place
        magnitude = jnp.abs(relative)
        marked = sum(((magnitude >= mark).astype(jnp.int32) for mark in marks))
        bucket = jnp.where(relative > 0, 16, 0) + jnp.where(magnitude < 8, magnitude, 7 + marked)
        looked = [jnp.full(bucket.shape, table[0, h], wide) for h in range(heads)]
        for b in range(1, table.shape[0]):
            hit = bucket == b
            looked = [jnp.where(hit, table[b, h], looked[h]) for h in range(heads)]
        for h in range(heads):
            out[h, pl.ds(at, 16), :] = jnp.where(allowed, looked[h], masked_score)
        return 0

    lax.fori_loop(0, length // 16, rows_of, 0)


def tree_blocks(n_ctx, half, own, mine, rest):
    for k in range(n_ctx):
        yield 0, k, own[half] if k == 0 else mine[k - 1][...]
    for k in range(n_ctx):
        yield 1, k, own[1 - half] if k == 0 else rest[k - 1]


def norm_one(n_ctx, n_shard, idx, x_in, *refs):
    s, half = idx[0], idx[2]
    mine, rest = refs[: n_ctx - 1], refs[n_ctx - 1]
    bufs = refs[n_ctx : n_ctx + n_shard]
    normed, gains, held = refs[n_ctx + n_shard :]
    r = held.shape[2]
    _, rows, width = x_in.shape
    for k, buf in enumerate(bufs):
        at = buf.shape[0] - 16
        held[wrap(s - k, n_shard), 0:2, :] = buf[at : at + 2, 0:r].astype(wide)
    for j in range(n_shard):
        gains[:, r * j : r * (j + 1)] = held[j, 0:2, :]
    for m, k, x in tree_blocks(n_ctx, half, x_in, mine, rest):
        x = x.astype(wide)
        y = x * lax.rsqrt(jnp.mean(x * x, axis=-1, keepdims=True) + norm_eps)
        at = (m * n_ctx + k) * rows
        normed[at : at + rows, :] = (y * gains[0:1, :]).astype(low)


def attend(n_ctx, n_shard, rows, heads, place, idx, normed, w_q, w_k, w_v, w_o, bias, *refs):
    s, c = idx[0], idx[1]
    groups = 1 + max((g for pieces in place.values() for g, _, _ in pieces))
    got = [refs[g * n_ctx : (g + 1) * n_ctx] for g in range(groups)]
    att_mine, att_other, soft, qkv, mixed, every, held = refs[groups * n_ctx :]
    inner, r = w_o.shape
    length = n_ctx * rows
    for i, ref in enumerate((w_q, w_k, w_v, w_o)):
        held[s, i * inner : (i + 1) * inner, :] = ref[...]
    for v in range(n_ctx):

        @pl.when(c == v)
        def _(v=v):
            for k in range(n_ctx):
                for z, pieces in place.items():
                    at, last = (v ^ k) * inner, ((v ^ k) + 1) * inner
                    for g, row, size in pieces:
                        size = min(size, last - at)
                        held[wrap(s - z, n_shard), at : at + size, :] = got[g][k][
                            row : row + size, 0:r
                        ]
                        at += size

    for j in range(n_shard):
        every[:, r * j : r * (j + 1)] = held[j]
    qkv[...] = dot_nt(normed[...], every[0 : 3 * inner, :]).astype(low)
    for m in (1, 0):
        low_row = m * length
        for h in range(heads):
            at = DK * h
            keys = qkv[low_row : low_row + length, inner + at : inner + at + DK]
            values = qkv[low_row : low_row + length, 2 * inner + at : 2 * inner + at + DK]
            for b in range(n_ctx):
                top = low_row + b * rows
                scores = dot_nt(qkv[top : top + rows, at : at + DK], keys)
                scores += bias[h, b * rows : (b + 1) * rows, :]
                raised = jnp.exp(scores - jnp.max(scores, axis=-1, keepdims=True))
                share = raised / jnp.sum(raised, axis=-1, keepdims=True)
                if b == 0:
                    soft[m, h] = share
                mixed[top : top + rows, at : at + DK] = dot_nn(share.astype(low), values).astype(low)
        out = att_mine if m == 0 else att_other
        out[...] = dot_nn(
            mixed[low_row : low_row + length, :], every[3 * inner : 4 * inner, :]
        ).astype(low)


def middle_norm(n_ctx, idx, x_in, *refs):
    mine, (att, got, gains, normed, middle_own) = refs[: n_ctx - 1], refs[n_ctx - 1 :]
    rows = x_in.shape[1]
    for k in range(n_ctx):
        at = slice(k * rows, (k + 1) * rows)
        x = x_in[idx[2]] if k == 0 else mine[k - 1][...]
        mid = x.astype(wide) + (att[at, :].astype(wide) + got[at, :].astype(wide))
        scale = lax.rsqrt(jnp.mean(mid * mid, axis=-1, keepdims=True) + norm_eps)
        normed[at, :] = (mid * scale * gains[1:2, :]).astype(low)
        if k == 0:
            middle_own[...] = mid


def feed_forward(n_ctx, n_shard, widths, idx, buf_far, nt_mine, nt_other, cot_in, *refs):
    half = idx[2]
    mine, rest, refs = refs[: n_ctx - 1], refs[n_ctx - 1], refs[n_ctx:]
    sent, feed, two = refs[0], refs[1:3], refs[3:5]
    n_parts = len(widths)
    buf, nt, cot, feed_held, two_held, sems, sems_out = refs[5:12]
    weights, hidden, pair = (refs[12 + i * n_parts : 12 + (i + 1) * n_parts] for i in range(3))
    length, _ = nt_mine.shape
    rows = length // n_ctx
    r = weights[0].shape[0] // n_shard

    def blocks(m, first, count=1):
        at = (m * n_ctx + first) * rows
        return slice(at, at + count * rows)

    begun = [pltpu.make_async_copy(buf_far.at[0], buf.at[0], sems.at[0])]
    moves = [
        (nt_mine, nt.at[0:length, :]),
        (nt_other, nt.at[length : 2 * length, :]),
        (cot_in.at[half], cot.at[blocks(0, 0), :]),
        (cot_in.at[1 - half], cot.at[blocks(1, 0), :]),
    ]
    moves += [(buf_far.at[j], buf.at[j]) for j in range(1, n_shard)]
    for k in range(1, n_ctx):
        moves.append((mine[k - 1], cot.at[blocks(0, k), :]))
        moves.append((rest.at[k - 1], cot.at[blocks(1, k), :]))
    begun += [pltpu.make_async_copy(a, b, sems.at[i + 1]) for i, (a, b) in enumerate(moves)]
    for copy in begun:
        copy.start()
    loads = [begun[0]] + begun[5 : 4 + n_shard]
    parts, _ = wide_tiles(r, widths)
    for j in range(n_shard):
        loads[j].wait()
        for e, pieces in enumerate(parts):
            for row, size, top, lane, lanes, at in pieces:
                weights[e][r * j + top : r * j + top + size, lane : lane + lanes] = buf[
                    j, row : row + size, at : at + lanes
                ]
    for copy in begun[1:5] + begun[4 + n_shard :]:
        copy.wait()
    c0, c1 = 0.7978845608028654, 0.044715
    out = []

    def write(source, target):
        copy = pltpu.make_async_copy(source, target, sems_out.at[len(out)])
        copy.start()
        out.append(copy)

    for m in (1, 0):
        at = slice(m * length, (m + 1) * length)
        for e, n in enumerate(widths):
            both = dot_nn(nt[at, :], weights[e][:, 0 : 2 * n])
            back = dot_nn(cot[at, :], weights[e][:, 2 * n : 3 * n])
            gate, up = both[:, :n], both[:, n:]
            square = gate * gate
            bent = jnp.tanh(c0 * (gate + c1 * gate * square))
            half_one = 0.5 * (1.0 + bent)
            active = gate * half_one
            slope = half_one + 0.5 * gate * (1.0 - bent * bent) * (c0 * (1.0 + 3.0 * c1 * square))
            hidden[e][at, :] = (active * up).astype(low)
            pair[e][at, 0:n] = (back * up * slope).astype(low)
            pair[e][at, n : 2 * n] = (back * active).astype(low)
        for held, given, make in (
            (two_held, two, lambda e, n: dot_nt(pair[e][at, :], weights[e][:, 0 : 2 * n])),
            (feed_held, feed, lambda e, n: dot_nt(hidden[e][at, :], weights[e][:, 2 * n : 3 * n])),
        ):
            total = sum((make(e, n) for e, n in enumerate(widths)))
            for i in range(n_ctx):
                held[m, i] = total[i * rows : (i + 1) * rows].astype(low)
            write(held.at[m], given[m])
    for e, n in enumerate(widths):
        for_in = dot_tn(nt[...], pair[e][...]).astype(low)
        for_down = dot_tn(cot[...], hidden[e][...]).astype(low)
        first, last = parts[e][0][0], parts[e][-1][0] + parts[e][-1][1]
        for j in range(n_shard):
            for row, size, top, lane, lanes, at in parts[e]:
                top = r * j + top
                inside = max(0, min(lanes, 2 * n - lane))
                if inside:
                    buf[j, row : row + size, at : at + inside] = for_in[
                        top : top + size, lane : lane + inside
                    ]
                if inside < lanes:
                    begin = lane + inside - 2 * n
                    buf[j, row : row + size, at + inside : at + lanes] = for_down[
                        top : top + size, begin : begin + lanes - inside
                    ]
            here = slice(first, last if e < n_parts - 1 else buf.shape[1])
            write(buf.at[j, here, :], sent.at[j, here, :])
    for copy in out:
        copy.wait()


def norm_two_back(n_shard, n_parts, idx, cot_in, *refs):
    parts, refs = refs[:n_parts], refs[n_parts:]
    middle, gains, out_in, grad, gain_grad = refs
    r = gain_grad.shape[2]
    mid = middle[...]
    two = sum((p[...].astype(wide) for p in parts))
    scale = lax.rsqrt(jnp.mean(mid * mid, axis=-1, keepdims=True) + norm_eps)
    u = two * gains[1:2, :]
    inner = jnp.mean(u * mid, axis=-1, keepdims=True) * (scale * scale * scale)
    back = cot_in[idx[2]].astype(wide) + scale * u - mid * inner
    grad[...] = back
    out_in[...] = back.astype(low)
    total = jnp.sum(two * mid * scale, axis=0, keepdims=True)
    for j in range(n_shard):
        gain_grad[j] = total[:, r * j : r * (j + 1)]


def attend_back(n_ctx, heads, o_mine, o_other, soft, qkv, every, *refs):
    kv, (q_grad, kv_all, mixed_grad) = refs[:n_ctx], refs[n_ctx:]
    rows = o_mine.shape[0]
    length = n_ctx * rows
    inner = heads * DK
    for m, o_in in ((0, o_mine), (1, o_other)):
        top, own = m * length, m * rows
        mixed_grad[own : own + rows, :] = dot_nt(o_in[...], every[3 * inner :, :]).astype(low)
        for h in range(heads):
            at = DK * h
            share = soft[m, h]
            grad = mixed_grad[own : own + rows, at : at + DK]
            keys = qkv[top : top + length, inner + at : inner + at + DK]
            values = qkv[top : top + length, 2 * inner + at : 2 * inner + at + DK]
            queries = qkv[top : top + rows, at : at + DK]
            weight = dot_nt(grad, values)
            ds = share * (weight - jnp.sum(weight * share, axis=-1, keepdims=True))
            ds = ds.astype(low)
            q_grad[own : own + rows, at : at + DK] = dot_nn(ds, keys).astype(low)
            kv_all[top : top + length, at : at + DK] = dot_tn(ds, queries).astype(low)
            kv_all[top : top + length, inner + at : inner + at + DK] = dot_tn(
                share.astype(low), grad
            ).astype(low)
        for k in range(n_ctx):
            kv[k][own : own + rows, :] = kv_all[top + k * rows : top + (k + 1) * rows, :]


def first_grad(n_ctx, idx, *refs):
    parts, (q_grad, every, out_mine, out_other), pieces, three = (
        refs[:n_ctx],
        refs[n_ctx : n_ctx + 4],
        refs[n_ctx + 4 : 2 * n_ctx + 4],
        refs[2 * n_ctx + 4],
    )
    rows2, inner = q_grad.shape
    rows = rows2 // 2
    three[:, 0:inner] = q_grad[...]
    three[:, inner:] = sum((p[...].astype(wide) for p in parts)).astype(low)
    for v in range(n_ctx):

        @pl.when(idx[1] == v)
        def _(v=v):
            for k in range(n_ctx):
                which = min(v ^ k, 2)
                pieces[k][...] = three[:, which * inner : (which + 1) * inner]

    got = dot_nn(three[...], every[0 : 3 * inner, :]).astype(low)
    out_mine[...] = got[0:rows]
    out_other[...] = got[rows:]


def weight_grads(n_ctx, n_shard, idx, normed, mixed, *refs):
    pieces, outs_mine, refs = refs[:n_ctx], refs[n_ctx : 2 * n_ctx], refs[2 * n_ctx :]
    outs_rest, gain_one, gain_two = refs[:2], refs[2], refs[3]
    stack, grads, held, pieces_held, sems = refs[4:]
    s, c = idx[0], idx[1]
    rows = outs_mine[0].shape[0]
    length = n_ctx * rows
    r = stack.shape[2]
    inner = grads.shape[1]
    for j in range(n_shard):
        stack[wrap(j - s, n_shard), inner : inner + 1, :] = gain_one[j].astype(low)
        stack[wrap(j - s, n_shard), inner + 1 : inner + 2, :] = gain_two[j].astype(low)

    def fetch(moves):
        copies = [pltpu.make_async_copy(x, y, sems.at[i]) for i, (x, y) in enumerate(moves)]
        for copy in copies:
            copy.start()
        for copy in copies:
            copy.wait()

    def emit(got):
        for j in range(n_shard):
            stack[wrap(j - s, n_shard), 0:inner, :] = got[:, r * j : r * (j + 1)].astype(low)

    @pl.when(c != 3)
    def _():
        fetch([(normed, held)] + [(pieces[k], pieces_held.at[k]) for k in range(n_ctx)])
        for m in range(2):
            for k in range(n_ctx):
                at = (m * n_ctx + k) * rows
                grads[at : at + rows, :] = pieces_held[k, m * rows : (m + 1) * rows, :]
        emit(dot_tn(grads[...], held[...]))

    @pl.when(c == 3)
    def _():
        moves = [(mixed, grads)]
        for k in range(n_ctx):
            moves.append((outs_mine[k], held.at[k * rows : (k + 1) * rows, :]))
        moves.append((outs_rest[0], held.at[length : length + rows, :]))
        for k in range(1, n_ctx):
            at = length + k * rows
            moves.append((outs_rest[1].at[k - 1], held.at[at : at + rows, :]))
        fetch(moves)
        emit(dot_tn(grads[...], held[...]))


def place_outputs(idx, a_mine, a_other, b_mine, b_other, a, b):
    half = idx[2]
    a[half] = a_mine[...]
    a[1 - half] = a_other[...]
    b[half] = b_mine[...]
    b[1 - half] = b_other[...]


def norm_one_back(n_shard, idx, x_in, mine, got, grad, gains, out, gain_grad):
    r = gain_grad.shape[2]
    x = x_in[idx[2]].astype(wide)
    one = mine[...].astype(wide) + got[...].astype(wide)
    scale = lax.rsqrt(jnp.mean(x * x, axis=-1, keepdims=True) + norm_eps)
    u = one * gains[0:1, :]
    inner = jnp.mean(u * x, axis=-1, keepdims=True) * (scale * scale * scale)
    out[...] = (grad[...] + scale * u - x * inner).astype(low)
    total = jnp.sum(one * x * scale, axis=0, keepdims=True)
    for j in range(n_shard):
        gain_grad[j] = total[:, r * j : r * (j + 1)]


def produce(n_parts, *refs):
    parts, (middle, out) = refs[:n_parts], refs[n_parts:]
    out[...] = (middle[...] + sum((p[...].astype(wide) for p in parts))).astype(low)


def finish_wide(n_ctx, widths, which, idx, *refs):
    count = sum((n for _, n in which))
    sources, refs = refs[:count], refs[count:]
    outs, (stage, held, sems) = refs[-6:-3], refs[-3:]
    r = outs[0].shape[0]
    columns = sum(widths)
    parts, rows = wide_tiles(r, widths)
    span = held.shape[2]
    for v in range(n_ctx):
        start = min(((v ^ k) * columns for k, _ in which))

        @pl.when(idx[1] == v)
        def _(v=v, start=start):
            first = 0
            for k, pieces in which:
                size_each = rows // pieces
                for i, n in enumerate(widths):
                    for row, size, top, lane, lanes, at in parts[i]:
                        done = 0
                        while done < size:
                            part, here = divmod(row + done, size_each)
                            many = min(size - done, size_each - here)
                            stage[top + done : top + done + many, lane : lane + lanes] = sources[
                                first + part
                            ][here : here + many, at : at + lanes].astype(wide)
                            done += many
                    at = (v ^ k) * columns + sum(widths[:i]) - start
                    for j in range(3):
                        held[j, :, at : at + n] = stage[:, j * n : (j + 1) * n]
                first += pieces
            copies = [
                pltpu.make_async_copy(
                    held.at[j], outs[j].at[:, start : start + span], sems.at[j]
                )
                for j in range(3)
            ]
            for copy in copies:
                copy.start()
            for copy in copies:
                copy.wait()


def finish_attention(n_ctx, idx, *refs):
    pieces, (outs, gains) = refs[:n_ctx], (refs[n_ctx:-1], refs[-1])
    inner, r = outs[0].shape
    for v in range(n_ctx):

        @pl.when(idx[1] == v)
        def _(v=v):
            for k in range(n_ctx):
                outs[v ^ k][...] = pieces[k][0:inner, 0:r].astype(wide)

    gains[...] = sum((p[inner : inner + 2, 0:r].astype(wide) for p in pieces))


def on_device(
    inputs,
    cotangent,
    norm1_gain,
    w_query,
    w_key,
    w_value,
    w_out,
    norm2_gain,
    w_gate,
    w_up,
    w_down,
    bias_table,
):
    _, rows, width = inputs.shape
    shards, ctx = lax.axis_size("shard"), lax.axis_size("ctx")
    inner, r = w_out.shape
    heads = inner // DK
    length = ctx * rows
    columns = w_gate.shape[1] // ctx
    first_width = pl.cdiv(columns, 2 * LANES) * LANES
    widths = (first_width, columns - first_width)
    lanes_r = pl.cdiv(r, LANES) * LANES
    s, c, half = lax.axis_index("shard"), lax.axis_index("ctx"), lax.axis_index("tensor")
    idx = jnp.stack([s, c, half]).astype(jnp.int32)
    attention_weights = (w_query.T, w_key.T, w_value.T, w_out)


    wide_rows = wide_tiles(r, widths)[1]
    window = min(pl.cdiv(columns, LANES) * LANES, w_gate.shape[1])
    (packed,) = run(
        functools.partial(pack_wide, ctx, widths, window),
        "pack_wide",
        [((wide_rows, LANES), low)],
        [idx, w_gate, w_up, w_down.T],
        scratch=[
            pltpu.VMEM((r, 3 * max(widths)), low),
            pltpu.VMEM((3, r, window), low),
            pltpu.SemaphoreType.DMA((3,)),
        ],
        cost=2,
        far=3,
        vmem=60,
    )
    chunks = lax.all_gather(packed, "shard", axis=0, tiled=False)
    own_x = lax.dynamic_index_in_dim(inputs, half, 0, keepdims=False)
    (own_buf,) = run(
        functools.partial(pack_attention, ctx),
        "pack_attention",
        [((inner + 16, lanes_r), low)],
        [after(idx, packed), *attention_weights, jnp.stack([norm1_gain, norm2_gain])],
        scratch=[pltpu.VMEM((inner, r), low), pltpu.SemaphoreType.DMA],
        far=4,
        vmem=60,
    )
    from_shard = [step(own_buf, "shard", k) for k in range(1, shards)]
    mine_x = [swap(own_x, "ctx", k) for k in range(1, ctx)]
    table = lax.dynamic_slice_in_dim(bias_table, half * heads, heads, 1)
    (bias,) = run(
        functools.partial(bias_body, rows, rows // 5, distance_marks),
        "bias",
        [((heads, length, length), wide)],
        [after(idx, own_buf), table],
        scalars=2,
        cost=5,
    )
    now = after(idx, *from_shard, *mine_x, bias)

    group = jnp.concatenate(from_shard)
    buf_rows = inner + 16
    place = {z: [(0, (z - 1) * buf_rows, inner)] for z in range(1, shards)}
    gathered = [group] + [swap(after(group, now), "ctx", k) for k in range(1, ctx)]
    rest_x = swap(after(jnp.stack(mine_x), now), "tensor")
    normed_one, gains = run(
        functools.partial(norm_one, ctx, shards),
        "norm_one",
        [((2 * length, width), low), ((2, width), wide)],
        [now, inputs, *mine_x, rest_x, own_buf, *from_shard],
        scratch=[pltpu.VMEM((shards, 8, r), wide)],
        cost=3,
    )
    now = after(now, *gathered[1:], normed_one)

    own_cot = lax.dynamic_index_in_dim(cotangent, half, 0, keepdims=False)
    mine_cot = [swap(after(own_cot, now), "ctx", k) for k in range(1, ctx)]
    att_mine, att_other, soft, qkv, mixed, every = run(
        functools.partial(attend, ctx, shards, rows, heads, place),
        "attend",
        [
            ((length, width), low),
            ((length, width), low),
            ((2, heads, rows, length), wide),
            ((2 * length, 3 * inner), low),
            ((2 * length, inner), low),
            ((4 * inner, width), low),
        ],
        [now, normed_one, *attention_weights, bias, *gathered],
        scratch=[pltpu.VMEM((shards, 4 * inner, r), low)],
        cost=14,
        vmem=24,
    )
    now = after(now, *mine_cot, att_other)

    att_got = swap(after(att_other, now), "tensor")
    rest_cot = swap(after(jnp.stack(mine_cot), now), "tensor")
    nt_mine, middle_own = run(
        functools.partial(middle_norm, ctx),
        "middle_norm",
        [((length, width), low), ((rows, width), wide)],
        [now, inputs, *mine_x, att_mine, att_got, gains],
    )
    nt_other = swap(nt_mine, "tensor")
    now = after(now, nt_other, rest_cot)

    def add(a, b):
        return (a.astype(wide) + b.astype(wide)).astype(low)

    tokens_out = ((ctx, rows, width), low)
    wide_grads, feed_mine, feed_other, two_mine, two_other = run(
        functools.partial(feed_forward, ctx, shards, widths),
        "feed_forward",
        [((shards, wide_rows, LANES), low)] + [tokens_out] * 4,
        [now, chunks, nt_mine, nt_other, cotangent, *mine_cot, rest_cot],
        scratch=[
            pltpu.VMEM((shards, wide_rows, LANES), low),
            pltpu.VMEM((2 * length, width), low),
            pltpu.VMEM((2 * length, width), low),
            pltpu.VMEM((2, ctx, rows, width), low),
            pltpu.VMEM((2, ctx, rows, width), low),
            pltpu.SemaphoreType.DMA((3 + shards + 2 * ctx,)),
            pltpu.SemaphoreType.DMA((4 + shards * len(widths),)),
        ]
        + [pltpu.VMEM((width, 3 * n), low) for n in widths]
        + [pltpu.VMEM((2 * length, n), low) for n in widths]
        + [pltpu.VMEM((2 * length, 2 * n), low) for n in widths],
        far=5 + ctx - 1,
        far_out=True,
        cost=20,
        vmem=60,
    )
    wide_own = lax.psum_scatter(wide_grads, "shard", scatter_dimension=0, tiled=False)
    now = after(now, two_other)

    two_got = swap(after(two_other, now), "tensor")
    two_both = [add(two_mine[k], two_got[k]) for k in range(ctx)]
    two_parts = [two_both[0]] + [swap(two_both[k], "ctx", k) for k in range(1, ctx)]
    out_in, middle_grad, gain_two = run(
        functools.partial(norm_two_back, shards, ctx),
        "norm_two_back",
        [((rows, width), low), ((rows, width), wide), ((shards, 1, r), wide)],
        [now, cotangent, *two_parts, middle_own, gains],
    )
    out_in_other = swap(out_in, "tensor")
    now = after(now, out_in_other)

    feed_got = swap(after(feed_other, now), "tensor")
    got = run(
        functools.partial(attend_back, ctx, heads),
        "attend_back",
        [((2 * rows, 2 * inner), low)] * ctx + [((2 * rows, inner), low)],
        [out_in, out_in_other, soft, qkv, every],
        scalars=0,
        scratch=[pltpu.VMEM((2 * length, 2 * inner), low), pltpu.VMEM((2 * rows, inner), low)],
        cost=4,
        vmem=24,
    )
    kv_parts, q_grad = got[:ctx], got[ctx]
    now = after(now, feed_got, q_grad)

    kv_parts = [kv_parts[0]] + [swap(after(kv_parts[k], now), "ctx", k) for k in range(1, ctx)]
    outs_mine = [out_in] + [
        lax.ppermute(after(out_in, now), "ctx", [((ctx - 1) ^ k, ctx - 1)]) for k in range(1, ctx)
    ]
    feed_both = [add(feed_mine[k], feed_got[k]) for k in range(ctx)]
    got = run(
        functools.partial(first_grad, ctx),
        "first_grad",
        [((rows, width), low)] * 2 + [((2 * rows, inner), low)] * ctx,
        [now, *kv_parts, q_grad, every],
        scratch=[pltpu.VMEM((2 * rows, 3 * inner), low)],
    )
    first_mine, first_other, pieces = got[0], got[1], got[2:]
    now = after(now, first_other, *feed_both)

    pieces = [pieces[0]] + [swap(after(pieces[k], now), "ctx", k) for k in range(1, ctx)]
    first_got = swap(after(first_other, now), "tensor")
    input_mine, gain_one = run(
        functools.partial(norm_one_back, shards),
        "norm_one_back",
        [((rows, width), low), ((shards, 1, r), wide)],
        [now, inputs, first_mine, first_got, middle_grad, gains],
    )
    outs_rest = [out_in_other, swap(jnp.stack(outs_mine[1:]), "tensor")]
    now = after(now, *pieces[1:], input_mine, outs_rest[1])

    feed_parts = [feed_both[0]] + [swap(after(feed_both[k], now), "ctx", k) for k in range(1, ctx)]
    input_other = swap(after(input_mine, now), "tensor")
    (four,) = run(
        functools.partial(weight_grads, ctx, shards),
        "weight_grads",
        [((shards, inner + 16, r), low)],
        [now, normed_one, mixed, *pieces, *outs_mine, *outs_rest, gain_one, gain_two],
        scratch=[
            pltpu.VMEM((2 * length, inner), low),
            pltpu.VMEM((2 * length, width), low),
            pltpu.VMEM((ctx, 2 * rows, inner), low),
            pltpu.SemaphoreType.DMA((2 * ctx + 1,)),
        ],
        far=4 + 2 * ctx,
        cost=2,
        vmem=60,
    )
    (produced_mine,) = run(
        functools.partial(produce, ctx),
        "produce",
        [((rows, width), low)],
        [*feed_parts, middle_own],
        scalars=0,
    )
    now = after(now, produced_mine, four, input_other)

    four_shard = [four[0]] + [step(after(four[d], now), "shard", d) for d in range(1, shards)]
    produced_other = swap(after(produced_mine, now), "tensor")
    out_y, out_x = run(
        place_outputs,
        "place_outputs",
        [(inputs.shape, low)] * 2,
        [now, produced_mine, produced_other, input_mine, input_other],
    )
    now = after(now, wide_own, out_y)

    wide_own = after(wide_own, now)
    half_rows = wide_rows // 2
    pair = ctx == 4
    wide_all = [swap(wide_own, "ctx", k) for k in ((1, 2) if pair else range(1, ctx))]
    four_own = sum((part.astype(wide) for part in four_shard)).astype(low)
    four_all = [four_own] + [swap(after(four_own, now), "ctx", k) for k in range(1, ctx)]
    now = after(now, *wide_all, *four_all[1:])

    far_halves = []
    if pair:
        far_halves = [
            swap(after(wide_all[0], now)[:half_rows], "ctx", 2),
            swap(after(wide_all[1], now)[half_rows:], "ctx", 1),
        ]
    out_q, out_k, out_v, out_o, own_gain = run(
        functools.partial(finish_attention, ctx),
        "finish_attention",
        [((inner, r), wide)] * 4 + [((2, r), wide)],
        [now, *four_all],
    )
    own_gain = own_gain + swap(own_gain, "tensor")

    def finish(now, which, sources, span, before):
        return run(
            functools.partial(finish_wide, ctx, widths, which),
            "finish_wide",
            [(w_gate.shape, wide)] * 3,
            [now, *sources, *before],
            scratch=[
                pltpu.VMEM((r, 3 * max(widths)), wide),
                pltpu.VMEM((3, r, span), wide),
                pltpu.SemaphoreType.DMA((3,)),
            ],
            far_out=True,
            into=len(before),
            cost=3,
            vmem=24,
        )

    if pair and 2 * columns % LANES == 0:
        outs = finish(now, [(0, 1), (1, 1)], [wide_own, wide_all[0]], 2 * columns, [])
        now = after(now, *far_halves, outs[0], own_gain)
        outs = finish(now, [(2, 1), (3, 2)], [wide_all[1], *far_halves], 2 * columns, outs)
    else:
        which = [(k, 1) for k in range(ctx)]
        outs = finish(now, which, [wide_own, *wide_all], ctx * columns, [])
    out_g, out_u, out_d = outs

    return (
        out_y,
        out_x,
        own_gain[0],
        out_q.T,
        out_k.T,
        out_v.T,
        out_o,
        own_gain[1],
        out_g,
        out_u,
        out_d.T,
    )


def solution(mesh):
    placed = (
        P(None, ("shard", "ctx"), None),
        P(None, ("shard", "ctx"), None),
        P("shard"),
        P("shard", "tensor"),
        P("shard", "tensor"),
        P("shard", "tensor"),
        P("tensor", "shard"),
        P("shard"),
        P("shard", "tensor"),
        P("shard", "tensor"),
        P("tensor", "shard"),
        P(),
    )
    return jax.shard_map(
        on_device, mesh=mesh, in_specs=placed, out_specs=placed[:2] + placed[2:11], check_vma=False
    )
```

```python
import functools

import jax
import jax.numpy as jnp
from jax import lax
from jax.experimental import pallas as pl
from jax.experimental.pallas import tpu as pltpu
from jax.sharding import PartitionSpec as P

DK = 64
norm_eps = 1e-06
distance_marks = (8, 12, 16, 23, 32, 46, 64, 91)
masked_score = -1e30
low = jnp.bfloat16
wide = jnp.float32
LANES = 128
COST = 1e8


def dot_nn(left, right):
    return lax.dot_general(left, right, (((1,), (0,)), ((), ())), preferred_element_type=wide)


def dot_nt(left, right):
    return lax.dot_general(left, right, (((1,), (1,)), ((), ())), preferred_element_type=wide)


def dot_tn(left, right):
    return lax.dot_general(left, right, (((0,), (0,)), ((), ())), preferred_element_type=wide)


def wrap(value, n):
    return lax.rem(value + 2 * n, n)


def run(body, name, outs, operands, scratch=(), scalars=1, cost=1, far=0, far_out=False, into=0, vmem=16):
    return pl.pallas_call(
        body,
        name=name,
        out_shape=[jax.ShapeDtypeStruct(s, d) for s, d in outs],
        in_specs=[pl.BlockSpec(memory_space=pltpu.SMEM)] * scalars
        + [pl.BlockSpec(memory_space=pltpu.HBM)] * far
        + [pl.BlockSpec(memory_space=pltpu.VMEM)] * (len(operands) - scalars - far - into)
        + [pl.BlockSpec(memory_space=pltpu.HBM)] * into,
        out_specs=[pl.BlockSpec(memory_space=pltpu.HBM if far_out else pltpu.VMEM)] * len(outs),
        scratch_shapes=list(scratch),
        input_output_aliases={len(operands) - into + i: i for i in range(into)},
        compiler_params=pltpu.CompilerParams(vmem_limit_bytes=vmem * 2**20),
        cost_estimate=pl.CostEstimate(flops=int(cost * COST), bytes_accessed=0, transcendentals=0),
    )(*operands)


def step(x, axis, k=1):
    n = lax.axis_size(axis)
    return lax.ppermute(x, axis, [(i, (i + k) % n) for i in range(n)])


def swap(x, axis, k=1):
    n = lax.axis_size(axis)
    return lax.ppermute(x, axis, [(i, i ^ k) for i in range(n)])


def after(x, *others):
    return lax.optimization_barrier((x, *others))[0]


def pack_attention(n_ctx, idx, w_q, w_k, w_v, w_o, gain, buf, held, sem):
    inner, r = w_o.shape
    for v, ref in enumerate((w_q, w_k, w_v, w_o)):

        @pl.when(idx[1] == v)
        def _(ref=ref):
            copy = pltpu.make_async_copy(ref, held, sem)
            copy.start()
            copy.wait()

    buf[0:inner, 0:r] = held[...]

    buf[inner : inner + 2, 0:r] = gain[...]


def wide_tiles(r, widths):
    rp = pl.cdiv(r, 16) * 16
    row, parts = 0, []
    for n in widths:
        full, left = divmod(3 * n, LANES)
        pieces = [(row + rp * q, r, 0, LANES * q, LANES, 0) for q in range(full)]
        row += rp * full
        if left:
            assert 2 * left == LANES
            pieces.append((row, r // 2, 0, LANES * full, left, 0))
            pieces.append((row, r // 2, r // 2, LANES * full, left, left))
            row += pl.cdiv(r // 2, 8) * 8
        parts.append(pieces)
    return parts, pl.cdiv(row, 32) * 32


def pack_wide(n_ctx, widths, window, idx, w_g, w_u, w_d, buf, stage, held, sems):
    r = w_g.shape[0]
    columns = sum(widths)
    parts, _ = wide_tiles(r, widths)
    for v in range(n_ctx):

        @pl.when(idx[1] == v)
        def _(v=v):
            start = min(v * columns // LANES * LANES, w_g.shape[1] - window)
            copies = [
                pltpu.make_async_copy(ref.at[:, start : start + window], held.at[i], sems.at[i])
                for i, ref in enumerate((w_g, w_u, w_d))
            ]
            for copy in copies:
                copy.start()
            for copy in copies:
                copy.wait()
            at = v * columns - start
            for n, pieces in zip(widths, parts, strict=True):
                for i in range(3):
                    stage[:, i * n : (i + 1) * n] = held[i, :, at : at + n]
                for row, size, top, lane, lanes, to in pieces:
                    buf[row : row + size, to : to + lanes] = stage[
                        top : top + size, lane : lane + lanes
                    ]
                at += n


def bias_body(rows, seg_len, marks, idx, table, out):
    c = idx[1]
    heads, length, _ = out.shape

    def info(position):
        block = sum(((position >= rows * b).astype(jnp.int32) for b in range(1, length // rows)))
        token = (block ^ c) * rows + position - block * rows
        seg = sum(((token >= q * seg_len).astype(jnp.int32) for q in range(8, 20)))
        parent = jnp.where(seg == 0, -1, jnp.where(seg <= 4, 0, (seg - 3) >> 1))
        shift = jnp.where(seg == 0, 0, jnp.where(seg <= 4, seg - 1, seg - 2))
        return seg, parent, token - shift * seg_len

    key_seg, _, key_place = info(lax.broadcasted_iota(jnp.int32, (16, length), 1))

    def rows_of(i, _):
        at = pl.multiple_of(i * 16, 16)
        seg, parent, place = info(lax.broadcasted_iota(jnp.int32, (16, length), 0) + at)
        allowed = (key_seg == 0) | (key_seg == seg) | (key_seg == parent)
        relative = key_place - place
        magnitude = jnp.abs(relative)
        marked = sum(((magnitude >= mark).astype(jnp.int32) for mark in marks))
        bucket = jnp.where(relative > 0, 16, 0) + jnp.where(magnitude < 8, magnitude, 7 + marked)
        looked = [jnp.full(bucket.shape, table[0, h], wide) for h in range(heads)]
        for b in range(1, table.shape[0]):
            hit = bucket == b
            looked = [jnp.where(hit, table[b, h], looked[h]) for h in range(heads)]
        for h in range(heads):
            out[h, pl.ds(at, 16), :] = jnp.where(allowed, looked[h], masked_score)
        return 0

    lax.fori_loop(0, length // 16, rows_of, 0)


def tree_blocks(n_ctx, half, own, mine, rest):
    for k in range(n_ctx):
        yield 0, k, own[half] if k == 0 else mine[k - 1][...]
    for k in range(n_ctx):
        yield 1, k, own[1 - half] if k == 0 else rest[k - 1]


def norm_one(n_ctx, n_shard, idx, x_in, *refs):
    s, half = idx[0], idx[2]
    mine, rest = refs[: n_ctx - 1], refs[n_ctx - 1]
    bufs = refs[n_ctx : n_ctx + n_shard]
    normed, gains, held = refs[n_ctx + n_shard :]
    r = held.shape[2]
    _, rows, width = x_in.shape
    for k, buf in enumerate(bufs):
        at = buf.shape[0] - 16
        held[wrap(s - k, n_shard), 0:2, :] = buf[at : at + 2, 0:r].astype(wide)
    for j in range(n_shard):
        gains[:, r * j : r * (j + 1)] = held[j, 0:2, :]
    for m, k, x in tree_blocks(n_ctx, half, x_in, mine, rest):
        x = x.astype(wide)
        y = x * lax.rsqrt(jnp.mean(x * x, axis=-1, keepdims=True) + norm_eps)
        at = (m * n_ctx + k) * rows
        normed[at : at + rows, :] = (y * gains[0:1, :]).astype(low)


def attend(n_ctx, n_shard, rows, heads, place, idx, normed, w_q, w_k, w_v, w_o, bias, *refs):
    s, c = idx[0], idx[1]
    groups = 1 + max((g for pieces in place.values() for g, _, _ in pieces))
    got = [refs[g * n_ctx : (g + 1) * n_ctx] for g in range(groups)]
    att_mine, att_other, soft, qkv, mixed, every, held = refs[groups * n_ctx :]
    inner, r = w_o.shape
    length = n_ctx * rows
    for i, ref in enumerate((w_q, w_k, w_v, w_o)):
        held[s, i * inner : (i + 1) * inner, :] = ref[...]
    for v in range(n_ctx):

        @pl.when(c == v)
        def _(v=v):
            for k in range(n_ctx):
                for z, pieces in place.items():
                    at, last = (v ^ k) * inner, ((v ^ k) + 1) * inner
                    for g, row, size in pieces:
                        size = min(size, last - at)
                        held[wrap(s - z, n_shard), at : at + size, :] = got[g][k][
                            row : row + size, 0:r
                        ]
                        at += size

    for j in range(n_shard):
        every[:, r * j : r * (j + 1)] = held[j]
    qkv[...] = dot_nt(normed[...], every[0 : 3 * inner, :]).astype(low)
    for m in (1, 0):
        low_row = m * length
        for h in range(heads):
            at = DK * h
            keys = qkv[low_row : low_row + length, inner + at : inner + at + DK]
            values = qkv[low_row : low_row + length, 2 * inner + at : 2 * inner + at + DK]
            for b in range(n_ctx):
                top = low_row + b * rows
                scores = dot_nt(qkv[top : top + rows, at : at + DK], keys)
                scores += bias[h, b * rows : (b + 1) * rows, :]
                raised = jnp.exp(scores - jnp.max(scores, axis=-1, keepdims=True))
                share = raised / jnp.sum(raised, axis=-1, keepdims=True)
                if b == 0:
                    soft[m, h] = share
                mixed[top : top + rows, at : at + DK] = dot_nn(share.astype(low), values).astype(low)
        out = att_mine if m == 0 else att_other
        out[...] = dot_nn(
            mixed[low_row : low_row + length, :], every[3 * inner : 4 * inner, :]
        ).astype(low)


def middle_norm(n_ctx, idx, x_in, *refs):
    mine, (att, got, gains, normed, middle_own) = refs[: n_ctx - 1], refs[n_ctx - 1 :]
    rows = x_in.shape[1]
    for k in range(n_ctx):
        at = slice(k * rows, (k + 1) * rows)
        x = x_in[idx[2]] if k == 0 else mine[k - 1][...]
        mid = x.astype(wide) + (att[at, :].astype(wide) + got[at, :].astype(wide))
        scale = lax.rsqrt(jnp.mean(mid * mid, axis=-1, keepdims=True) + norm_eps)
        normed[at, :] = (mid * scale * gains[1:2, :]).astype(low)
        if k == 0:
            middle_own[...] = mid


def feed_forward(n_ctx, n_shard, widths, idx, buf_far, nt_mine, nt_other, cot_in, *refs):
    half = idx[2]
    mine, rest, refs = refs[: n_ctx - 1], refs[n_ctx - 1], refs[n_ctx:]
    sent, feed, two = refs[0], refs[1:3], refs[3:5]
    n_parts = len(widths)
    buf, nt, cot, feed_held, two_held, sems, sems_out = refs[5:12]
    weights, hidden, pair = (refs[12 + i * n_parts : 12 + (i + 1) * n_parts] for i in range(3))
    length, _ = nt_mine.shape
    rows = length // n_ctx
    r = weights[0].shape[0] // n_shard

    def blocks(m, first, count=1):
        at = (m * n_ctx + first) * rows
        return slice(at, at + count * rows)

    begun = [pltpu.make_async_copy(buf_far.at[0], buf.at[0], sems.at[0])]
    moves = [
        (nt_mine, nt.at[0:length, :]),
        (nt_other, nt.at[length : 2 * length, :]),
        (cot_in.at[half], cot.at[blocks(0, 0), :]),
        (cot_in.at[1 - half], cot.at[blocks(1, 0), :]),
    ]
    moves += [(buf_far.at[j], buf.at[j]) for j in range(1, n_shard)]
    for k in range(1, n_ctx):
        moves.append((mine[k - 1], cot.at[blocks(0, k), :]))
        moves.append((rest.at[k - 1], cot.at[blocks(1, k), :]))
    begun += [pltpu.make_async_copy(a, b, sems.at[i + 1]) for i, (a, b) in enumerate(moves)]
    for copy in begun:
        copy.start()
    loads = [begun[0]] + begun[5 : 4 + n_shard]
    parts, _ = wide_tiles(r, widths)
    for j in range(n_shard):
        loads[j].wait()
        for e, pieces in enumerate(parts):
            for row, size, top, lane, lanes, at in pieces:
                weights[e][r * j + top : r * j + top + size, lane : lane + lanes] = buf[
                    j, row : row + size, at : at + lanes
                ]
    for copy in begun[1:5] + begun[4 + n_shard :]:
        copy.wait()
    c0, c1 = 0.7978845608028654, 0.044715
    out = []

    def write(source, target):
        copy = pltpu.make_async_copy(source, target, sems_out.at[len(out)])
        copy.start()
        out.append(copy)

    for m in (1, 0):
        at = slice(m * length, (m + 1) * length)
        for e, n in enumerate(widths):
            both = dot_nn(nt[at, :], weights[e][:, 0 : 2 * n])
            back = dot_nn(cot[at, :], weights[e][:, 2 * n : 3 * n])
            gate, up = both[:, :n], both[:, n:]
            square = gate * gate
            bent = jnp.tanh(c0 * (gate + c1 * gate * square))
            half_one = 0.5 * (1.0 + bent)
            active = gate * half_one
            slope = half_one + 0.5 * gate * (1.0 - bent * bent) * (c0 * (1.0 + 3.0 * c1 * square))
            hidden[e][at, :] = (active * up).astype(low)
            pair[e][at, 0:n] = (back * up * slope).astype(low)
            pair[e][at, n : 2 * n] = (back * active).astype(low)
        for held, given, make in (
            (two_held, two, lambda e, n: dot_nt(pair[e][at, :], weights[e][:, 0 : 2 * n])),
            (feed_held, feed, lambda e, n: dot_nt(hidden[e][at, :], weights[e][:, 2 * n : 3 * n])),
        ):
            total = sum((make(e, n) for e, n in enumerate(widths)))
            for i in range(n_ctx):
                held[m, i] = total[i * rows : (i + 1) * rows].astype(low)
            write(held.at[m], given[m])
    for e, n in enumerate(widths):
        for_in = dot_tn(nt[...], pair[e][...]).astype(low)
        for_down = dot_tn(cot[...], hidden[e][...]).astype(low)
        first, last = parts[e][0][0], parts[e][-1][0] + parts[e][-1][1]
        for j in range(n_shard):
            for row, size, top, lane, lanes, at in parts[e]:
                top = r * j + top
                inside = max(0, min(lanes, 2 * n - lane))
                if inside:
                    buf[j, row : row + size, at : at + inside] = for_in[
                        top : top + size, lane : lane + inside
                    ]
                if inside < lanes:
                    begin = lane + inside - 2 * n
                    buf[j, row : row + size, at + inside : at + lanes] = for_down[
                        top : top + size, begin : begin + lanes - inside
                    ]
            here = slice(first, last if e < n_parts - 1 else buf.shape[1])
            write(buf.at[j, here, :], sent.at[j, here, :])
    for copy in out:
        copy.wait()


def norm_two_back(n_shard, n_parts, idx, cot_in, *refs):
    parts, refs = refs[:n_parts], refs[n_parts:]
    middle, gains, out_in, grad, gain_grad = refs
    r = gain_grad.shape[2]
    mid = middle[...]
    two = sum((p[...].astype(wide) for p in parts))
    scale = lax.rsqrt(jnp.mean(mid * mid, axis=-1, keepdims=True) + norm_eps)
    u = two * gains[1:2, :]
    inner = jnp.mean(u * mid, axis=-1, keepdims=True) * (scale * scale * scale)
    back = cot_in[idx[2]].astype(wide) + scale * u - mid * inner
    grad[...] = back
    out_in[...] = back.astype(low)
    total = jnp.sum(two * mid * scale, axis=0, keepdims=True)
    for j in range(n_shard):
        gain_grad[j] = total[:, r * j : r * (j + 1)]


def attend_back(n_ctx, heads, idx, o_mine, o_other, soft, qkv, every, mixed, *refs):
    kv, for_out, (q_grad, kv_all, mixed_grad) = refs[:n_ctx], refs[n_ctx : 2 * n_ctx], refs[2 * n_ctx :]
    rows = o_mine.shape[0]
    length = n_ctx * rows
    inner = heads * DK
    share_rows = for_out[0].shape[0]
    for m, o_in in ((0, o_mine), (1, o_other)):
        top, own = m * length, m * rows
        mixed_grad[own : own + rows, :] = dot_nt(o_in[...], every[3 * inner :, :]).astype(low)
        for h in range(heads):
            at = DK * h
            share = soft[m, h]
            grad = mixed_grad[own : own + rows, at : at + DK]
            keys = qkv[top : top + length, inner + at : inner + at + DK]
            values = qkv[top : top + length, 2 * inner + at : 2 * inner + at + DK]
            queries = qkv[top : top + rows, at : at + DK]
            weight = dot_nt(grad, values)
            ds = share * (weight - jnp.sum(weight * share, axis=-1, keepdims=True))
            ds = ds.astype(low)
            q_grad[own : own + rows, at : at + DK] = dot_nn(ds, keys).astype(low)
            kv_all[top : top + length, at : at + DK] = dot_tn(ds, queries).astype(low)
            kv_all[top : top + length, inner + at : inner + at + DK] = dot_tn(
                share.astype(low), grad
            ).astype(low)
        for k in range(n_ctx):
            kv[k][own : own + rows, :] = kv_all[top + k * rows : top + (k + 1) * rows, :]
    got = dot_tn(mixed[0:rows, :], o_mine[...])
    got += dot_tn(mixed[length : length + rows, :], o_other[...])
    got = got.astype(low)
    for v in range(n_ctx):

        @pl.when(idx[1] == v)
        def _(v=v):
            for k in range(n_ctx):
                for_out[k][...] = got[(v ^ k) * share_rows : ((v ^ k) + 1) * share_rows, :]


def first_grad(n_ctx, idx, *refs):
    parts, (q_grad, every, out_mine, out_other), pieces, three = (
        refs[:n_ctx],
        refs[n_ctx : n_ctx + 4],
        refs[n_ctx + 4 : 2 * n_ctx + 4],
        refs[2 * n_ctx + 4],
    )
    rows2, inner = q_grad.shape
    rows = rows2 // 2
    size = inner // n_ctx
    three[:, 0:inner] = q_grad[...]
    three[:, inner:] = sum((p[...].astype(wide) for p in parts)).astype(low)
    for v in range(n_ctx):

        @pl.when(idx[1] == v)
        def _(v=v):
            for k in range(n_ctx):
                for i in range(3):
                    at = i * inner + (v ^ k) * size
                    pieces[k][:, i * size : (i + 1) * size] = three[:, at : at + size]

    got = dot_nn(three[...], every[0 : 3 * inner, :]).astype(low)
    out_mine[...] = got[0:rows]
    out_other[...] = got[rows:]


def weight_grads(n_ctx, n_shard, idx, normed, *refs):
    pieces, for_out, refs = refs[:n_ctx], refs[n_ctx : 2 * n_ctx], refs[2 * n_ctx :]
    gain_one, gain_two, stack, grads, held, sem = refs
    s = idx[0]
    copy = pltpu.make_async_copy(normed, held, sem)
    copy.start()
    size, r = for_out[0].shape[0], stack.shape[2]
    rows = pieces[0].shape[0] // 2
    out_rows = sum((p[...].astype(wide) for p in for_out))
    for j in range(n_shard):
        d = wrap(j - s, n_shard)
        stack[d, 3 * size : 4 * size, :] = out_rows[:, r * j : r * (j + 1)].astype(low)
        stack[d, 4 * size : 4 * size + 1, :] = gain_one[j].astype(low)
        stack[d, 4 * size + 1 : 4 * size + 2, :] = gain_two[j].astype(low)
    for m in range(2):
        for k in range(n_ctx):
            at = (m * n_ctx + k) * rows
            grads[at : at + rows, :] = pieces[k][m * rows : (m + 1) * rows, :]
    copy.wait()
    got = dot_tn(grads[...], held[...])
    for j in range(n_shard):
        stack[wrap(j - s, n_shard), 0 : 3 * size, :] = got[:, r * j : r * (j + 1)].astype(low)


def place_outputs(idx, a_mine, a_other, b_mine, b_other, a, b):
    half = idx[2]
    a[half] = a_mine[...]
    a[1 - half] = a_other[...]
    b[half] = b_mine[...]
    b[1 - half] = b_other[...]


def norm_one_back(n_shard, idx, x_in, mine, got, grad, gains, out, gain_grad):
    r = gain_grad.shape[2]
    x = x_in[idx[2]].astype(wide)
    one = mine[...].astype(wide) + got[...].astype(wide)
    scale = lax.rsqrt(jnp.mean(x * x, axis=-1, keepdims=True) + norm_eps)
    u = one * gains[0:1, :]
    inner = jnp.mean(u * x, axis=-1, keepdims=True) * (scale * scale * scale)
    out[...] = (grad[...] + scale * u - x * inner).astype(low)
    total = jnp.sum(one * x * scale, axis=0, keepdims=True)
    for j in range(n_shard):
        gain_grad[j] = total[:, r * j : r * (j + 1)]


def produce(n_parts, *refs):
    parts, (middle, out) = refs[:n_parts], refs[n_parts:]
    out[...] = (middle[...] + sum((p[...].astype(wide) for p in parts))).astype(low)


def finish_wide(n_ctx, widths, which, idx, *refs):
    count = sum((n for _, n in which))
    sources, refs = refs[:count], refs[count:]
    outs, (stage, held, sems) = refs[-6:-3], refs[-3:]
    r = outs[0].shape[0]
    columns = sum(widths)
    parts, rows = wide_tiles(r, widths)
    span = held.shape[2]
    for v in range(n_ctx):
        start = min(((v ^ k) * columns for k, _ in which))

        @pl.when(idx[1] == v)
        def _(v=v, start=start):
            first = 0
            for k, pieces in which:
                size_each = rows // pieces
                for i, n in enumerate(widths):
                    for row, size, top, lane, lanes, at in parts[i]:
                        done = 0
                        while done < size:
                            part, here = divmod(row + done, size_each)
                            many = min(size - done, size_each - here)
                            stage[top + done : top + done + many, lane : lane + lanes] = sources[
                                first + part
                            ][here : here + many, at : at + lanes].astype(wide)
                            done += many
                    at = (v ^ k) * columns + sum(widths[:i]) - start
                    for j in range(3):
                        held[j, :, at : at + n] = stage[:, j * n : (j + 1) * n]
                first += pieces
            copies = [
                pltpu.make_async_copy(
                    held.at[j], outs[j].at[:, start : start + span], sems.at[j]
                )
                for j in range(3)
            ]
            for copy in copies:
                copy.start()
            for copy in copies:
                copy.wait()


def finish_attention(n_ctx, idx, *refs):
    pieces, (outs, gains) = refs[:n_ctx], (refs[n_ctx:-1], refs[-1])
    inner, _ = outs[0].shape
    size = inner // n_ctx
    for v in range(n_ctx):

        @pl.when(idx[1] == v)
        def _(v=v):
            for k in range(n_ctx):
                at = (v ^ k) * size
                for i in range(4):
                    outs[i][at : at + size, :] = pieces[k][i * size : (i + 1) * size, :].astype(wide)

    gains[...] = sum((p[inner : inner + 2, :].astype(wide) for p in pieces))


def on_device(
    inputs,
    cotangent,
    norm1_gain,
    w_query,
    w_key,
    w_value,
    w_out,
    norm2_gain,
    w_gate,
    w_up,
    w_down,
    bias_table,
):
    _, rows, width = inputs.shape
    shards, ctx = lax.axis_size("shard"), lax.axis_size("ctx")
    inner, r = w_out.shape
    heads = inner // DK
    length = ctx * rows
    columns = w_gate.shape[1] // ctx
    first_width = pl.cdiv(columns, 2 * LANES) * LANES
    widths = (first_width, columns - first_width)
    lanes_r = pl.cdiv(r, LANES) * LANES
    s, c, half = lax.axis_index("shard"), lax.axis_index("ctx"), lax.axis_index("tensor")
    idx = jnp.stack([s, c, half]).astype(jnp.int32)
    attention_weights = (w_query.T, w_key.T, w_value.T, w_out)


    wide_rows = wide_tiles(r, widths)[1]
    window = min(pl.cdiv(columns, LANES) * LANES, w_gate.shape[1])
    (packed,) = run(
        functools.partial(pack_wide, ctx, widths, window),
        "pack_wide",
        [((wide_rows, LANES), low)],
        [idx, w_gate, w_up, w_down.T],
        scratch=[
            pltpu.VMEM((r, 3 * max(widths)), low),
            pltpu.VMEM((3, r, window), low),
            pltpu.SemaphoreType.DMA((3,)),
        ],
        cost=2,
        far=3,
        vmem=60,
    )
    chunks = lax.all_gather(packed, "shard", axis=0, tiled=False)
    own_x = lax.dynamic_index_in_dim(inputs, half, 0, keepdims=False)
    (own_buf,) = run(
        functools.partial(pack_attention, ctx),
        "pack_attention",
        [((inner + 16, lanes_r), low)],
        [after(idx, packed), *attention_weights, jnp.stack([norm1_gain, norm2_gain])],
        scratch=[pltpu.VMEM((inner, r), low), pltpu.SemaphoreType.DMA],
        far=4,
        vmem=60,
    )
    if shards == 4:
        low_one, high_one = step(own_buf, "shard", 1), step(own_buf, "shard", -1)
        middle = own_buf.shape[0] // 2
        far = [step(low_one[:middle], "shard", 1), step(high_one[middle:], "shard", -1)]
        from_shard = [low_one, jnp.concatenate(far), high_one]
    else:
        from_shard = [step(own_buf, "shard", k) for k in range(1, shards)]
    mine_x = [swap(own_x, "ctx", k) for k in range(1, ctx)]
    table = lax.dynamic_slice_in_dim(bias_table, half * heads, heads, 1)
    (bias,) = run(
        functools.partial(bias_body, rows, rows // 5, distance_marks),
        "bias",
        [((heads, length, length), wide)],
        [after(idx, own_buf), table],
        scalars=2,
        cost=5,
    )
    now = after(idx, *from_shard, *mine_x, bias)

    group = jnp.concatenate(from_shard)
    buf_rows = inner + 16
    place = {z: [(0, (z - 1) * buf_rows, inner)] for z in range(1, shards)}
    gathered = [group] + [swap(after(group, now), "ctx", k) for k in range(1, ctx)]
    rest_x = swap(after(jnp.stack(mine_x), now), "tensor")
    normed_one, gains = run(
        functools.partial(norm_one, ctx, shards),
        "norm_one",
        [((2 * length, width), low), ((2, width), wide)],
        [now, inputs, *mine_x, rest_x, own_buf, *from_shard],
        scratch=[pltpu.VMEM((shards, 8, r), wide)],
        cost=3,
    )
    now = after(now, *gathered[1:], normed_one)

    own_cot = lax.dynamic_index_in_dim(cotangent, half, 0, keepdims=False)
    mine_cot = [swap(after(own_cot, now), "ctx", k) for k in range(1, ctx)]
    att_mine, att_other, soft, qkv, mixed, every = run(
        functools.partial(attend, ctx, shards, rows, heads, place),
        "attend",
        [
            ((length, width), low),
            ((length, width), low),
            ((2, heads, rows, length), wide),
            ((2 * length, 3 * inner), low),
            ((2 * length, inner), low),
            ((4 * inner, width), low),
        ],
        [now, normed_one, *attention_weights, bias, *gathered],
        scratch=[pltpu.VMEM((shards, 4 * inner, r), low)],
        cost=14,
        vmem=24,
    )
    now = after(now, *mine_cot, att_other)

    att_got = swap(after(att_other, now), "tensor")
    rest_cot = swap(after(jnp.stack(mine_cot), now), "tensor")
    nt_mine, middle_own = run(
        functools.partial(middle_norm, ctx),
        "middle_norm",
        [((length, width), low), ((rows, width), wide)],
        [now, inputs, *mine_x, att_mine, att_got, gains],
    )
    nt_other = swap(nt_mine, "tensor")
    now = after(now, nt_other, rest_cot)

    def add(a, b):
        return (a.astype(wide) + b.astype(wide)).astype(low)

    tokens_out = ((ctx, rows, width), low)
    wide_grads, feed_mine, feed_other, two_mine, two_other = run(
        functools.partial(feed_forward, ctx, shards, widths),
        "feed_forward",
        [((shards, wide_rows, LANES), low)] + [tokens_out] * 4,
        [now, chunks, nt_mine, nt_other, cotangent, *mine_cot, rest_cot],
        scratch=[
            pltpu.VMEM((shards, wide_rows, LANES), low),
            pltpu.VMEM((2 * length, width), low),
            pltpu.VMEM((2 * length, width), low),
            pltpu.VMEM((2, ctx, rows, width), low),
            pltpu.VMEM((2, ctx, rows, width), low),
            pltpu.SemaphoreType.DMA((3 + shards + 2 * ctx,)),
            pltpu.SemaphoreType.DMA((4 + shards * len(widths),)),
        ]
        + [pltpu.VMEM((width, 3 * n), low) for n in widths]
        + [pltpu.VMEM((2 * length, n), low) for n in widths]
        + [pltpu.VMEM((2 * length, 2 * n), low) for n in widths],
        far=5 + ctx - 1,
        far_out=True,
        cost=20,
        vmem=60,
    )
    wide_own = lax.psum_scatter(wide_grads, "shard", scatter_dimension=0, tiled=False)
    now = after(now, two_other)

    two_got = swap(after(two_other, now), "tensor")
    two_both = [add(two_mine[k], two_got[k]) for k in range(ctx)]
    two_parts = [two_both[0]] + [swap(two_both[k], "ctx", k) for k in range(1, ctx)]
    out_in, middle_grad, gain_two = run(
        functools.partial(norm_two_back, shards, ctx),
        "norm_two_back",
        [((rows, width), low), ((rows, width), wide), ((shards, 1, r), wide)],
        [now, cotangent, *two_parts, middle_own, gains],
    )
    out_in_other = swap(out_in, "tensor")
    now = after(now, out_in_other)

    feed_got = swap(after(feed_other, now), "tensor")
    got = run(
        functools.partial(attend_back, ctx, heads),
        "attend_back",
        [((2 * rows, 2 * inner), low)] * ctx
        + [((inner // ctx, width), low)] * ctx
        + [((2 * rows, inner), low)],
        [now, out_in, out_in_other, soft, qkv, every, mixed],
        scratch=[pltpu.VMEM((2 * length, 2 * inner), low), pltpu.VMEM((2 * rows, inner), low)],
        cost=4,
        vmem=24,
    )
    kv_parts, for_out, q_grad = got[:ctx], got[ctx : 2 * ctx], got[2 * ctx]
    now = after(now, feed_got, q_grad)

    kv_parts = [kv_parts[0]] + [swap(after(kv_parts[k], now), "ctx", k) for k in range(1, ctx)]
    for_out = [for_out[0]] + [swap(after(for_out[k], now), "ctx", k) for k in range(1, ctx)]
    got = run(
        functools.partial(first_grad, ctx),
        "first_grad",
        [((rows, width), low)] * 2 + [((2 * rows, 3 * inner // ctx), low)] * ctx,
        [now, *kv_parts, q_grad, every],
        scratch=[pltpu.VMEM((2 * rows, 3 * inner), low)],
    )
    first_mine, first_other, pieces = got[0], got[1], got[2:]
    now = after(now, first_other)

    pieces = [pieces[0]] + [swap(after(pieces[k], now), "ctx", k) for k in range(1, ctx)]
    first_got = swap(after(first_other, now), "tensor")
    input_mine, gain_one = run(
        functools.partial(norm_one_back, shards),
        "norm_one_back",
        [((rows, width), low), ((shards, 1, r), wide)],
        [now, inputs, first_mine, first_got, middle_grad, gains],
    )
    (four,) = run(
        functools.partial(weight_grads, ctx, shards),
        "weight_grads",
        [((shards, inner + 16, r), low)],
        [now, normed_one, *pieces, *for_out, gain_one, gain_two],
        scratch=[
            pltpu.VMEM((2 * length, 3 * inner // ctx), low),
            pltpu.VMEM((2 * length, width), low),
            pltpu.SemaphoreType.DMA,
        ],
        far=1,
        cost=2,
        vmem=24,
    )
    now = after(now, four, input_mine)

    feed_both = [add(after(feed_mine, now)[k], feed_got[k]) for k in range(ctx)]
    feed_parts = [feed_both[0]] + [swap(feed_both[k], "ctx", k) for k in range(1, ctx)]
    (produced_mine,) = run(
        functools.partial(produce, ctx),
        "produce",
        [((rows, width), low)],
        [*feed_parts, middle_own],
        scalars=0,
    )
    input_other = swap(after(input_mine, now), "tensor")
    produced_other = swap(produced_mine, "tensor")
    out_y, out_x = run(
        place_outputs,
        "place_outputs",
        [(inputs.shape, low)] * 2,
        [now, produced_mine, produced_other, input_mine, input_other],
    )
    now = after(now, wide_own, out_y)

    wide_own = after(wide_own, now)
    half_rows = wide_rows // 2
    pair = ctx == 4
    wide_all = [swap(wide_own, "ctx", k) for k in ((1, 2) if pair else range(1, ctx))]
    four_shard = [four[0]] + [step(after(four[d], now), "shard", d) for d in range(1, shards)]
    four_own = sum((part.astype(wide) for part in four_shard)).astype(low)
    four_all = [four_own] + [swap(after(four_own, now), "ctx", k) for k in range(1, ctx)]
    now = after(now, *wide_all, *four_all[1:])

    far_halves = []
    if pair:
        far_halves = [
            swap(after(wide_all[0], now)[:half_rows], "ctx", 2),
            swap(after(wide_all[1], now)[half_rows:], "ctx", 1),
        ]
    out_q, out_k, out_v, out_o, own_gain = run(
        functools.partial(finish_attention, ctx),
        "finish_attention",
        [((inner, r), wide)] * 4 + [((2, r), wide)],
        [now, *four_all],
    )
    own_gain = own_gain + swap(own_gain, "tensor")

    def finish(now, which, sources, span, before):
        return run(
            functools.partial(finish_wide, ctx, widths, which),
            "finish_wide",
            [(w_gate.shape, wide)] * 3,
            [now, *sources, *before],
            scratch=[
                pltpu.VMEM((r, 3 * max(widths)), wide),
                pltpu.VMEM((3, r, span), wide),
                pltpu.SemaphoreType.DMA((3,)),
            ],
            far_out=True,
            into=len(before),
            cost=3,
            vmem=24,
        )

    if pair and 2 * columns % LANES == 0:
        outs = finish(now, [(0, 1), (1, 1)], [wide_own, wide_all[0]], 2 * columns, [])
        now = after(now, *far_halves, outs[0], own_gain)
        outs = finish(now, [(2, 1), (3, 2)], [wide_all[1], *far_halves], 2 * columns, outs)
    else:
        which = [(k, 1) for k in range(ctx)]
        outs = finish(now, which, [wide_own, *wide_all], ctx * columns, [])
    out_g, out_u, out_d = outs

    return (
        out_y,
        out_x,
        own_gain[0],
        out_q.T,
        out_k.T,
        out_v.T,
        out_o,
        own_gain[1],
        out_g,
        out_u,
        out_d.T,
    )


def solution(mesh):
    placed = (
        P(None, ("shard", "ctx"), None),
        P(None, ("shard", "ctx"), None),
        P("shard"),
        P("shard", "tensor"),
        P("shard", "tensor"),
        P("shard", "tensor"),
        P("tensor", "shard"),
        P("shard"),
        P("shard", "tensor"),
        P("shard", "tensor"),
        P("tensor", "shard"),
        P(),
    )
    return jax.shard_map(
        on_device, mesh=mesh, in_specs=placed, out_specs=placed[:2] + placed[2:11], check_vma=False
    )
```

```python
import functools

import jax
import jax.numpy as jnp
from jax import lax
from jax.experimental import pallas as pl
from jax.experimental.pallas import tpu as pltpu
from jax.sharding import PartitionSpec as P

DK = 64
norm_eps = 1e-06
distance_marks = (8, 12, 16, 23, 32, 46, 64, 91)
masked_score = -1e30
low = jnp.bfloat16
wide = jnp.float32
LANES = 128
COST = 1e8


def dot_nn(left, right):
    return lax.dot_general(left, right, (((1,), (0,)), ((), ())), preferred_element_type=wide)


def dot_nt(left, right):
    return lax.dot_general(left, right, (((1,), (1,)), ((), ())), preferred_element_type=wide)


def dot_tn(left, right):
    return lax.dot_general(left, right, (((0,), (0,)), ((), ())), preferred_element_type=wide)


def wrap(value, n):
    return lax.rem(value + 2 * n, n)


def run(body, name, outs, operands, scratch=(), scalars=1, cost=1, far=0, far_out=False, into=0, vmem=16):
    return pl.pallas_call(
        body,
        name=name,
        out_shape=[jax.ShapeDtypeStruct(s, d) for s, d in outs],
        in_specs=[pl.BlockSpec(memory_space=pltpu.SMEM)] * scalars
        + [pl.BlockSpec(memory_space=pltpu.HBM)] * far
        + [pl.BlockSpec(memory_space=pltpu.VMEM)] * (len(operands) - scalars - far - into)
        + [pl.BlockSpec(memory_space=pltpu.HBM)] * into,
        out_specs=[pl.BlockSpec(memory_space=pltpu.HBM if far_out else pltpu.VMEM)] * len(outs),
        scratch_shapes=list(scratch),
        input_output_aliases={len(operands) - into + i: i for i in range(into)},
        compiler_params=pltpu.CompilerParams(vmem_limit_bytes=vmem * 2**20),
        cost_estimate=pl.CostEstimate(flops=int(cost * COST), bytes_accessed=0, transcendentals=0),
    )(*operands)


def step(x, axis, k=1):
    n = lax.axis_size(axis)
    return lax.ppermute(x, axis, [(i, (i + k) % n) for i in range(n)])


def swap(x, axis, k=1):
    n = lax.axis_size(axis)
    return lax.ppermute(x, axis, [(i, i ^ k) for i in range(n)])


def after(x, *others):
    return lax.optimization_barrier((x, *others))[0]


def pack_attention(n_ctx, idx, w_q, w_k, w_v, w_o, gain, buf, held, sem):
    inner, r = w_o.shape
    for v, ref in enumerate((w_q, w_k, w_v, w_o)):

        @pl.when(idx[1] == v)
        def _(ref=ref):
            copy = pltpu.make_async_copy(ref, held, sem)
            copy.start()
            copy.wait()

    buf[0:inner, 0:r] = held[...]

    buf[inner : inner + 2, 0:r] = gain[...]


def wide_tiles(r, widths):
    rp = pl.cdiv(r, 16) * 16
    row, parts = 0, []
    for n in widths:
        full, left = divmod(3 * n, LANES)
        pieces = [(row + rp * q, r, 0, LANES * q, LANES, 0) for q in range(full)]
        row += rp * full
        if left:
            assert 2 * left == LANES
            pieces.append((row, r // 2, 0, LANES * full, left, 0))
            pieces.append((row, r // 2, r // 2, LANES * full, left, left))
            row += pl.cdiv(r // 2, 8) * 8
        parts.append(pieces)
    return parts, pl.cdiv(row, 32) * 32


def pack_wide(n_ctx, widths, window, w_g, w_u, w_d, buf, held, sems):
    c = lax.axis_index("ctx")
    r = w_g.shape[0]
    columns = sum(widths)
    parts, _ = wide_tiles(r, widths)
    for v in range(n_ctx):

        @pl.when(c == v)
        def _(v=v):
            start = min(v * columns // LANES * LANES, w_g.shape[1] - window)
            copies = [
                pltpu.make_async_copy(ref.at[:, start : start + window], held.at[i], sems.at[i])
                for i, ref in enumerate((w_g, w_u, w_d))
            ]
            for copy in copies:
                copy.start()
            for copy in copies:
                copy.wait()
            at = v * columns - start
            for n, pieces in zip(widths, parts, strict=True):
                for row, size, top, lane, lanes, to in pieces:
                    while lanes:
                        which, inside = divmod(lane, n)
                        take = min(lanes, n - inside)
                        buf[row : row + size, to : to + take] = held[
                            which, top : top + size, at + inside : at + inside + take
                        ]
                        lane, to, lanes = lane + take, to + take, lanes - take
                at += n


def bias_body(rows, seg_len, marks, idx, table, out):
    c = idx[1]
    heads, length, _ = out.shape

    def info(position):
        block = sum(((position >= rows * b).astype(jnp.int32) for b in range(1, length // rows)))
        token = (block ^ c) * rows + position - block * rows
        seg = sum(((token >= q * seg_len).astype(jnp.int32) for q in range(8, 20)))
        parent = jnp.where(seg == 0, -1, jnp.where(seg <= 4, 0, (seg - 3) >> 1))
        shift = jnp.where(seg == 0, 0, jnp.where(seg <= 4, seg - 1, seg - 2))
        return seg, parent, token - shift * seg_len

    key_seg, _, key_place = info(lax.broadcasted_iota(jnp.int32, (16, length), 1))

    def rows_of(i, _):
        at = pl.multiple_of(i * 16, 16)
        seg, parent, place = info(lax.broadcasted_iota(jnp.int32, (16, length), 0) + at)
        allowed = (key_seg == 0) | (key_seg == seg) | (key_seg == parent)
        relative = key_place - place
        magnitude = jnp.abs(relative)
        marked = sum(((magnitude >= mark).astype(jnp.int32) for mark in marks))
        bucket = jnp.where(relative > 0, 16, 0) + jnp.where(magnitude < 8, magnitude, 7 + marked)
        looked = [jnp.full(bucket.shape, table[0, h], wide) for h in range(heads)]
        for b in range(1, table.shape[0]):
            hit = bucket == b
            looked = [jnp.where(hit, table[b, h], looked[h]) for h in range(heads)]
        for h in range(heads):
            out[h, pl.ds(at, 16), :] = jnp.where(allowed, looked[h], masked_score)
        return 0

    lax.fori_loop(0, length // 16, rows_of, 0)


def tree_blocks(n_ctx, half, own, mine, rest):
    for k in range(n_ctx):
        yield 0, k, own[half] if k == 0 else mine[k - 1][...]
    for k in range(n_ctx):
        yield 1, k, own[1 - half] if k == 0 else rest[k - 1]


def norm_one(n_ctx, n_shard, idx, x_in, *refs):
    s, half = idx[0], idx[2]
    mine, rest = refs[: n_ctx - 1], refs[n_ctx - 1]
    bufs = refs[n_ctx : n_ctx + n_shard]
    normed, gains, held = refs[n_ctx + n_shard :]
    r = held.shape[2]
    _, rows, width = x_in.shape
    for k, buf in enumerate(bufs):
        at = buf.shape[0] - 16
        held[wrap(s - k, n_shard), 0:2, :] = buf[at : at + 2, 0:r].astype(wide)
    for j in range(n_shard):
        gains[:, r * j : r * (j + 1)] = held[j, 0:2, :]
    for m, k, x in tree_blocks(n_ctx, half, x_in, mine, rest):
        x = x.astype(wide)
        y = x * lax.rsqrt(jnp.mean(x * x, axis=-1, keepdims=True) + norm_eps)
        at = (m * n_ctx + k) * rows
        normed[at : at + rows, :] = (y * gains[0:1, :]).astype(low)


def attend(n_ctx, n_shard, rows, heads, place, idx, normed, w_q, w_k, w_v, w_o, bias, *refs):
    s, c = idx[0], idx[1]
    groups = 1 + max((g for pieces in place.values() for g, _, _ in pieces))
    got = [refs[g * n_ctx : (g + 1) * n_ctx] for g in range(groups)]
    att_mine, att_other, soft, qkv, mixed, every, held = refs[groups * n_ctx :]
    inner, r = w_o.shape
    length = n_ctx * rows
    for i, ref in enumerate((w_q, w_k, w_v, w_o)):
        held[s, i * inner : (i + 1) * inner, :] = ref[...]
    for v in range(n_ctx):

        @pl.when(c == v)
        def _(v=v):
            for k in range(n_ctx):
                for z, pieces in place.items():
                    at, last = (v ^ k) * inner, ((v ^ k) + 1) * inner
                    for g, row, size in pieces:
                        size = min(size, last - at)
                        held[wrap(s - z, n_shard), at : at + size, :] = got[g][k][
                            row : row + size, 0:r
                        ]
                        at += size

    for j in range(n_shard):
        every[:, r * j : r * (j + 1)] = held[j]
    qkv[...] = dot_nt(normed[...], every[0 : 3 * inner, :]).astype(low)
    for m in (1, 0):
        low_row = m * length
        for h in range(heads):
            at = DK * h
            keys = qkv[low_row : low_row + length, inner + at : inner + at + DK]
            values = qkv[low_row : low_row + length, 2 * inner + at : 2 * inner + at + DK]
            for b in range(n_ctx):
                top = low_row + b * rows
                scores = dot_nt(qkv[top : top + rows, at : at + DK], keys)
                scores += bias[h, b * rows : (b + 1) * rows, :]
                raised = jnp.exp(scores - jnp.max(scores, axis=-1, keepdims=True))
                share = raised / jnp.sum(raised, axis=-1, keepdims=True)
                if b == 0:
                    soft[m, h] = share
                mixed[top : top + rows, at : at + DK] = dot_nn(share.astype(low), values).astype(low)
        out = att_mine if m == 0 else att_other
        out[...] = dot_nn(
            mixed[low_row : low_row + length, :], every[3 * inner : 4 * inner, :]
        ).astype(low)


def middle_norm(n_ctx, idx, x_in, *refs):
    mine, (att, got, gains, normed, middle_own) = refs[: n_ctx - 1], refs[n_ctx - 1 :]
    rows = x_in.shape[1]
    for k in range(n_ctx):
        at = slice(k * rows, (k + 1) * rows)
        x = x_in[idx[2]] if k == 0 else mine[k - 1][...]
        mid = x.astype(wide) + (att[at, :].astype(wide) + got[at, :].astype(wide))
        scale = lax.rsqrt(jnp.mean(mid * mid, axis=-1, keepdims=True) + norm_eps)
        normed[at, :] = (mid * scale * gains[1:2, :]).astype(low)
        if k == 0:
            middle_own[...] = mid


def unpack_wide(parts, r, buf, weights, j):
    for e, pieces in enumerate(parts):
        for row, size, top, lane, lanes, at in pieces:
            weights[e][r * j + top : r * j + top + size, lane : lane + lanes] = buf[
                j, row : row + size, at : at + lanes
            ]


def feed_forward(n_ctx, n_shard, widths, idx, buf_far, nt_mine, nt_other, cot_in, *refs):
    half = idx[2]
    n_parts = len(widths)
    mine, rest, refs = refs[: n_ctx - 1], refs[n_ctx - 1], refs[n_ctx:]
    sent, given, refs = refs[0], refs[1 : 1 + 2 * n_parts], refs[1 + 2 * n_parts :]
    buf, nt, cot, sems, sems_out = refs[:5]
    weights, hidden, pair = (refs[5 + i * n_parts : 5 + (i + 1) * n_parts] for i in range(3))
    length, _ = nt_mine.shape
    rows = length // n_ctx
    r = weights[0].shape[0] // n_shard

    def block(m, k):
        at = (m * n_ctx + k) * rows
        return slice(at, at + rows)

    begun = [pltpu.make_async_copy(buf_far.at[0], buf.at[0], sems.at[0])]
    moves = [
        (nt_mine, nt.at[0:length, :]),
        (nt_other, nt.at[length : 2 * length, :]),
        (cot_in.at[half], cot.at[block(0, 0), :]),
        (cot_in.at[1 - half], cot.at[block(1, 0), :]),
    ]
    moves += [(buf_far.at[j], buf.at[j]) for j in range(1, n_shard)]
    for k in range(1, n_ctx):
        moves.append((mine[k - 1], cot.at[block(0, k), :]))
        moves.append((rest.at[k - 1], cot.at[block(1, k), :]))
    begun += [pltpu.make_async_copy(x, y, sems.at[i + 1]) for i, (x, y) in enumerate(moves)]
    for copy in begun:
        copy.start()
    loads = [begun[0]] + begun[5 : 4 + n_shard]
    parts, _ = wide_tiles(r, widths)
    for j in range(n_shard):
        loads[j].wait()
        unpack_wide(parts, r, buf, weights, j)
    for copy in begun[1:5] + begun[4 + n_shard :]:
        copy.wait()
    c0, c1 = 0.7978845608028654, 0.044715
    out = []

    def write(source, target):
        copy = pltpu.make_async_copy(source, target, sems_out.at[len(out)])
        copy.start()
        out.append(copy)

    for m in (1, 0):
        at = slice(m * length, (m + 1) * length)
        for e, n in enumerate(widths):
            both = dot_nn(nt[at, :], weights[e][:, 0 : 2 * n])
            back = dot_nn(cot[at, :], weights[e][:, 2 * n : 3 * n])
            gate, up = both[:, :n], both[:, n:]
            square = gate * gate
            bent = jnp.tanh(c0 * (gate + c1 * gate * square))
            half_one = 0.5 * (1.0 + bent)
            active = gate * half_one
            slope = half_one + 0.5 * gate * (1.0 - bent * bent) * (c0 * (1.0 + 3.0 * c1 * square))
            hidden[e][at, :] = (active * up).astype(low)
            pair[e][at, 0:n] = (back * up * slope).astype(low)
            pair[e][at, n : 2 * n] = (back * active).astype(low)
    for source, target in zip((*hidden, *pair), given, strict=True):
        write(source, target)
    for e, n in enumerate(widths):
        for_in = dot_tn(nt[...], pair[e][...]).astype(low)
        for_down = dot_tn(cot[...], hidden[e][...]).astype(low)
        first, last = parts[e][0][0], parts[e][-1][0] + parts[e][-1][1]
        for j in range(n_shard):
            for row, size, top, lane, lanes, at in parts[e]:
                top = r * j + top
                inside = max(0, min(lanes, 2 * n - lane))
                if inside:
                    buf[j, row : row + size, at : at + inside] = for_in[
                        top : top + size, lane : lane + inside
                    ]
                if inside < lanes:
                    begin = lane + inside - 2 * n
                    buf[j, row : row + size, at + inside : at + lanes] = for_down[
                        top : top + size, begin : begin + lanes - inside
                    ]
            here = slice(first, last if e < n_parts - 1 else buf.shape[1])
            write(buf.at[j, here, :], sent.at[j, here, :])
    for copy in out:
        copy.wait()


def feed_out(n_ctx, n_shard, widths, idx, buf_far, *refs):
    n_parts = len(widths)
    far, refs = refs[: 2 * n_parts], refs[2 * n_parts :]
    feed, two, refs = refs[0:2], refs[2:4], refs[4:]
    buf, feed_held, two_held, sems, sems_out = refs[:5]
    weights, hidden, pair = (refs[5 + i * n_parts : 5 + (i + 1) * n_parts] for i in range(3))
    _, _, rows, _ = two_held.shape
    length = n_ctx * rows
    r = weights[0].shape[0] // n_shard
    parts, _ = wide_tiles(r, widths)
    moves = [(buf_far.at[j], buf.at[j]) for j in range(n_shard)]
    moves += list(zip(far, (*hidden, *pair), strict=True))
    begun = [pltpu.make_async_copy(x, y, sems.at[i]) for i, (x, y) in enumerate(moves)]
    for copy in begun:
        copy.start()
    for j in range(n_shard):
        begun[j].wait()
        unpack_wide(parts, r, buf, weights, j)
    for copy in begun[n_shard:]:
        copy.wait()
    out = []
    for held, given, lefts, first, last in (
        (two_held, two, pair, 0, 2),
        (feed_held, feed, hidden, 2, 3),
    ):
        for m in (1, 0):
            at = slice(m * length, (m + 1) * length)
            total = sum(
                (
                    dot_nt(lefts[e][at, :], weights[e][:, first * n : last * n])
                    for e, n in enumerate(widths)
                )
            )
            for i in range(n_ctx):
                held[m, i] = total[i * rows : (i + 1) * rows].astype(low)
            copy = pltpu.make_async_copy(held.at[m], given[m], sems_out.at[len(out)])
            copy.start()
            out.append(copy)
    for copy in out:
        copy.wait()


def norm_two_back(n_shard, n_parts, idx, cot_in, *refs):
    parts, refs = refs[:n_parts], refs[n_parts:]
    middle, gains, out_in, grad, gain_grad = refs
    r = gain_grad.shape[2]
    mid = middle[...]
    two = sum((p[...].astype(wide) for p in parts))
    scale = lax.rsqrt(jnp.mean(mid * mid, axis=-1, keepdims=True) + norm_eps)
    u = two * gains[1:2, :]
    inner = jnp.mean(u * mid, axis=-1, keepdims=True) * (scale * scale * scale)
    back = cot_in[idx[2]].astype(wide) + scale * u - mid * inner
    grad[...] = back
    out_in[...] = back.astype(low)
    total = jnp.sum(two * mid * scale, axis=0, keepdims=True)
    for j in range(n_shard):
        gain_grad[j] = total[:, r * j : r * (j + 1)]


def attend_back(n_ctx, heads, idx, o_mine, o_other, soft, qkv, every, mixed, *refs):
    kv, for_out, (q_grad, kv_all, mixed_grad) = refs[:n_ctx], refs[n_ctx : 2 * n_ctx], refs[2 * n_ctx :]
    rows = o_mine.shape[0]
    length = n_ctx * rows
    inner = heads * DK
    share_rows = for_out[0].shape[0]
    for m, o_in in ((0, o_mine), (1, o_other)):
        top, own = m * length, m * rows
        mixed_grad[own : own + rows, :] = dot_nt(o_in[...], every[3 * inner :, :]).astype(low)
        for h in range(heads):
            at = DK * h
            share = soft[m, h]
            grad = mixed_grad[own : own + rows, at : at + DK]
            keys = qkv[top : top + length, inner + at : inner + at + DK]
            values = qkv[top : top + length, 2 * inner + at : 2 * inner + at + DK]
            queries = qkv[top : top + rows, at : at + DK]
            weight = dot_nt(grad, values)
            ds = share * (weight - jnp.sum(weight * share, axis=-1, keepdims=True))
            ds = ds.astype(low)
            q_grad[own : own + rows, at : at + DK] = dot_nn(ds, keys).astype(low)
            kv_all[top : top + length, at : at + DK] = dot_tn(ds, queries).astype(low)
            kv_all[top : top + length, inner + at : inner + at + DK] = dot_tn(
                share.astype(low), grad
            ).astype(low)
        for k in range(n_ctx):
            kv[k][own : own + rows, :] = kv_all[top + k * rows : top + (k + 1) * rows, :]
    got = dot_tn(mixed[0:rows, :], o_mine[...])
    got += dot_tn(mixed[length : length + rows, :], o_other[...])
    got = got.astype(low)
    for v in range(n_ctx):

        @pl.when(idx[1] == v)
        def _(v=v):
            for k in range(n_ctx):
                for_out[k][...] = got[(v ^ k) * share_rows : ((v ^ k) + 1) * share_rows, :]


def first_grad(n_ctx, idx, *refs):
    parts, (q_grad, every, out_mine, out_other), pieces, three = (
        refs[:n_ctx],
        refs[n_ctx : n_ctx + 4],
        refs[n_ctx + 4 : 2 * n_ctx + 4],
        refs[2 * n_ctx + 4],
    )
    rows2, inner = q_grad.shape
    rows = rows2 // 2
    size = inner // n_ctx
    three[:, 0:inner] = q_grad[...]
    three[:, inner:] = sum((p[...].astype(wide) for p in parts)).astype(low)
    for v in range(n_ctx):

        @pl.when(idx[1] == v)
        def _(v=v):
            for k in range(n_ctx):
                for i in range(3):
                    at = i * inner + (v ^ k) * size
                    pieces[k][:, i * size : (i + 1) * size] = three[:, at : at + size]

    got = dot_nn(three[...], every[0 : 3 * inner, :]).astype(low)
    out_mine[...] = got[0:rows]
    out_other[...] = got[rows:]


def weight_grads(n_ctx, n_shard, idx, normed, *refs):
    pieces, for_out, refs = refs[:n_ctx], refs[n_ctx : 2 * n_ctx], refs[2 * n_ctx :]
    gain_one, gain_two, stack, grads, held, sem = refs
    s = idx[0]
    copy = pltpu.make_async_copy(normed, held, sem)
    copy.start()
    size, r = for_out[0].shape[0], stack.shape[2]
    rows = pieces[0].shape[0] // 2
    out_rows = sum((p[...].astype(wide) for p in for_out))
    for j in range(n_shard):
        d = wrap(j - s, n_shard)
        stack[d, 3 * size : 4 * size, :] = out_rows[:, r * j : r * (j + 1)].astype(low)
        stack[d, 4 * size : 4 * size + 1, :] = gain_one[j].astype(low)
        stack[d, 4 * size + 1 : 4 * size + 2, :] = gain_two[j].astype(low)
    for m in range(2):
        for k in range(n_ctx):
            at = (m * n_ctx + k) * rows
            grads[at : at + rows, :] = pieces[k][m * rows : (m + 1) * rows, :]
    copy.wait()
    got = dot_tn(grads[...], held[...])
    for j in range(n_shard):
        stack[wrap(j - s, n_shard), 0 : 3 * size, :] = got[:, r * j : r * (j + 1)].astype(low)


def place_outputs(idx, a_mine, a_other, b_mine, b_other, a, b):
    half = idx[2]
    a[half] = a_mine[...]
    a[1 - half] = a_other[...]
    b[half] = b_mine[...]
    b[1 - half] = b_other[...]


def norm_one_back(n_shard, idx, x_in, mine, got, grad, gains, out, gain_grad):
    r = gain_grad.shape[2]
    x = x_in[idx[2]].astype(wide)
    one = mine[...].astype(wide) + got[...].astype(wide)
    scale = lax.rsqrt(jnp.mean(x * x, axis=-1, keepdims=True) + norm_eps)
    u = one * gains[0:1, :]
    inner = jnp.mean(u * x, axis=-1, keepdims=True) * (scale * scale * scale)
    out[...] = (grad[...] + scale * u - x * inner).astype(low)
    total = jnp.sum(one * x * scale, axis=0, keepdims=True)
    for j in range(n_shard):
        gain_grad[j] = total[:, r * j : r * (j + 1)]


def produce(n_parts, *refs):
    parts, (middle, out) = refs[:n_parts], refs[n_parts:]
    out[...] = (middle[...] + sum((p[...].astype(wide) for p in parts))).astype(low)


def finish_wide(n_ctx, widths, groups, idx, *refs):
    flat = [item for group in groups for item in group]
    count = sum((pieces for _, pieces, _ in flat))
    sources, refs = refs[:count], refs[count:]
    n_outs = 3
    outs, (stage, held, sems) = refs[-3 - n_outs : -3], refs[-3:]
    r = outs[0].shape[0]
    columns = sum(widths)
    parts, rows = wide_tiles(r, widths)
    for v in range(n_ctx):

        @pl.when(idx[1] == v)
        def _(v=v):
            first = 0
            copies = []
            for g, group in enumerate(groups):
                taken = []
                for k, pieces, lanes_kind in group:
                    begin = (v ^ k) * columns
                    tile_low = pl.cdiv(begin, LANES) * LANES - begin
                    tile_high = (begin + columns) // LANES * LANES - begin
                    if lanes_kind == "all":
                        low_lane, high_lane = 0, columns
                    elif lanes_kind == "full":
                        low_lane, high_lane = tile_low, tile_high
                    elif tile_low:
                        low_lane, high_lane = 0, tile_low
                    else:
                        low_lane, high_lane = tile_high, columns
                    taken.append((k, pieces, low_lane, high_lane, first))
                    first += pieces
                start = min(((v ^ k) * columns + lo for k, _, lo, _, _ in taken))
                stop = max(((v ^ k) * columns + hi for k, _, _, hi, _ in taken))
                for k, pieces, low_lane, high_lane, at_source in taken:
                    size_each = rows // pieces
                    for i, n in enumerate(widths):
                        base = sum(widths[:i])
                        lo, hi = max(low_lane, base), min(high_lane, base + n)
                        if lo >= hi:
                            continue
                        for row, size, top, lane, lanes, at in parts[i]:
                            done = 0
                            while done < size:
                                part, here = divmod(row + done, size_each)
                                many = min(size - done, size_each - here)
                                stage[top + done : top + done + many, lane : lane + lanes] = (
                                    sources[at_source + part][
                                        here : here + many, at : at + lanes
                                    ].astype(wide)
                                )
                                done += many
                        to = (v ^ k) * columns + lo - start
                        for j in range(3):
                            held[g, j, :, to : to + hi - lo] = stage[
                                :, j * n + lo - base : j * n + hi - base
                            ]
                for j in range(3):
                    copy = pltpu.make_async_copy(
                        held.at[g, j, :, 0 : stop - start],
                        outs[j].at[:, start:stop],
                        sems.at[3 * g + j],
                    )
                    copy.start()
                    copies.append(copy)
            for copy in copies:
                copy.wait()


def finish_attention(n_ctx, idx, *refs):
    pieces, (outs, gains) = refs[:n_ctx], (refs[n_ctx:-1], refs[-1])
    inner, _ = outs[0].shape
    size = inner // n_ctx
    for v in range(n_ctx):

        @pl.when(idx[1] == v)
        def _(v=v):
            for k in range(n_ctx):
                at = (v ^ k) * size
                for i in range(4):
                    outs[i][at : at + size, :] = pieces[k][i * size : (i + 1) * size, :].astype(wide)

    gains[...] = sum((p[inner : inner + 2, :].astype(wide) for p in pieces))


def on_device(
    inputs,
    cotangent,
    norm1_gain,
    w_query,
    w_key,
    w_value,
    w_out,
    norm2_gain,
    w_gate,
    w_up,
    w_down,
    bias_table,
):
    _, rows, width = inputs.shape
    shards, ctx = lax.axis_size("shard"), lax.axis_size("ctx")
    inner, r = w_out.shape
    heads = inner // DK
    length = ctx * rows
    columns = w_gate.shape[1] // ctx
    first_width = pl.cdiv(columns, 2 * LANES) * LANES
    widths = (first_width, columns - first_width)
    lanes_r = pl.cdiv(r, LANES) * LANES
    s, c, half = lax.axis_index("shard"), lax.axis_index("ctx"), lax.axis_index("tensor")
    idx = jnp.stack([s, c, half]).astype(jnp.int32)
    attention_weights = (w_query.T, w_key.T, w_value.T, w_out)


    wide_rows = wide_tiles(r, widths)[1]
    window = min(pl.cdiv(columns, LANES) * LANES, w_gate.shape[1])
    (packed,) = run(
        functools.partial(pack_wide, ctx, widths, window),
        "pack_wide",
        [((wide_rows, LANES), low)],
        [w_gate, w_up, w_down.T],
        scalars=0,
        scratch=[
            pltpu.VMEM((3, r, window), low),
            pltpu.SemaphoreType.DMA((3,)),
        ],
        cost=2,
        far=3,
        vmem=60,
    )
    chunks = lax.all_gather(packed, "shard", axis=0, tiled=False)
    own_x = lax.dynamic_index_in_dim(inputs, half, 0, keepdims=False)
    (own_buf,) = run(
        functools.partial(pack_attention, ctx),
        "pack_attention",
        [((inner + 16, lanes_r), low)],
        [after(idx, packed), *attention_weights, jnp.stack([norm1_gain, norm2_gain])],
        scratch=[pltpu.VMEM((inner, r), low), pltpu.SemaphoreType.DMA],
        far=4,
        vmem=60,
    )
    if shards == 4:
        low_one, high_one = step(own_buf, "shard", 1), step(own_buf, "shard", -1)
        middle = own_buf.shape[0] // 2
        far = [step(low_one[:middle], "shard", 1), step(high_one[middle:], "shard", -1)]
        from_shard = [low_one, jnp.concatenate(far), high_one]
    else:
        from_shard = [step(own_buf, "shard", k) for k in range(1, shards)]
    mine_x = [swap(own_x, "ctx", k) for k in range(1, ctx)]
    table = lax.dynamic_slice_in_dim(bias_table, half * heads, heads, 1)
    (bias,) = run(
        functools.partial(bias_body, rows, rows // 5, distance_marks),
        "bias",
        [((heads, length, length), wide)],
        [after(idx, own_buf), table],
        scalars=2,
        cost=5,
    )
    now = after(idx, *from_shard, *mine_x, bias)

    group = jnp.concatenate(from_shard)
    buf_rows = inner + 16
    place = {z: [(0, (z - 1) * buf_rows, inner)] for z in range(1, shards)}
    gathered = [group] + [swap(after(group, now), "ctx", k) for k in range(1, ctx)]
    rest_x = swap(after(jnp.stack(mine_x), now), "tensor")
    normed_one, gains = run(
        functools.partial(norm_one, ctx, shards),
        "norm_one",
        [((2 * length, width), low), ((2, width), wide)],
        [now, inputs, *mine_x, rest_x, own_buf, *from_shard],
        scratch=[pltpu.VMEM((shards, 8, r), wide)],
        cost=3,
    )
    now = after(now, *gathered[1:], normed_one)

    own_cot = lax.dynamic_index_in_dim(cotangent, half, 0, keepdims=False)
    mine_cot = [swap(after(own_cot, now), "ctx", k) for k in range(1, ctx)]
    att_mine, att_other, soft, qkv, mixed, every = run(
        functools.partial(attend, ctx, shards, rows, heads, place),
        "attend",
        [
            ((length, width), low),
            ((length, width), low),
            ((2, heads, rows, length), wide),
            ((2 * length, 3 * inner), low),
            ((2 * length, inner), low),
            ((4 * inner, width), low),
        ],
        [now, normed_one, *attention_weights, bias, *gathered],
        scratch=[pltpu.VMEM((shards, 4 * inner, r), low)],
        cost=14,
        vmem=24,
    )
    now = after(now, *mine_cot, att_other)

    att_got = swap(after(att_other, now), "tensor")
    rest_cot = swap(after(jnp.stack(mine_cot), now), "tensor")
    nt_mine, middle_own = run(
        functools.partial(middle_norm, ctx),
        "middle_norm",
        [((length, width), low), ((rows, width), wide)],
        [now, inputs, *mine_x, att_mine, att_got, gains],
    )
    nt_other = swap(nt_mine, "tensor")
    now = after(now, nt_other, rest_cot)

    def add(a, b):
        return (a.astype(wide) + b.astype(wide)).astype(low)

    tokens_out = ((ctx, rows, width), low)
    units = [((2 * length, n), low) for n in (*widths, *(2 * n for n in widths))]
    unit_scratch = [pltpu.VMEM(shape, kind) for shape, kind in units]
    weight_scratch = [pltpu.VMEM((width, 3 * n), low) for n in widths]
    wide_grads, *units = run(
        functools.partial(feed_forward, ctx, shards, widths),
        "feed_forward",
        [((shards, wide_rows, LANES), low), *units],
        [now, chunks, nt_mine, nt_other, cotangent, *mine_cot, rest_cot],
        scratch=[
            pltpu.VMEM((shards, wide_rows, LANES), low),
            pltpu.VMEM((2 * length, width), low),
            pltpu.VMEM((2 * length, width), low),
            pltpu.SemaphoreType.DMA((3 + shards + 2 * ctx,)),
            pltpu.SemaphoreType.DMA(((2 + shards) * len(widths),)),
            *weight_scratch,
            *unit_scratch,
        ],
        far=5 + ctx - 1,
        far_out=True,
        cost=14,
        vmem=60,
    )
    wide_own = lax.psum_scatter(wide_grads, "shard", scatter_dimension=0, tiled=False)
    feed_mine, feed_other, two_mine, two_other = run(
        functools.partial(feed_out, ctx, shards, widths),
        "feed_out",
        [tokens_out] * 4,
        [now, chunks, *units],
        scratch=[
            pltpu.VMEM((shards, wide_rows, LANES), low),
            pltpu.VMEM((2, ctx, rows, width), low),
            pltpu.VMEM((2, ctx, rows, width), low),
            pltpu.SemaphoreType.DMA((shards + 2 * len(widths),)),
            pltpu.SemaphoreType.DMA((4,)),
            *weight_scratch,
            *unit_scratch,
        ],
        far=1 + 2 * len(widths),
        far_out=True,
        cost=5,
        vmem=60,
    )
    now = after(now, two_other)

    two_got = swap(after(two_other, now), "tensor")
    two_both = [add(two_mine[k], two_got[k]) for k in range(ctx)]
    two_parts = [two_both[0]] + [swap(two_both[k], "ctx", k) for k in range(1, ctx)]
    out_in, middle_grad, gain_two = run(
        functools.partial(norm_two_back, shards, ctx),
        "norm_two_back",
        [((rows, width), low), ((rows, width), wide), ((shards, 1, r), wide)],
        [now, cotangent, *two_parts, middle_own, gains],
    )
    out_in_other = swap(out_in, "tensor")
    now = after(now, out_in_other)

    feed_got = swap(after(feed_other, now), "tensor")
    got = run(
        functools.partial(attend_back, ctx, heads),
        "attend_back",
        [((2 * rows, 2 * inner), low)] * ctx
        + [((inner // ctx, width), low)] * ctx
        + [((2 * rows, inner), low)],
        [now, out_in, out_in_other, soft, qkv, every, mixed],
        scratch=[pltpu.VMEM((2 * length, 2 * inner), low), pltpu.VMEM((2 * rows, inner), low)],
        cost=4,
        vmem=24,
    )
    kv_parts, for_out, q_grad = got[:ctx], got[ctx : 2 * ctx], got[2 * ctx]
    now = after(now, feed_got, q_grad)

    kv_parts = [kv_parts[0]] + [swap(after(kv_parts[k], now), "ctx", k) for k in range(1, ctx)]
    for_out = [for_out[0]] + [swap(after(for_out[k], now), "ctx", k) for k in range(1, ctx)]
    got = run(
        functools.partial(first_grad, ctx),
        "first_grad",
        [((rows, width), low)] * 2 + [((2 * rows, 3 * inner // ctx), low)] * ctx,
        [now, *kv_parts, q_grad, every],
        scratch=[pltpu.VMEM((2 * rows, 3 * inner), low)],
    )
    first_mine, first_other, pieces = got[0], got[1], got[2:]
    now = after(now, first_other)

    pieces = [pieces[0]] + [swap(after(pieces[k], now), "ctx", k) for k in range(1, ctx)]
    first_got = swap(after(first_other, now), "tensor")
    input_mine, gain_one = run(
        functools.partial(norm_one_back, shards),
        "norm_one_back",
        [((rows, width), low), ((shards, 1, r), wide)],
        [now, inputs, first_mine, first_got, middle_grad, gains],
    )
    feed_both = [add(after(feed_mine, now)[k], feed_got[k]) for k in range(ctx)]
    feed_parts = [feed_both[0]] + [swap(feed_both[k], "ctx", k) for k in range(1, ctx)]
    now = after(now, *pieces[1:], *for_out[1:], *feed_parts[1:], input_mine)
    (four,) = run(
        functools.partial(weight_grads, ctx, shards),
        "weight_grads",
        [((shards, inner + 16, r), low)],
        [now, normed_one, *pieces, *for_out, gain_one, gain_two],
        scratch=[
            pltpu.VMEM((2 * length, 3 * inner // ctx), low),
            pltpu.VMEM((2 * length, width), low),
            pltpu.SemaphoreType.DMA,
        ],
        far=1,
        cost=2,
        vmem=24,
    )
    now = after(now, four, input_mine)

    (produced_mine,) = run(
        functools.partial(produce, ctx),
        "produce",
        [((rows, width), low)],
        [*feed_parts, middle_own],
        scalars=0,
    )
    input_other = swap(after(input_mine, now), "tensor")
    produced_other = swap(produced_mine, "tensor")
    now = after(now, wide_own, produced_other, input_other)

    wide_own = after(wide_own, now)
    half_rows = wide_rows // 2
    pair = ctx == 4
    wide_all = [swap(wide_own, "ctx", k) for k in ((1, 2) if pair else range(1, ctx))]
    four_shard = [four[0]] + [step(after(four[d], now), "shard", d) for d in range(1, shards)]
    out_y, out_x = run(
        place_outputs,
        "place_outputs",
        [(inputs.shape, low)] * 2,
        [now, produced_mine, produced_other, input_mine, input_other],
    )
    four_shard = [four[0]] + [after(part, out_y) for part in four_shard[1:]]
    four_own = sum((part.astype(wide) for part in four_shard)).astype(low)
    four_all = [four_own] + [swap(after(four_own, now), "ctx", k) for k in range(1, ctx)]
    now = after(now, *wide_all, *four_all[1:])

    far_halves = []
    if pair:
        far_halves = [
            swap(after(wide_all[0], now)[:half_rows], "ctx", 2),
            swap(after(wide_all[1], now)[half_rows:], "ctx", 1),
        ]
    out_q, out_k, out_v, out_o, own_gain = run(
        functools.partial(finish_attention, ctx),
        "finish_attention",
        [((inner, r), wide)] * 4 + [((2, r), wide)],
        [now, *four_all],
    )
    own_gain = own_gain + swap(own_gain, "tensor")

    def finish(now, groups, sources, span, before):
        return run(
            functools.partial(finish_wide, ctx, widths, groups),
            "finish_wide",
            [(w_gate.shape, wide)] * 3,
            [now, *sources, *before],
            scratch=[
                pltpu.VMEM((r, 3 * max(widths)), wide),
                pltpu.VMEM((len(groups), 3, r, span), wide),
                pltpu.SemaphoreType.DMA((3 * len(groups),)),
            ],
            far_out=True,
            into=len(before),
            cost=3,
            vmem=24,
        )

    if pair and 2 * columns % LANES == 0:
        groups = [[(0, 1, "all"), (1, 1, "all")], [(2, 1, "full")]]
        outs = finish(now, groups, [wide_own, *wide_all], 2 * columns, [])
        now = after(now, *far_halves, outs[0], own_gain)
        groups = [[(2, 1, "rest"), (3, 2, "all")]]
        outs = finish(now, groups, [wide_all[1], *far_halves], 2 * columns, outs)
    else:
        groups = [[(k, 1, "all") for k in range(ctx)]]
        outs = finish(now, groups, [wide_own, *wide_all], ctx * columns, [])
    out_g, out_u, out_d = outs

    return (
        out_y,
        out_x,
        own_gain[0],
        out_q.T,
        out_k.T,
        out_v.T,
        out_o,
        own_gain[1],
        out_g,
        out_u,
        out_d.T,
    )


def solution(mesh):
    placed = (
        P(None, ("shard", "ctx"), None),
        P(None, ("shard", "ctx"), None),
        P("shard"),
        P("shard", "tensor"),
        P("shard", "tensor"),
        P("shard", "tensor"),
        P("tensor", "shard"),
        P("shard"),
        P("shard", "tensor"),
        P("shard", "tensor"),
        P("tensor", "shard"),
        P(),
    )
    return jax.shard_map(
        on_device, mesh=mesh, in_specs=placed, out_specs=placed[:2] + placed[2:11], check_vma=False
    )
```

```python
import functools

import jax
import jax.numpy as jnp
from jax import lax
from jax.experimental import pallas as pl
from jax.experimental.pallas import tpu as pltpu
from jax.sharding import PartitionSpec as P

DK = 64
norm_eps = 1e-06
distance_marks = (8, 12, 16, 23, 32, 46, 64, 91)
masked_score = -1e30
low = jnp.bfloat16
wide = jnp.float32
LANES = 128
COST = 1e8


def dot_nn(left, right):
    return lax.dot_general(left, right, (((1,), (0,)), ((), ())), preferred_element_type=wide)


def dot_nt(left, right):
    return lax.dot_general(left, right, (((1,), (1,)), ((), ())), preferred_element_type=wide)


def dot_tn(left, right):
    return lax.dot_general(left, right, (((0,), (0,)), ((), ())), preferred_element_type=wide)


def wrap(value, n):
    return lax.rem(value + 2 * n, n)


def run(body, name, outs, operands, scratch=(), scalars=1, cost=1, far=0, far_out=False, into=0, vmem=16):
    return pl.pallas_call(
        body,
        name=name,
        out_shape=[jax.ShapeDtypeStruct(s, d) for s, d in outs],
        in_specs=[pl.BlockSpec(memory_space=pltpu.SMEM)] * scalars
        + [pl.BlockSpec(memory_space=pltpu.HBM)] * far
        + [pl.BlockSpec(memory_space=pltpu.VMEM)] * (len(operands) - scalars - far - into)
        + [pl.BlockSpec(memory_space=pltpu.HBM)] * into,
        out_specs=[pl.BlockSpec(memory_space=pltpu.HBM if far_out else pltpu.VMEM)] * len(outs),
        scratch_shapes=list(scratch),
        input_output_aliases={len(operands) - into + i: i for i in range(into)},
        compiler_params=pltpu.CompilerParams(vmem_limit_bytes=vmem * 2**20),
        cost_estimate=pl.CostEstimate(flops=int(cost * COST), bytes_accessed=0, transcendentals=0),
    )(*operands)


def step(x, axis, k=1):
    n = lax.axis_size(axis)
    return lax.ppermute(x, axis, [(i, (i + k) % n) for i in range(n)])


def swap(x, axis, k=1):
    n = lax.axis_size(axis)
    return lax.ppermute(x, axis, [(i, i ^ k) for i in range(n)])


def after(x, *others):
    return lax.optimization_barrier((x, *others))[0]


def pack_attention(n_ctx, idx, w_q, w_k, w_v, w_o, gain, buf, held, sem):
    inner, r = w_o.shape
    for v, ref in enumerate((w_q, w_k, w_v, w_o)):

        @pl.when(idx[1] == v)
        def _(ref=ref):
            copy = pltpu.make_async_copy(ref, held, sem)
            copy.start()
            copy.wait()

    buf[0:inner, 0:r] = held[...]

    buf[inner : inner + 2, 0:r] = gain[...]


def wide_tiles(r, widths):
    rp = pl.cdiv(r, 16) * 16
    row, parts = 0, []
    for n in widths:
        full, left = divmod(3 * n, LANES)
        pieces = [(row + rp * q, r, 0, LANES * q, LANES, 0) for q in range(full)]
        row += rp * full
        if left:
            assert 2 * left == LANES
            pieces.append((row, r // 2, 0, LANES * full, left, 0))
            pieces.append((row, r // 2, r // 2, LANES * full, left, left))
            row += pl.cdiv(r // 2, 8) * 8
        parts.append(pieces)
    return parts, pl.cdiv(row, 32) * 32


def pack_wide(period, widths, window, w_g, w_u, w_d, buf, held, sems):
    c = lax.axis_index("ctx")
    r = w_g.shape[0]
    columns = sum(widths)
    parts, _ = wide_tiles(r, widths)
    for v in range(period):

        @pl.when(lax.rem(c, period) == v)
        def _(v=v):
            start = v * columns // LANES * LANES
            far = lax.div(c, period) * (period * columns) + start
            here = pl.ds(pl.multiple_of(far, LANES), window)
            copies = [
                pltpu.make_async_copy(ref.at[:, here], held.at[i], sems.at[i])
                for i, ref in enumerate((w_g, w_u, w_d))
            ]
            for copy in copies:
                copy.start()
            for copy in copies:
                copy.wait()
            at = v * columns - start
            for n, pieces in zip(widths, parts, strict=True):
                for row, size, top, lane, lanes, to in pieces:
                    while lanes:
                        which, inside = divmod(lane, n)
                        take = min(lanes, n - inside)
                        buf[row : row + size, to : to + take] = held[
                            which, top : top + size, at + inside : at + inside + take
                        ]
                        lane, to, lanes = lane + take, to + take, lanes - take
                at += n


def bias_body(rows, seg_len, marks, idx, table, out):
    c = idx[1]
    heads, length, _ = out.shape

    def info(position):
        block = sum(((position >= rows * b).astype(jnp.int32) for b in range(1, length // rows)))
        token = (block ^ c) * rows + position - block * rows
        seg = sum(((token >= q * seg_len).astype(jnp.int32) for q in range(8, 20)))
        parent = jnp.where(seg == 0, -1, jnp.where(seg <= 4, 0, (seg - 3) >> 1))
        shift = jnp.where(seg == 0, 0, jnp.where(seg <= 4, seg - 1, seg - 2))
        return seg, parent, token - shift * seg_len

    key_seg, _, key_place = info(lax.broadcasted_iota(jnp.int32, (16, length), 1))

    def rows_of(i, _):
        at = pl.multiple_of(i * 16, 16)
        seg, parent, place = info(lax.broadcasted_iota(jnp.int32, (16, length), 0) + at)
        allowed = (key_seg == 0) | (key_seg == seg) | (key_seg == parent)
        relative = key_place - place
        magnitude = jnp.abs(relative)
        marked = sum(((magnitude >= mark).astype(jnp.int32) for mark in marks))
        bucket = jnp.where(relative > 0, 16, 0) + jnp.where(magnitude < 8, magnitude, 7 + marked)
        looked = [jnp.full(bucket.shape, table[0, h], wide) for h in range(heads)]
        for b in range(1, table.shape[0]):
            hit = bucket == b
            looked = [jnp.where(hit, table[b, h], looked[h]) for h in range(heads)]
        for h in range(heads):
            out[h, pl.ds(at, 16), :] = jnp.where(allowed, looked[h], masked_score)
        return 0

    lax.fori_loop(0, length // 16, rows_of, 0)


def tree_blocks(n_ctx, half, own, mine, rest):
    for k in range(n_ctx):
        yield 0, k, own[half] if k == 0 else mine[k - 1][...]
    for k in range(n_ctx):
        yield 1, k, own[1 - half] if k == 0 else rest[k - 1]


def norm_one(n_ctx, n_shard, idx, x_in, *refs):
    s, half = idx[0], idx[2]
    mine, rest = refs[: n_ctx - 1], refs[n_ctx - 1]
    bufs = refs[n_ctx : n_ctx + n_shard]
    normed, gains, held = refs[n_ctx + n_shard :]
    r = held.shape[2]
    _, rows, width = x_in.shape
    for k, buf in enumerate(bufs):
        at = buf.shape[0] - 16
        held[wrap(s - k, n_shard), 0:2, :] = buf[at : at + 2, 0:r].astype(wide)
    for j in range(n_shard):
        gains[:, r * j : r * (j + 1)] = held[j, 0:2, :]
    for m, k, x in tree_blocks(n_ctx, half, x_in, mine, rest):
        x = x.astype(wide)
        y = x * lax.rsqrt(jnp.mean(x * x, axis=-1, keepdims=True) + norm_eps)
        at = (m * n_ctx + k) * rows
        normed[at : at + rows, :] = (y * gains[0:1, :]).astype(low)


def attend(n_ctx, n_shard, rows, heads, place, idx, normed, w_q, w_k, w_v, w_o, bias, *refs):
    s, c = idx[0], idx[1]
    groups = 1 + max((g for pieces in place.values() for g, _, _ in pieces))
    got = [refs[g * n_ctx : (g + 1) * n_ctx] for g in range(groups)]
    att_mine, att_other, soft, qkv, mixed, every, held = refs[groups * n_ctx :]
    inner, r = w_o.shape
    length = n_ctx * rows
    for i, ref in enumerate((w_q, w_k, w_v, w_o)):
        held[s, i * inner : (i + 1) * inner, :] = ref[...]
    for v in range(n_ctx):

        @pl.when(c == v)
        def _(v=v):
            for k in range(n_ctx):
                for z, pieces in place.items():
                    at, last = (v ^ k) * inner, ((v ^ k) + 1) * inner
                    for g, row, size in pieces:
                        size = min(size, last - at)
                        held[wrap(s - z, n_shard), at : at + size, :] = got[g][k][
                            row : row + size, 0:r
                        ]
                        at += size

    for j in range(n_shard):
        every[:, r * j : r * (j + 1)] = held[j]
    qkv[...] = dot_nt(normed[...], every[0 : 3 * inner, :]).astype(low)
    for m in (1, 0):
        low_row = m * length
        for h in range(heads):
            at = DK * h
            keys = qkv[low_row : low_row + length, inner + at : inner + at + DK]
            values = qkv[low_row : low_row + length, 2 * inner + at : 2 * inner + at + DK]
            for b in range(n_ctx):
                top = low_row + b * rows
                scores = dot_nt(qkv[top : top + rows, at : at + DK], keys)
                scores += bias[h, b * rows : (b + 1) * rows, :]
                raised = jnp.exp(scores - jnp.max(scores, axis=-1, keepdims=True))
                share = raised / jnp.sum(raised, axis=-1, keepdims=True)
                if b == 0:
                    soft[m, h] = share
                mixed[top : top + rows, at : at + DK] = dot_nn(share.astype(low), values).astype(low)
        out = att_mine if m == 0 else att_other
        out[...] = dot_nn(
            mixed[low_row : low_row + length, :], every[3 * inner : 4 * inner, :]
        ).astype(low)


def middle_norm(n_ctx, idx, x_in, *refs):
    mine, (att, got, gains, normed, middle_own) = refs[: n_ctx - 1], refs[n_ctx - 1 :]
    rows = x_in.shape[1]
    for k in range(n_ctx):
        at = slice(k * rows, (k + 1) * rows)
        x = x_in[idx[2]] if k == 0 else mine[k - 1][...]
        mid = x.astype(wide) + (att[at, :].astype(wide) + got[at, :].astype(wide))
        scale = lax.rsqrt(jnp.mean(mid * mid, axis=-1, keepdims=True) + norm_eps)
        normed[at, :] = (mid * scale * gains[1:2, :]).astype(low)
        if k == 0:
            middle_own[...] = mid


def unpack_wide(parts, r, buf, weights, j):
    for e, pieces in enumerate(parts):
        for row, size, top, lane, lanes, at in pieces:
            weights[e][r * j + top : r * j + top + size, lane : lane + lanes] = buf[
                j, row : row + size, at : at + lanes
            ]


def feed_forward(n_ctx, n_shard, widths, idx, buf_far, nt_mine, nt_other, cot_in, *refs):
    half = idx[2]
    n_parts = len(widths)
    mine, rest, refs = refs[: n_ctx - 1], refs[n_ctx - 1], refs[n_ctx:]
    sent, given, refs = refs[0], refs[1 : 1 + 2 * n_parts], refs[1 + 2 * n_parts :]
    buf, nt, cot, sems, sems_out = refs[:5]
    weights, hidden, pair = (refs[5 + i * n_parts : 5 + (i + 1) * n_parts] for i in range(3))
    length, _ = nt_mine.shape
    rows = length // n_ctx
    r = weights[0].shape[0] // n_shard

    def block(m, k):
        at = (m * n_ctx + k) * rows
        return slice(at, at + rows)

    begun = [pltpu.make_async_copy(buf_far.at[0], buf.at[0], sems.at[0])]
    moves = [
        (nt_mine, nt.at[0:length, :]),
        (nt_other, nt.at[length : 2 * length, :]),
        (cot_in.at[half], cot.at[block(0, 0), :]),
        (cot_in.at[1 - half], cot.at[block(1, 0), :]),
    ]
    moves += [(buf_far.at[j], buf.at[j]) for j in range(1, n_shard)]
    for k in range(1, n_ctx):
        moves.append((mine[k - 1], cot.at[block(0, k), :]))
        moves.append((rest.at[k - 1], cot.at[block(1, k), :]))
    begun += [pltpu.make_async_copy(x, y, sems.at[i + 1]) for i, (x, y) in enumerate(moves)]
    for copy in begun:
        copy.start()
    loads = [begun[0]] + begun[5 : 4 + n_shard]
    parts, _ = wide_tiles(r, widths)
    for j in range(n_shard):
        loads[j].wait()
        unpack_wide(parts, r, buf, weights, j)
    for copy in begun[1:5] + begun[4 + n_shard :]:
        copy.wait()
    c0, c1 = 0.7978845608028654, 0.044715
    out = []

    def write(source, target):
        copy = pltpu.make_async_copy(source, target, sems_out.at[len(out)])
        copy.start()
        out.append(copy)

    for m in (1, 0):
        at = slice(m * length, (m + 1) * length)
        for e, n in enumerate(widths):
            both = dot_nn(nt[at, :], weights[e][:, 0 : 2 * n])
            back = dot_nn(cot[at, :], weights[e][:, 2 * n : 3 * n])
            gate, up = both[:, :n], both[:, n:]
            square = gate * gate
            bent = jnp.tanh(c0 * (gate + c1 * gate * square))
            half_one = 0.5 * (1.0 + bent)
            active = gate * half_one
            slope = half_one + 0.5 * gate * (1.0 - bent * bent) * (c0 * (1.0 + 3.0 * c1 * square))
            hidden[e][at, :] = (active * up).astype(low)
            pair[e][at, 0:n] = (back * up * slope).astype(low)
            pair[e][at, n : 2 * n] = (back * active).astype(low)
    for source, target in zip((*hidden, *pair), given, strict=True):
        write(source, target)
    for e, n in enumerate(widths):
        for_in = dot_tn(nt[...], pair[e][...]).astype(low)
        for_down = dot_tn(cot[...], hidden[e][...]).astype(low)
        first, last = parts[e][0][0], parts[e][-1][0] + parts[e][-1][1]
        for j in range(n_shard):
            for row, size, top, lane, lanes, at in parts[e]:
                top = r * j + top
                inside = max(0, min(lanes, 2 * n - lane))
                if inside:
                    buf[j, row : row + size, at : at + inside] = for_in[
                        top : top + size, lane : lane + inside
                    ]
                if inside < lanes:
                    begin = lane + inside - 2 * n
                    buf[j, row : row + size, at + inside : at + lanes] = for_down[
                        top : top + size, begin : begin + lanes - inside
                    ]
            here = slice(first, last if e < n_parts - 1 else buf.shape[1])
            write(buf.at[j, here, :], sent.at[j, here, :])
    for copy in out:
        copy.wait()


def feed_out(n_ctx, n_shard, widths, idx, buf_far, *refs):
    n_parts = len(widths)
    far, refs = refs[: 2 * n_parts], refs[2 * n_parts :]
    feed, two, refs = refs[0:2], refs[2:4], refs[4:]
    buf, feed_held, two_held, sems, sems_out = refs[:5]
    weights, hidden, pair = (refs[5 + i * n_parts : 5 + (i + 1) * n_parts] for i in range(3))
    _, _, rows, _ = two_held.shape
    length = n_ctx * rows
    r = weights[0].shape[0] // n_shard
    parts, _ = wide_tiles(r, widths)
    moves = [(buf_far.at[j], buf.at[j]) for j in range(n_shard)]
    moves += list(zip(far, (*hidden, *pair), strict=True))
    begun = [pltpu.make_async_copy(x, y, sems.at[i]) for i, (x, y) in enumerate(moves)]
    for copy in begun:
        copy.start()
    for j in range(n_shard):
        begun[j].wait()
        unpack_wide(parts, r, buf, weights, j)
    for copy in begun[n_shard:]:
        copy.wait()
    for held, given, lefts, first, last in (
        (two_held, two, pair, 0, 2),
        (feed_held, feed, hidden, 2, 3),
    ):

        def half_rows(m, _, held=held, lefts=lefts, first=first, last=last):
            at = pl.ds(pl.multiple_of(m * length, length), length)
            total = sum(
                (
                    dot_nt(lefts[e][at, :], weights[e][:, first * n : last * n])
                    for e, n in enumerate(widths)
                )
            )
            for i in range(n_ctx):
                held[m, i] = total[i * rows : (i + 1) * rows].astype(low)
            return 0

        lax.fori_loop(0, 2, half_rows, 0)
    copies = [
        pltpu.make_async_copy(held.at[m], given[m], sems_out.at[2 * i + m])
        for i, (held, given) in enumerate(((two_held, two), (feed_held, feed)))
        for m in range(2)
    ]
    for copy in copies:
        copy.start()
    for copy in copies:
        copy.wait()


def norm_two_back(n_shard, n_parts, idx, cot_in, *refs):
    parts, refs = refs[:n_parts], refs[n_parts:]
    middle, gains, out_in, grad, gain_grad = refs
    r = gain_grad.shape[2]
    mid = middle[...]
    two = sum((p[...].astype(wide) for p in parts))
    scale = lax.rsqrt(jnp.mean(mid * mid, axis=-1, keepdims=True) + norm_eps)
    u = two * gains[1:2, :]
    inner = jnp.mean(u * mid, axis=-1, keepdims=True) * (scale * scale * scale)
    back = cot_in[idx[2]].astype(wide) + scale * u - mid * inner
    grad[...] = back
    out_in[...] = back.astype(low)
    total = jnp.sum(two * mid * scale, axis=0, keepdims=True)
    for j in range(n_shard):
        gain_grad[j] = total[:, r * j : r * (j + 1)]


def attend_back(n_ctx, heads, idx, o_mine, o_other, soft, qkv, every, mixed, *refs):
    kv, for_out, (q_grad, kv_all, mixed_grad) = refs[:n_ctx], refs[n_ctx : 2 * n_ctx], refs[2 * n_ctx :]
    rows = o_mine.shape[0]
    length = n_ctx * rows
    inner = heads * DK
    share_rows = for_out[0].shape[0]
    for m, o_in in ((0, o_mine), (1, o_other)):
        top, own = m * length, m * rows
        mixed_grad[own : own + rows, :] = dot_nt(o_in[...], every[3 * inner :, :]).astype(low)
        for h in range(heads):
            at = DK * h
            share = soft[m, h]
            grad = mixed_grad[own : own + rows, at : at + DK]
            keys = qkv[top : top + length, inner + at : inner + at + DK]
            values = qkv[top : top + length, 2 * inner + at : 2 * inner + at + DK]
            queries = qkv[top : top + rows, at : at + DK]
            weight = dot_nt(grad, values)
            ds = share * (weight - jnp.sum(weight * share, axis=-1, keepdims=True))
            ds = ds.astype(low)
            q_grad[own : own + rows, at : at + DK] = dot_nn(ds, keys).astype(low)
            kv_all[top : top + length, at : at + DK] = dot_tn(ds, queries).astype(low)
            kv_all[top : top + length, inner + at : inner + at + DK] = dot_tn(
                share.astype(low), grad
            ).astype(low)
        for k in range(n_ctx):
            kv[k][own : own + rows, :] = kv_all[top + k * rows : top + (k + 1) * rows, :]
    got = dot_tn(mixed[0:rows, :], o_mine[...])
    got += dot_tn(mixed[length : length + rows, :], o_other[...])
    got = got.astype(low)
    for v in range(n_ctx):

        @pl.when(idx[1] == v)
        def _(v=v):
            for k in range(n_ctx):
                for_out[k][...] = got[(v ^ k) * share_rows : ((v ^ k) + 1) * share_rows, :]


def first_grad(n_ctx, idx, *refs):
    parts, (q_grad, every, out_mine, out_other), pieces, three = (
        refs[:n_ctx],
        refs[n_ctx : n_ctx + 4],
        refs[n_ctx + 4 : 2 * n_ctx + 4],
        refs[2 * n_ctx + 4],
    )
    rows2, inner = q_grad.shape
    rows = rows2 // 2
    size = inner // n_ctx
    three[:, 0:inner] = q_grad[...]
    three[:, inner:] = sum((p[...].astype(wide) for p in parts)).astype(low)
    for v in range(n_ctx):

        @pl.when(idx[1] == v)
        def _(v=v):
            for k in range(n_ctx):
                for i in range(3):
                    at = i * inner + (v ^ k) * size
                    pieces[k][:, i * size : (i + 1) * size] = three[:, at : at + size]

    got = dot_nn(three[...], every[0 : 3 * inner, :]).astype(low)
    out_mine[...] = got[0:rows]
    out_other[...] = got[rows:]


def weight_grads(n_ctx, n_shard, idx, normed, *refs):
    pieces, for_out, refs = refs[:n_ctx], refs[n_ctx : 2 * n_ctx], refs[2 * n_ctx :]
    gain_one, gain_two, stack, grads, held, sem = refs
    s = idx[0]
    copy = pltpu.make_async_copy(normed, held, sem)
    copy.start()
    size, r = for_out[0].shape[0], stack.shape[2]
    rows = pieces[0].shape[0] // 2
    out_rows = sum((p[...].astype(wide) for p in for_out))
    for j in range(n_shard):
        d = wrap(j - s, n_shard)
        stack[d, 3 * size : 4 * size, :] = out_rows[:, r * j : r * (j + 1)].astype(low)
        stack[d, 4 * size : 4 * size + 1, :] = gain_one[j].astype(low)
        stack[d, 4 * size + 1 : 4 * size + 2, :] = gain_two[j].astype(low)
    for m in range(2):
        for k in range(n_ctx):
            at = (m * n_ctx + k) * rows
            grads[at : at + rows, :] = pieces[k][m * rows : (m + 1) * rows, :]
    copy.wait()
    got = dot_tn(grads[...], held[...])
    for j in range(n_shard):
        stack[wrap(j - s, n_shard), 0 : 3 * size, :] = got[:, r * j : r * (j + 1)].astype(low)


def place_outputs(idx, a_mine, a_other, b_mine, b_other, a, b):
    half = idx[2]
    a[half] = a_mine[...]
    a[1 - half] = a_other[...]
    b[half] = b_mine[...]
    b[1 - half] = b_other[...]


def norm_one_back(n_shard, idx, x_in, mine, got, grad, gains, out, gain_grad):
    r = gain_grad.shape[2]
    x = x_in[idx[2]].astype(wide)
    one = mine[...].astype(wide) + got[...].astype(wide)
    scale = lax.rsqrt(jnp.mean(x * x, axis=-1, keepdims=True) + norm_eps)
    u = one * gains[0:1, :]
    inner = jnp.mean(u * x, axis=-1, keepdims=True) * (scale * scale * scale)
    out[...] = (grad[...] + scale * u - x * inner).astype(low)
    total = jnp.sum(one * x * scale, axis=0, keepdims=True)
    for j in range(n_shard):
        gain_grad[j] = total[:, r * j : r * (j + 1)]


def produce(n_parts, *refs):
    parts, (middle, out) = refs[:n_parts], refs[n_parts:]
    out[...] = (middle[...] + sum((p[...].astype(wide) for p in parts))).astype(low)


def finish_wide(period, widths, groups, idx, *refs):
    flat = [item for group in groups for item in group]
    count = sum((pieces for _, pieces, _ in flat))
    sources, refs = refs[:count], refs[count:]
    n_outs = 3
    outs, (stage, held, sems) = refs[-3 - n_outs : -3], refs[-3:]
    r = outs[0].shape[0]
    columns = sum(widths)
    parts, rows = wide_tiles(r, widths)
    c = idx[1]
    for v in range(period):

        @pl.when(lax.rem(c, period) == v)
        def _(v=v):
            first = 0
            copies = []
            for g, group in enumerate(groups):
                taken = []
                for k, pieces, lanes_kind in group:
                    begin = ((v ^ k) % period) * columns
                    tile_low = pl.cdiv(begin, LANES) * LANES - begin
                    tile_high = (begin + columns) // LANES * LANES - begin
                    if lanes_kind == "all":
                        low_lane, high_lane = 0, columns
                    elif lanes_kind == "full":
                        low_lane, high_lane = tile_low, tile_high
                    elif tile_low:
                        low_lane, high_lane = 0, tile_low
                    else:
                        low_lane, high_lane = tile_high, columns
                    taken.append((k, pieces, low_lane, high_lane, first))
                    first += pieces
                start = min((((v ^ k) % period) * columns + lo for k, _, lo, _, _ in taken))
                stop = max((((v ^ k) % period) * columns + hi for k, _, _, hi, _ in taken))
                far = (lax.div(c, period) ^ (group[0][0] // period)) * (period * columns) + start
                for k, pieces, low_lane, high_lane, at_source in taken:
                    size_each = rows // pieces
                    for i, n in enumerate(widths):
                        base = sum(widths[:i])
                        lo, hi = max(low_lane, base), min(high_lane, base + n)
                        if lo >= hi:
                            continue
                        for row, size, top, lane, lanes, at in parts[i]:
                            done = 0
                            while done < size:
                                part, here = divmod(row + done, size_each)
                                many = min(size - done, size_each - here)
                                stage[top + done : top + done + many, lane : lane + lanes] = (
                                    sources[at_source + part][
                                        here : here + many, at : at + lanes
                                    ].astype(wide)
                                )
                                done += many
                        to = ((v ^ k) % period) * columns + lo - start
                        for j in range(3):
                            held[g, j, :, to : to + hi - lo] = stage[
                                :, j * n + lo - base : j * n + hi - base
                            ]
                for j in range(3):
                    copy = pltpu.make_async_copy(
                        held.at[g, j, :, 0 : stop - start],
                        outs[j].at[:, pl.ds(pl.multiple_of(far, LANES), stop - start)],
                        sems.at[3 * g + j],
                    )
                    copy.start()
                    copies.append(copy)
            for copy in copies:
                copy.wait()


def finish_attention(n_ctx, idx, *refs):
    pieces, (outs, gains) = refs[:n_ctx], (refs[n_ctx:-1], refs[-1])
    inner, _ = outs[0].shape
    size = inner // n_ctx
    for v in range(n_ctx):

        @pl.when(idx[1] == v)
        def _(v=v):
            for k in range(n_ctx):
                at = (v ^ k) * size
                for i in range(4):
                    outs[i][at : at + size, :] = pieces[k][i * size : (i + 1) * size, :].astype(wide)

    gains[...] = sum((p[inner : inner + 2, :].astype(wide) for p in pieces))


def on_device(
    inputs,
    cotangent,
    norm1_gain,
    w_query,
    w_key,
    w_value,
    w_out,
    norm2_gain,
    w_gate,
    w_up,
    w_down,
    bias_table,
):
    _, rows, width = inputs.shape
    shards, ctx = lax.axis_size("shard"), lax.axis_size("ctx")
    inner, r = w_out.shape
    heads = inner // DK
    length = ctx * rows
    columns = w_gate.shape[1] // ctx
    first_width = pl.cdiv(columns, 2 * LANES) * LANES
    widths = (first_width, columns - first_width)
    lanes_r = pl.cdiv(r, LANES) * LANES
    s, c, half = lax.axis_index("shard"), lax.axis_index("ctx"), lax.axis_index("tensor")
    idx = jnp.stack([s, c, half]).astype(jnp.int32)
    attention_weights = (w_query.T, w_key.T, w_value.T, w_out)


    wide_rows = wide_tiles(r, widths)[1]
    period = next(p for p in range(1, ctx + 1) if p == ctx or p * columns % LANES == 0)
    window = max(
        pl.cdiv((v + 1) * columns, LANES) * LANES - v * columns // LANES * LANES
        for v in range(period)
    )
    (packed,) = run(
        functools.partial(pack_wide, period, widths, window),
        "pack_wide",
        [((wide_rows, LANES), low)],
        [w_gate, w_up, w_down.T],
        scalars=0,
        scratch=[
            pltpu.VMEM((3, r, window), low),
            pltpu.SemaphoreType.DMA((3,)),
        ],
        cost=2,
        far=3,
        vmem=60,
    )
    chunks = lax.all_gather(packed, "shard", axis=0, tiled=False)
    own_x = lax.dynamic_index_in_dim(inputs, half, 0, keepdims=False)
    (own_buf,) = run(
        functools.partial(pack_attention, ctx),
        "pack_attention",
        [((inner + 16, lanes_r), low)],
        [after(idx, packed), *attention_weights, jnp.stack([norm1_gain, norm2_gain])],
        scratch=[pltpu.VMEM((inner, r), low), pltpu.SemaphoreType.DMA],
        far=4,
        vmem=60,
    )
    if shards == 4:
        low_one, high_one = step(own_buf, "shard", 1), step(own_buf, "shard", -1)
        middle = own_buf.shape[0] // 2
        far = [step(low_one[:middle], "shard", 1), step(high_one[middle:], "shard", -1)]
        from_shard = [low_one, jnp.concatenate(far), high_one]
    else:
        from_shard = [step(own_buf, "shard", k) for k in range(1, shards)]
    mine_x = [swap(own_x, "ctx", k) for k in range(1, ctx)]
    table = lax.dynamic_slice_in_dim(bias_table, half * heads, heads, 1)
    (bias,) = run(
        functools.partial(bias_body, rows, rows // 5, distance_marks),
        "bias",
        [((heads, length, length), wide)],
        [after(idx, own_buf), table],
        scalars=2,
        cost=5,
    )
    now = after(idx, *from_shard, *mine_x, bias)

    group = jnp.concatenate(from_shard)
    buf_rows = inner + 16
    place = {z: [(0, (z - 1) * buf_rows, inner)] for z in range(1, shards)}
    gathered = [group] + [swap(after(group, now), "ctx", k) for k in range(1, ctx)]
    rest_x = swap(after(jnp.stack(mine_x), now), "tensor")
    normed_one, gains = run(
        functools.partial(norm_one, ctx, shards),
        "norm_one",
        [((2 * length, width), low), ((2, width), wide)],
        [now, inputs, *mine_x, rest_x, own_buf, *from_shard],
        scratch=[pltpu.VMEM((shards, 8, r), wide)],
        cost=3,
    )
    now = after(now, *gathered[1:], normed_one)

    own_cot = lax.dynamic_index_in_dim(cotangent, half, 0, keepdims=False)
    mine_cot = [swap(after(own_cot, now), "ctx", k) for k in range(1, ctx)]
    att_mine, att_other, soft, qkv, mixed, every = run(
        functools.partial(attend, ctx, shards, rows, heads, place),
        "attend",
        [
            ((length, width), low),
            ((length, width), low),
            ((2, heads, rows, length), wide),
            ((2 * length, 3 * inner), low),
            ((2 * length, inner), low),
            ((4 * inner, width), low),
        ],
        [now, normed_one, *attention_weights, bias, *gathered],
        scratch=[pltpu.VMEM((shards, 4 * inner, r), low)],
        cost=14,
        vmem=24,
    )
    now = after(now, *mine_cot, att_other)

    att_got = swap(after(att_other, now), "tensor")
    rest_cot = swap(after(jnp.stack(mine_cot), now), "tensor")
    nt_mine, middle_own = run(
        functools.partial(middle_norm, ctx),
        "middle_norm",
        [((length, width), low), ((rows, width), wide)],
        [now, inputs, *mine_x, att_mine, att_got, gains],
    )
    nt_other = swap(nt_mine, "tensor")
    now = after(now, nt_other, rest_cot)

    def add(a, b):
        return (a.astype(wide) + b.astype(wide)).astype(low)

    tokens_out = ((ctx, rows, width), low)
    units = [((2 * length, n), low) for n in (*widths, *(2 * n for n in widths))]
    unit_scratch = [pltpu.VMEM(shape, kind) for shape, kind in units]
    weight_scratch = [pltpu.VMEM((width, 3 * n), low) for n in widths]
    wide_grads, *units = run(
        functools.partial(feed_forward, ctx, shards, widths),
        "feed_forward",
        [((shards, wide_rows, LANES), low), *units],
        [now, chunks, nt_mine, nt_other, cotangent, *mine_cot, rest_cot],
        scratch=[
            pltpu.VMEM((shards, wide_rows, LANES), low),
            pltpu.VMEM((2 * length, width), low),
            pltpu.VMEM((2 * length, width), low),
            pltpu.SemaphoreType.DMA((3 + shards + 2 * ctx,)),
            pltpu.SemaphoreType.DMA(((2 + shards) * len(widths),)),
            *weight_scratch,
            *unit_scratch,
        ],
        far=5 + ctx - 1,
        far_out=True,
        cost=14,
        vmem=60,
    )
    wide_own = lax.psum_scatter(wide_grads, "shard", scatter_dimension=0, tiled=False)
    feed_mine, feed_other, two_mine, two_other = run(
        functools.partial(feed_out, ctx, shards, widths),
        "feed_out",
        [tokens_out] * 4,
        [now, chunks, *units],
        scratch=[
            pltpu.VMEM((shards, wide_rows, LANES), low),
            pltpu.VMEM((2, ctx, rows, width), low),
            pltpu.VMEM((2, ctx, rows, width), low),
            pltpu.SemaphoreType.DMA((shards + 2 * len(widths),)),
            pltpu.SemaphoreType.DMA((4,)),
            *weight_scratch,
            *unit_scratch,
        ],
        far=1 + 2 * len(widths),
        far_out=True,
        cost=5,
        vmem=60,
    )
    now = after(now, two_other)

    two_got = swap(after(two_other, now), "tensor")
    two_both = [add(two_mine[k], two_got[k]) for k in range(ctx)]
    two_parts = [two_both[0]] + [swap(two_both[k], "ctx", k) for k in range(1, ctx)]
    out_in, middle_grad, gain_two = run(
        functools.partial(norm_two_back, shards, ctx),
        "norm_two_back",
        [((rows, width), low), ((rows, width), wide), ((shards, 1, r), wide)],
        [now, cotangent, *two_parts, middle_own, gains],
    )
    out_in_other = swap(out_in, "tensor")
    now = after(now, out_in_other)

    feed_got = swap(after(feed_other, now), "tensor")
    got = run(
        functools.partial(attend_back, ctx, heads),
        "attend_back",
        [((2 * rows, 2 * inner), low)] * ctx
        + [((inner // ctx, width), low)] * ctx
        + [((2 * rows, inner), low)],
        [now, out_in, out_in_other, soft, qkv, every, mixed],
        scratch=[pltpu.VMEM((2 * length, 2 * inner), low), pltpu.VMEM((2 * rows, inner), low)],
        cost=4,
        vmem=24,
    )
    kv_parts, for_out, q_grad = got[:ctx], got[ctx : 2 * ctx], got[2 * ctx]
    now = after(now, feed_got, q_grad)

    kv_parts = [kv_parts[0]] + [swap(after(kv_parts[k], now), "ctx", k) for k in range(1, ctx)]
    for_out = [for_out[0]] + [swap(after(for_out[k], now), "ctx", k) for k in range(1, ctx)]
    got = run(
        functools.partial(first_grad, ctx),
        "first_grad",
        [((rows, width), low)] * 2 + [((2 * rows, 3 * inner // ctx), low)] * ctx,
        [now, *kv_parts, q_grad, every],
        scratch=[pltpu.VMEM((2 * rows, 3 * inner), low)],
    )
    first_mine, first_other, pieces = got[0], got[1], got[2:]
    now = after(now, first_other)

    pieces = [pieces[0]] + [swap(after(pieces[k], now), "ctx", k) for k in range(1, ctx)]
    first_got = swap(after(first_other, now), "tensor")
    input_mine, gain_one = run(
        functools.partial(norm_one_back, shards),
        "norm_one_back",
        [((rows, width), low), ((shards, 1, r), wide)],
        [now, inputs, first_mine, first_got, middle_grad, gains],
    )
    feed_both = [add(after(feed_mine, now)[k], feed_got[k]) for k in range(ctx)]
    feed_parts = [feed_both[0]] + [swap(feed_both[k], "ctx", k) for k in range(1, ctx)]
    now = after(now, *pieces[1:], *for_out[1:], *feed_parts[1:], input_mine)
    (four,) = run(
        functools.partial(weight_grads, ctx, shards),
        "weight_grads",
        [((shards, inner + 16, r), low)],
        [now, normed_one, *pieces, *for_out, gain_one, gain_two],
        scratch=[
            pltpu.VMEM((2 * length, 3 * inner // ctx), low),
            pltpu.VMEM((2 * length, width), low),
            pltpu.SemaphoreType.DMA,
        ],
        far=1,
        cost=2,
        vmem=24,
    )
    now = after(now, four, input_mine)

    (produced_mine,) = run(
        functools.partial(produce, ctx),
        "produce",
        [((rows, width), low)],
        [*feed_parts, middle_own],
        scalars=0,
    )
    input_other = swap(after(input_mine, now), "tensor")
    produced_other = swap(produced_mine, "tensor")
    now = after(now, wide_own, produced_other, input_other)

    wide_own = after(wide_own, now)
    half_rows = wide_rows // 2
    pair = ctx == 4
    wide_all = [swap(wide_own, "ctx", k) for k in ((1, 2) if pair else range(1, ctx))]
    four_shard = [four[0]] + [step(after(four[d], now), "shard", d) for d in range(1, shards)]
    out_y, out_x = run(
        place_outputs,
        "place_outputs",
        [(inputs.shape, low)] * 2,
        [now, produced_mine, produced_other, input_mine, input_other],
    )
    four_shard = [four[0]] + [after(part, out_y) for part in four_shard[1:]]
    four_own = sum((part.astype(wide) for part in four_shard)).astype(low)
    four_all = [four_own] + [swap(after(four_own, now), "ctx", k) for k in range(1, ctx)]
    now = after(now, *wide_all, *four_all[1:])

    far_halves = []
    if pair:
        far_halves = [
            swap(after(wide_all[0], now)[:half_rows], "ctx", 2),
            swap(after(wide_all[1], now)[half_rows:], "ctx", 1),
        ]
    out_q, out_k, out_v, out_o, own_gain = run(
        functools.partial(finish_attention, ctx),
        "finish_attention",
        [((inner, r), wide)] * 4 + [((2, r), wide)],
        [now, *four_all],
    )
    own_gain = own_gain + swap(own_gain, "tensor")

    pairs = pair and period <= 2
    period = 2 if pairs else ctx

    def finish(now, groups, sources, span, before):
        return run(
            functools.partial(finish_wide, period, widths, groups),
            "finish_wide",
            [(w_gate.shape, wide)] * 3,
            [now, *sources, *before],
            scratch=[
                pltpu.VMEM((r, 3 * max(widths)), wide),
                pltpu.VMEM((len(groups), 3, r, span), wide),
                pltpu.SemaphoreType.DMA((3 * len(groups),)),
            ],
            far_out=True,
            into=len(before),
            cost=3,
            vmem=24,
        )

    if pairs:
        groups = [[(0, 1, "all"), (1, 1, "all")], [(2, 1, "full")]]
        outs = finish(now, groups, [wide_own, *wide_all], 2 * columns, [])
        now = after(now, *far_halves, outs[0], own_gain)
        groups = [[(2, 1, "rest"), (3, 2, "all")]]
        outs = finish(now, groups, [wide_all[1], *far_halves], 2 * columns, outs)
    else:
        groups = [[(k, 1, "all") for k in range(ctx)]]
        outs = finish(now, groups, [wide_own, *wide_all], ctx * columns, [])
    out_g, out_u, out_d = outs

    return (
        out_y,
        out_x,
        own_gain[0],
        out_q.T,
        out_k.T,
        out_v.T,
        out_o,
        own_gain[1],
        out_g,
        out_u,
        out_d.T,
    )


def solution(mesh):
    placed = (
        P(None, ("shard", "ctx"), None),
        P(None, ("shard", "ctx"), None),
        P("shard"),
        P("shard", "tensor"),
        P("shard", "tensor"),
        P("shard", "tensor"),
        P("tensor", "shard"),
        P("shard"),
        P("shard", "tensor"),
        P("shard", "tensor"),
        P("tensor", "shard"),
        P(),
    )
    return jax.shard_map(
        on_device, mesh=mesh, in_specs=placed, out_specs=placed[:2] + placed[2:11], check_vma=False
    )
```

```python
import functools

import jax
import jax.numpy as jnp
from jax import lax
from jax.experimental import pallas as pl
from jax.experimental.pallas import tpu as pltpu
from jax.sharding import PartitionSpec as P

DK = 64
norm_eps = 1e-06
distance_marks = (8, 12, 16, 23, 32, 46, 64, 91)
masked_score = -1e30
low = jnp.bfloat16
wide = jnp.float32
LANES = 128
COST = 1e8


def dot_nn(left, right):
    return lax.dot_general(left, right, (((1,), (0,)), ((), ())), preferred_element_type=wide)


def dot_nt(left, right):
    return lax.dot_general(left, right, (((1,), (1,)), ((), ())), preferred_element_type=wide)


def dot_tn(left, right):
    return lax.dot_general(left, right, (((0,), (0,)), ((), ())), preferred_element_type=wide)


def wrap(value, n):
    return lax.rem(value + 2 * n, n)


def run(body, name, outs, operands, scratch=(), scalars=1, cost=1, far=0, far_out=False, into=0, vmem=16):
    return pl.pallas_call(
        body,
        name=name,
        out_shape=[jax.ShapeDtypeStruct(s, d) for s, d in outs],
        in_specs=[pl.BlockSpec(memory_space=pltpu.SMEM)] * scalars
        + [pl.BlockSpec(memory_space=pltpu.HBM)] * far
        + [pl.BlockSpec(memory_space=pltpu.VMEM)] * (len(operands) - scalars - far - into)
        + [pl.BlockSpec(memory_space=pltpu.HBM)] * into,
        out_specs=[pl.BlockSpec(memory_space=pltpu.HBM if far_out else pltpu.VMEM)] * len(outs),
        scratch_shapes=list(scratch),
        input_output_aliases={len(operands) - into + i: i for i in range(into)},
        compiler_params=pltpu.CompilerParams(vmem_limit_bytes=vmem * 2**20),
        cost_estimate=pl.CostEstimate(flops=int(cost * COST), bytes_accessed=0, transcendentals=0),
    )(*operands)


def step(x, axis, k=1):
    n = lax.axis_size(axis)
    return lax.ppermute(x, axis, [(i, (i + k) % n) for i in range(n)])


def swap(x, axis, k=1):
    n = lax.axis_size(axis)
    return lax.ppermute(x, axis, [(i, i ^ k) for i in range(n)])


def after(x, *others):
    return lax.optimization_barrier((x, *others))[0]


def pack_attention(n_ctx, idx, w_q, w_k, w_v, w_o, gain, buf, held, sem):
    inner, r = w_o.shape
    for v, ref in enumerate((w_q, w_k, w_v, w_o)):

        @pl.when(idx[1] == v)
        def _(ref=ref):
            copy = pltpu.make_async_copy(ref, held, sem)
            copy.start()
            copy.wait()

    buf[0:inner, 0:r] = held[...]

    buf[inner : inner + 2, 0:r] = gain[...]


def wide_tiles(r, widths):
    rp = pl.cdiv(r, 16) * 16
    row, parts = 0, []
    for n in widths:
        full, left = divmod(3 * n, LANES)
        pieces = [(row + rp * q, r, 0, LANES * q, LANES, 0) for q in range(full)]
        row += rp * full
        if left:
            assert 2 * left == LANES
            pieces.append((row, r // 2, 0, LANES * full, left, 0))
            pieces.append((row, r // 2, r // 2, LANES * full, left, left))
            row += pl.cdiv(r // 2, 8) * 8
        parts.append(pieces)
    return parts, pl.cdiv(row, 32) * 32


def pack_wide(period, widths, window, w_g, w_u, w_d, buf, held, sems):
    c = lax.axis_index("ctx")
    r = w_g.shape[0]
    columns = sum(widths)
    parts, _ = wide_tiles(r, widths)
    for v in range(period):

        @pl.when(lax.rem(c, period) == v)
        def _(v=v):
            start = v * columns // LANES * LANES
            far = lax.div(c, period) * (period * columns) + start
            here = pl.ds(pl.multiple_of(far, LANES), window)
            copies = [
                pltpu.make_async_copy(ref.at[:, here], held.at[i], sems.at[i])
                for i, ref in enumerate((w_g, w_u, w_d))
            ]
            for copy in copies:
                copy.start()
            for copy in copies:
                copy.wait()
            at = v * columns - start
            for n, pieces in zip(widths, parts, strict=True):
                for row, size, top, lane, lanes, to in pieces:
                    while lanes:
                        which, inside = divmod(lane, n)
                        take = min(lanes, n - inside)
                        buf[row : row + size, to : to + take] = held[
                            which, top : top + size, at + inside : at + inside + take
                        ]
                        lane, to, lanes = lane + take, to + take, lanes - take
                at += n


def bias_body(rows, seg_len, marks, idx, table, out):
    c = idx[1]
    heads, length, _ = out.shape

    def info(position):
        block = sum(((position >= rows * b).astype(jnp.int32) for b in range(1, length // rows)))
        token = (block ^ c) * rows + position - block * rows
        seg = sum(((token >= q * seg_len).astype(jnp.int32) for q in range(8, 20)))
        parent = jnp.where(seg == 0, -1, jnp.where(seg <= 4, 0, (seg - 3) >> 1))
        shift = jnp.where(seg == 0, 0, jnp.where(seg <= 4, seg - 1, seg - 2))
        return seg, parent, token - shift * seg_len

    key_seg, _, key_place = info(lax.broadcasted_iota(jnp.int32, (16, length), 1))

    def rows_of(i, _):
        at = pl.multiple_of(i * 16, 16)
        seg, parent, place = info(lax.broadcasted_iota(jnp.int32, (16, length), 0) + at)
        allowed = (key_seg == 0) | (key_seg == seg) | (key_seg == parent)
        relative = key_place - place
        magnitude = jnp.abs(relative)
        marked = sum(((magnitude >= mark).astype(jnp.int32) for mark in marks))
        bucket = jnp.where(relative > 0, 16, 0) + jnp.where(magnitude < 8, magnitude, 7 + marked)
        looked = [jnp.full(bucket.shape, table[0, h], wide) for h in range(heads)]
        for b in range(1, table.shape[0]):
            hit = bucket == b
            looked = [jnp.where(hit, table[b, h], looked[h]) for h in range(heads)]
        for h in range(heads):
            out[h, pl.ds(at, 16), :] = jnp.where(allowed, looked[h], masked_score)
        return 0

    lax.fori_loop(0, length // 16, rows_of, 0)


def tree_blocks(n_ctx, half, own, mine, rest):
    for k in range(n_ctx):
        yield 0, k, own[half] if k == 0 else mine[k - 1][...]
    for k in range(n_ctx):
        yield 1, k, own[1 - half] if k == 0 else rest[k - 1]


def norm_one(n_ctx, n_shard, idx, x_in, *refs):
    s, half = idx[0], idx[2]
    mine, rest = refs[: n_ctx - 1], refs[n_ctx - 1]
    bufs = refs[n_ctx : n_ctx + n_shard]
    normed, gains, held = refs[n_ctx + n_shard :]
    r = held.shape[2]
    _, rows, width = x_in.shape
    for k, buf in enumerate(bufs):
        at = buf.shape[0] - 16
        held[wrap(s - k, n_shard), 0:2, :] = buf[at : at + 2, 0:r].astype(wide)
    for j in range(n_shard):
        gains[:, r * j : r * (j + 1)] = held[j, 0:2, :]
    for m, k, x in tree_blocks(n_ctx, half, x_in, mine, rest):
        x = x.astype(wide)
        y = x * lax.rsqrt(jnp.mean(x * x, axis=-1, keepdims=True) + norm_eps)
        at = (m * n_ctx + k) * rows
        normed[at : at + rows, :] = (y * gains[0:1, :]).astype(low)


def attend(n_ctx, n_shard, rows, heads, place, idx, normed, w_q, w_k, w_v, w_o, bias, *refs):
    s, c = idx[0], idx[1]
    groups = 1 + max((g for pieces in place.values() for g, _, _ in pieces))
    got = [refs[g * n_ctx : (g + 1) * n_ctx] for g in range(groups)]
    att_mine, att_other, soft, qkv, mixed, every, held = refs[groups * n_ctx :]
    inner, r = w_o.shape
    length = n_ctx * rows
    for i, ref in enumerate((w_q, w_k, w_v, w_o)):
        held[s, i * inner : (i + 1) * inner, :] = ref[...]
    for v in range(n_ctx):

        @pl.when(c == v)
        def _(v=v):
            for k in range(n_ctx):
                for z, pieces in place.items():
                    at, last = (v ^ k) * inner, ((v ^ k) + 1) * inner
                    for g, row, size in pieces:
                        size = min(size, last - at)
                        held[wrap(s - z, n_shard), at : at + size, :] = got[g][k][
                            row : row + size, 0:r
                        ]
                        at += size

    for j in range(n_shard):
        every[:, r * j : r * (j + 1)] = held[j]
    qkv[...] = dot_nt(normed[...], every[0 : 3 * inner, :]).astype(low)
    for m in (1, 0):
        low_row = m * length
        for h in range(heads):
            at = DK * h
            keys = qkv[low_row : low_row + length, inner + at : inner + at + DK]
            values = qkv[low_row : low_row + length, 2 * inner + at : 2 * inner + at + DK]
            for b in range(n_ctx):
                top = low_row + b * rows
                scores = dot_nt(qkv[top : top + rows, at : at + DK], keys)
                scores += bias[h, b * rows : (b + 1) * rows, :]
                raised = jnp.exp(scores - jnp.max(scores, axis=-1, keepdims=True))
                share = raised / jnp.sum(raised, axis=-1, keepdims=True)
                if b == 0:
                    soft[m, h] = share
                mixed[top : top + rows, at : at + DK] = dot_nn(share.astype(low), values).astype(low)
        out = att_mine if m == 0 else att_other
        out[...] = dot_nn(
            mixed[low_row : low_row + length, :], every[3 * inner : 4 * inner, :]
        ).astype(low)


def middle_norm(n_ctx, idx, x_in, *refs):
    mine, (att, got, gains, normed, middle_own) = refs[: n_ctx - 1], refs[n_ctx - 1 :]
    rows = x_in.shape[1]
    for k in range(n_ctx):
        at = slice(k * rows, (k + 1) * rows)
        x = x_in[idx[2]] if k == 0 else mine[k - 1][...]
        mid = x.astype(wide) + (att[at, :].astype(wide) + got[at, :].astype(wide))
        scale = lax.rsqrt(jnp.mean(mid * mid, axis=-1, keepdims=True) + norm_eps)
        normed[at, :] = (mid * scale * gains[1:2, :]).astype(low)
        if k == 0:
            middle_own[...] = mid


def unpack_wide(parts, r, buf, weights, j):
    for e, pieces in enumerate(parts):
        for row, size, top, lane, lanes, at in pieces:
            weights[e][r * j + top : r * j + top + size, lane : lane + lanes] = buf[
                j, row : row + size, at : at + lanes
            ]


def feed_forward(n_ctx, n_shard, widths, idx, buf_far, nt_mine, nt_other, cot_in, *refs):
    half = idx[2]
    n_parts = len(widths)
    mine, rest, refs = refs[: n_ctx - 1], refs[n_ctx - 1], refs[n_ctx:]
    sent, given, refs = refs[0], refs[1 : 1 + 2 * n_parts], refs[1 + 2 * n_parts :]
    buf, nt, cot, sems, sems_out = refs[:5]
    weights, hidden, pair = (refs[5 + i * n_parts : 5 + (i + 1) * n_parts] for i in range(3))
    length, _ = nt_mine.shape
    rows = length // n_ctx
    r = weights[0].shape[0] // n_shard

    def block(m, k):
        at = (m * n_ctx + k) * rows
        return slice(at, at + rows)

    begun = [pltpu.make_async_copy(buf_far.at[0], buf.at[0], sems.at[0])]
    moves = [
        (nt_mine, nt.at[0:length, :]),
        (nt_other, nt.at[length : 2 * length, :]),
        (cot_in.at[half], cot.at[block(0, 0), :]),
        (cot_in.at[1 - half], cot.at[block(1, 0), :]),
    ]
    moves += [(buf_far.at[j], buf.at[j]) for j in range(1, n_shard)]
    for k in range(1, n_ctx):
        moves.append((mine[k - 1], cot.at[block(0, k), :]))
        moves.append((rest.at[k - 1], cot.at[block(1, k), :]))
    begun += [pltpu.make_async_copy(x, y, sems.at[i + 1]) for i, (x, y) in enumerate(moves)]
    for copy in begun:
        copy.start()
    loads = [begun[0]] + begun[5 : 4 + n_shard]
    parts, _ = wide_tiles(r, widths)
    for j in range(n_shard):
        loads[j].wait()
        unpack_wide(parts, r, buf, weights, j)
    for copy in begun[1:5] + begun[4 + n_shard :]:
        copy.wait()
    c0, c1 = 0.7978845608028654, 0.044715
    out = []

    def write(source, target):
        copy = pltpu.make_async_copy(source, target, sems_out.at[len(out)])
        copy.start()
        out.append(copy)

    for m in (1, 0):
        at = slice(m * length, (m + 1) * length)
        for e, n in enumerate(widths):
            both = dot_nn(nt[at, :], weights[e][:, 0 : 2 * n])
            back = dot_nn(cot[at, :], weights[e][:, 2 * n : 3 * n])
            gate, up = both[:, :n], both[:, n:]
            square = gate * gate
            bent = jnp.tanh(c0 * (gate + c1 * gate * square))
            half_one = 0.5 * (1.0 + bent)
            active = gate * half_one
            slope = half_one + 0.5 * gate * (1.0 - bent * bent) * (c0 * (1.0 + 3.0 * c1 * square))
            hidden[e][at, :] = (active * up).astype(low)
            pair[e][at, 0:n] = (back * up * slope).astype(low)
            pair[e][at, n : 2 * n] = (back * active).astype(low)
    for source, target in zip((*hidden, *pair), given, strict=True):
        write(source, target)
    for e, n in enumerate(widths):
        for_in = dot_tn(nt[...], pair[e][...]).astype(low)
        for_down = dot_tn(cot[...], hidden[e][...]).astype(low)
        first, last = parts[e][0][0], parts[e][-1][0] + parts[e][-1][1]
        for j in range(n_shard):
            for row, size, top, lane, lanes, at in parts[e]:
                top = r * j + top
                inside = max(0, min(lanes, 2 * n - lane))
                if inside:
                    buf[j, row : row + size, at : at + inside] = for_in[
                        top : top + size, lane : lane + inside
                    ]
                if inside < lanes:
                    begin = lane + inside - 2 * n
                    buf[j, row : row + size, at + inside : at + lanes] = for_down[
                        top : top + size, begin : begin + lanes - inside
                    ]
            here = slice(first, last if e < n_parts - 1 else buf.shape[1])
            write(buf.at[j, here, :], sent.at[j, here, :])
    for copy in out:
        copy.wait()


def feed_out(n_ctx, n_shard, widths, idx, buf_far, *refs):
    n_parts = len(widths)
    far, refs = refs[: 2 * n_parts], refs[2 * n_parts :]
    feed, two, refs = refs[0:2], refs[2:4], refs[4:]
    buf, feed_held, two_held, sems, sems_out = refs[:5]
    weights, hidden, pair = (refs[5 + i * n_parts : 5 + (i + 1) * n_parts] for i in range(3))
    _, _, rows, _ = two_held.shape
    length = n_ctx * rows
    r = weights[0].shape[0] // n_shard
    parts, _ = wide_tiles(r, widths)
    moves = [(buf_far.at[j], buf.at[j]) for j in range(n_shard)]
    moves += list(zip(far, (*hidden, *pair), strict=True))
    begun = [pltpu.make_async_copy(x, y, sems.at[i]) for i, (x, y) in enumerate(moves)]
    for copy in begun:
        copy.start()
    for j in range(n_shard):
        begun[j].wait()
        unpack_wide(parts, r, buf, weights, j)
    for copy in begun[n_shard:]:
        copy.wait()
    out = []
    for held, given, lefts, first, last in (
        (two_held, two, pair, 0, 2),
        (feed_held, feed, hidden, 2, 3),
    ):
        for m in (1, 0):
            at = slice(m * length, (m + 1) * length)
            total = sum(
                (
                    dot_nt(lefts[e][at, :], weights[e][:, first * n : last * n])
                    for e, n in enumerate(widths)
                )
            )
            for i in range(n_ctx):
                held[m, i] = total[i * rows : (i + 1) * rows].astype(low)
            copy = pltpu.make_async_copy(held.at[m], given[m], sems_out.at[len(out)])
            copy.start()
            out.append(copy)
    for copy in out:
        copy.wait()


def norm_two_back(n_shard, n_parts, idx, cot_in, *refs):
    parts, refs = refs[:n_parts], refs[n_parts:]
    middle, gains, out_in, grad, gain_grad = refs
    r = gain_grad.shape[2]
    mid = middle[...]
    two = sum((p[...].astype(wide) for p in parts))
    scale = lax.rsqrt(jnp.mean(mid * mid, axis=-1, keepdims=True) + norm_eps)
    u = two * gains[1:2, :]
    inner = jnp.mean(u * mid, axis=-1, keepdims=True) * (scale * scale * scale)
    back = cot_in[idx[2]].astype(wide) + scale * u - mid * inner
    grad[...] = back
    out_in[...] = back.astype(low)
    total = jnp.sum(two * mid * scale, axis=0, keepdims=True)
    for j in range(n_shard):
        gain_grad[j] = total[:, r * j : r * (j + 1)]


def attend_back(n_ctx, heads, idx, o_mine, o_other, soft, qkv, every, mixed, *refs):
    kv, for_out, (q_grad, kv_all, mixed_grad) = refs[:n_ctx], refs[n_ctx : 2 * n_ctx], refs[2 * n_ctx :]
    rows = o_mine.shape[0]
    length = n_ctx * rows
    inner = heads * DK
    share_rows = for_out[0].shape[0]
    for m, o_in in ((0, o_mine), (1, o_other)):
        top, own = m * length, m * rows
        mixed_grad[own : own + rows, :] = dot_nt(o_in[...], every[3 * inner :, :]).astype(low)
        for h in range(heads):
            at = DK * h
            share = soft[m, h]
            grad = mixed_grad[own : own + rows, at : at + DK]
            keys = qkv[top : top + length, inner + at : inner + at + DK]
            values = qkv[top : top + length, 2 * inner + at : 2 * inner + at + DK]
            queries = qkv[top : top + rows, at : at + DK]
            weight = dot_nt(grad, values)
            ds = share * (weight - jnp.sum(weight * share, axis=-1, keepdims=True))
            ds = ds.astype(low)
            q_grad[own : own + rows, at : at + DK] = dot_nn(ds, keys).astype(low)
            kv_all[top : top + length, at : at + DK] = dot_tn(ds, queries).astype(low)
            kv_all[top : top + length, inner + at : inner + at + DK] = dot_tn(
                share.astype(low), grad
            ).astype(low)
        for k in range(n_ctx):
            kv[k][own : own + rows, :] = kv_all[top + k * rows : top + (k + 1) * rows, :]
    got = dot_tn(mixed[0:rows, :], o_mine[...])
    got += dot_tn(mixed[length : length + rows, :], o_other[...])
    got = got.astype(low)
    for v in range(n_ctx):

        @pl.when(idx[1] == v)
        def _(v=v):
            for k in range(n_ctx):
                for_out[k][...] = got[(v ^ k) * share_rows : ((v ^ k) + 1) * share_rows, :]


def first_grad(n_ctx, idx, *refs):
    parts, (q_grad, every, out_mine, out_other), pieces, three = (
        refs[:n_ctx],
        refs[n_ctx : n_ctx + 4],
        refs[n_ctx + 4 : 2 * n_ctx + 4],
        refs[2 * n_ctx + 4],
    )
    rows2, inner = q_grad.shape
    rows = rows2 // 2
    size = inner // n_ctx
    three[:, 0:inner] = q_grad[...]
    three[:, inner:] = sum((p[...].astype(wide) for p in parts)).astype(low)
    for v in range(n_ctx):

        @pl.when(idx[1] == v)
        def _(v=v):
            for k in range(n_ctx):
                for i in range(3):
                    at = i * inner + (v ^ k) * size
                    pieces[k][:, i * size : (i + 1) * size] = three[:, at : at + size]

    got = dot_nn(three[...], every[0 : 3 * inner, :]).astype(low)
    out_mine[...] = got[0:rows]
    out_other[...] = got[rows:]


def weight_grads(n_ctx, n_shard, idx, normed, *refs):
    pieces, for_out, refs = refs[:n_ctx], refs[n_ctx : 2 * n_ctx], refs[2 * n_ctx :]
    gain_one, gain_two, stack, grads, held, sem = refs
    s = idx[0]
    copy = pltpu.make_async_copy(normed, held, sem)
    copy.start()
    size, r = for_out[0].shape[0], stack.shape[2]
    rows = pieces[0].shape[0] // 2
    out_rows = sum((p[...].astype(wide) for p in for_out))
    for j in range(n_shard):
        d = wrap(j - s, n_shard)
        stack[d, 3 * size : 4 * size, :] = out_rows[:, r * j : r * (j + 1)].astype(low)
        stack[d, 4 * size : 4 * size + 1, :] = gain_one[j].astype(low)
        stack[d, 4 * size + 1 : 4 * size + 2, :] = gain_two[j].astype(low)
    for m in range(2):
        for k in range(n_ctx):
            at = (m * n_ctx + k) * rows
            grads[at : at + rows, :] = pieces[k][m * rows : (m + 1) * rows, :]
    copy.wait()
    got = dot_tn(grads[...], held[...])
    for j in range(n_shard):
        stack[wrap(j - s, n_shard), 0 : 3 * size, :] = got[:, r * j : r * (j + 1)].astype(low)


def place_outputs(idx, a_mine, a_other, b_mine, b_other, a, b):
    half = idx[2]
    a[half] = a_mine[...]
    a[1 - half] = a_other[...]
    b[half] = b_mine[...]
    b[1 - half] = b_other[...]


def norm_one_back(n_shard, idx, x_in, mine, got, grad, gains, out, gain_grad):
    r = gain_grad.shape[2]
    x = x_in[idx[2]].astype(wide)
    one = mine[...].astype(wide) + got[...].astype(wide)
    scale = lax.rsqrt(jnp.mean(x * x, axis=-1, keepdims=True) + norm_eps)
    u = one * gains[0:1, :]
    inner = jnp.mean(u * x, axis=-1, keepdims=True) * (scale * scale * scale)
    out[...] = (grad[...] + scale * u - x * inner).astype(low)
    total = jnp.sum(one * x * scale, axis=0, keepdims=True)
    for j in range(n_shard):
        gain_grad[j] = total[:, r * j : r * (j + 1)]


def produce(n_parts, *refs):
    parts, (middle, out) = refs[:n_parts], refs[n_parts:]
    out[...] = (middle[...] + sum((p[...].astype(wide) for p in parts))).astype(low)


def finish_wide(period, widths, groups, idx, *refs):
    flat = [item for group in groups for item in group]
    count = sum((pieces for _, pieces, _ in flat))
    sources, refs = refs[:count], refs[count:]
    n_outs = 3
    outs, (stage, held, sems) = refs[-3 - n_outs : -3], refs[-3:]
    r = outs[0].shape[0]
    columns = sum(widths)
    parts, rows = wide_tiles(r, widths)
    c = idx[1]
    for v in range(period):

        @pl.when(lax.rem(c, period) == v)
        def _(v=v):
            first = 0
            copies = []
            for g, group in enumerate(groups):
                taken = []
                for k, pieces, lanes_kind in group:
                    begin = ((v ^ k) % period) * columns
                    tile_low = pl.cdiv(begin, LANES) * LANES - begin
                    tile_high = (begin + columns) // LANES * LANES - begin
                    if lanes_kind == "all":
                        low_lane, high_lane = 0, columns
                    elif lanes_kind == "full":
                        low_lane, high_lane = tile_low, tile_high
                    elif tile_low:
                        low_lane, high_lane = 0, tile_low
                    else:
                        low_lane, high_lane = tile_high, columns
                    taken.append((k, pieces, low_lane, high_lane, first))
                    first += pieces
                start = min((((v ^ k) % period) * columns + lo for k, _, lo, _, _ in taken))
                stop = max((((v ^ k) % period) * columns + hi for k, _, _, hi, _ in taken))
                far = (lax.div(c, period) ^ (group[0][0] // period)) * (period * columns) + start
                for k, pieces, low_lane, high_lane, at_source in taken:
                    size_each = rows // pieces
                    for i, n in enumerate(widths):
                        base = sum(widths[:i])
                        lo, hi = max(low_lane, base), min(high_lane, base + n)
                        if lo >= hi:
                            continue
                        for row, size, top, lane, lanes, at in parts[i]:
                            done = 0
                            while done < size:
                                part, here = divmod(row + done, size_each)
                                many = min(size - done, size_each - here)
                                stage[top + done : top + done + many, lane : lane + lanes] = (
                                    sources[at_source + part][
                                        here : here + many, at : at + lanes
                                    ].astype(wide)
                                )
                                done += many
                        to = ((v ^ k) % period) * columns + lo - start
                        for j in range(3):
                            held[g, j, :, to : to + hi - lo] = stage[
                                :, j * n + lo - base : j * n + hi - base
                            ]
                for j in range(3):
                    copy = pltpu.make_async_copy(
                        held.at[g, j, :, 0 : stop - start],
                        outs[j].at[:, pl.ds(pl.multiple_of(far, LANES), stop - start)],
                        sems.at[3 * g + j],
                    )
                    copy.start()
                    copies.append(copy)
            for copy in copies:
                copy.wait()


def finish_attention(n_ctx, idx, *refs):
    pieces, (outs, gains) = refs[:n_ctx], (refs[n_ctx:-1], refs[-1])
    inner, _ = outs[0].shape
    size = inner // n_ctx
    for v in range(n_ctx):

        @pl.when(idx[1] == v)
        def _(v=v):
            for k in range(n_ctx):
                at = (v ^ k) * size
                for i in range(4):
                    outs[i][at : at + size, :] = pieces[k][i * size : (i + 1) * size, :].astype(wide)

    gains[...] = sum((p[inner : inner + 2, :].astype(wide) for p in pieces))


def on_device(
    inputs,
    cotangent,
    norm1_gain,
    w_query,
    w_key,
    w_value,
    w_out,
    norm2_gain,
    w_gate,
    w_up,
    w_down,
    bias_table,
):
    _, rows, width = inputs.shape
    shards, ctx = lax.axis_size("shard"), lax.axis_size("ctx")
    inner, r = w_out.shape
    heads = inner // DK
    length = ctx * rows
    columns = w_gate.shape[1] // ctx
    first_width = pl.cdiv(columns, 2 * LANES) * LANES
    widths = (first_width, columns - first_width)
    lanes_r = pl.cdiv(r, LANES) * LANES
    s, c, half = lax.axis_index("shard"), lax.axis_index("ctx"), lax.axis_index("tensor")
    idx = jnp.stack([s, c, half]).astype(jnp.int32)
    attention_weights = (w_query.T, w_key.T, w_value.T, w_out)


    wide_rows = wide_tiles(r, widths)[1]
    period = next(p for p in range(1, ctx + 1) if p == ctx or p * columns % LANES == 0)
    window = max(
        pl.cdiv((v + 1) * columns, LANES) * LANES - v * columns // LANES * LANES
        for v in range(period)
    )
    (packed,) = run(
        functools.partial(pack_wide, period, widths, window),
        "pack_wide",
        [((wide_rows, LANES), low)],
        [w_gate, w_up, w_down.T],
        scalars=0,
        scratch=[
            pltpu.VMEM((3, r, window), low),
            pltpu.SemaphoreType.DMA((3,)),
        ],
        cost=2,
        far=3,
        vmem=60,
    )
    chunks = lax.all_gather(packed, "shard", axis=0, tiled=False)
    own_x = lax.dynamic_index_in_dim(inputs, half, 0, keepdims=False)
    (own_buf,) = run(
        functools.partial(pack_attention, ctx),
        "pack_attention",
        [((inner + 16, lanes_r), low)],
        [after(idx, packed), *attention_weights, jnp.stack([norm1_gain, norm2_gain])],
        scratch=[pltpu.VMEM((inner, r), low), pltpu.SemaphoreType.DMA],
        far=4,
        vmem=60,
    )
    if shards == 4:
        low_one, high_one = step(own_buf, "shard", 1), step(own_buf, "shard", -1)
        middle = own_buf.shape[0] // 2
        far = [step(low_one[:middle], "shard", 1), step(high_one[middle:], "shard", -1)]
        from_shard = [low_one, jnp.concatenate(far), high_one]
    else:
        from_shard = [step(own_buf, "shard", k) for k in range(1, shards)]
    table = lax.dynamic_slice_in_dim(bias_table, half * heads, heads, 1)
    (bias,) = run(
        functools.partial(bias_body, rows, rows // 5, distance_marks),
        "bias",
        [((heads, length, length), wide)],
        [after(idx, own_buf), table],
        scalars=2,
        cost=5,
    )
    mine_x = [swap(after(own_x, bias), "ctx", k) for k in range(1, ctx)]
    now = after(idx, *from_shard, *mine_x, bias)

    group = jnp.concatenate(from_shard)
    buf_rows = inner + 16
    place = {z: [(0, (z - 1) * buf_rows, inner)] for z in range(1, shards)}
    gathered = [group] + [swap(after(group, now), "ctx", k) for k in range(1, ctx)]
    rest_x = swap(after(jnp.stack(mine_x), now), "tensor")
    normed_one, gains = run(
        functools.partial(norm_one, ctx, shards),
        "norm_one",
        [((2 * length, width), low), ((2, width), wide)],
        [now, inputs, *mine_x, rest_x, own_buf, *from_shard],
        scratch=[pltpu.VMEM((shards, 8, r), wide)],
        cost=3,
    )
    now = after(now, *gathered[1:], normed_one)

    own_cot = lax.dynamic_index_in_dim(cotangent, half, 0, keepdims=False)
    mine_cot = [swap(after(own_cot, now), "ctx", k) for k in range(1, ctx)]
    att_mine, att_other, soft, qkv, mixed, every = run(
        functools.partial(attend, ctx, shards, rows, heads, place),
        "attend",
        [
            ((length, width), low),
            ((length, width), low),
            ((2, heads, rows, length), wide),
            ((2 * length, 3 * inner), low),
            ((2 * length, inner), low),
            ((4 * inner, width), low),
        ],
        [now, normed_one, *attention_weights, bias, *gathered],
        scratch=[pltpu.VMEM((shards, 4 * inner, r), low)],
        cost=14,
        vmem=24,
    )
    now = after(now, *mine_cot, att_other)

    att_got = swap(after(att_other, now), "tensor")
    rest_cot = swap(after(jnp.stack(mine_cot), now), "tensor")
    nt_mine, middle_own = run(
        functools.partial(middle_norm, ctx),
        "middle_norm",
        [((length, width), low), ((rows, width), wide)],
        [now, inputs, *mine_x, att_mine, att_got, gains],
    )
    nt_other = swap(nt_mine, "tensor")
    now = after(now, nt_other, rest_cot)

    def add(a, b):
        return (a.astype(wide) + b.astype(wide)).astype(low)

    tokens_out = ((ctx, rows, width), low)
    units = [((2 * length, n), low) for n in (*widths, *(2 * n for n in widths))]
    unit_scratch = [pltpu.VMEM(shape, kind) for shape, kind in units]
    weight_scratch = [pltpu.VMEM((width, 3 * n), low) for n in widths]
    wide_grads, *units = run(
        functools.partial(feed_forward, ctx, shards, widths),
        "feed_forward",
        [((shards, wide_rows, LANES), low), *units],
        [now, chunks, nt_mine, nt_other, cotangent, *mine_cot, rest_cot],
        scratch=[
            pltpu.VMEM((shards, wide_rows, LANES), low),
            pltpu.VMEM((2 * length, width), low),
            pltpu.VMEM((2 * length, width), low),
            pltpu.SemaphoreType.DMA((3 + shards + 2 * ctx,)),
            pltpu.SemaphoreType.DMA(((2 + shards) * len(widths),)),
            *weight_scratch,
            *unit_scratch,
        ],
        far=5 + ctx - 1,
        far_out=True,
        cost=14,
        vmem=60,
    )
    wide_own = lax.psum_scatter(wide_grads, "shard", scatter_dimension=0, tiled=False)
    feed_mine, feed_other, two_mine, two_other = run(
        functools.partial(feed_out, ctx, shards, widths),
        "feed_out",
        [tokens_out] * 4,
        [now, chunks, *units],
        scratch=[
            pltpu.VMEM((shards, wide_rows, LANES), low),
            pltpu.VMEM((2, ctx, rows, width), low),
            pltpu.VMEM((2, ctx, rows, width), low),
            pltpu.SemaphoreType.DMA((shards + 2 * len(widths),)),
            pltpu.SemaphoreType.DMA((4,)),
            *weight_scratch,
            *unit_scratch,
        ],
        far=1 + 2 * len(widths),
        far_out=True,
        cost=5,
        vmem=60,
    )
    now = after(now, two_other)

    two_got = swap(after(two_other, now), "tensor")
    two_both = [add(two_mine[k], two_got[k]) for k in range(ctx)]
    two_parts = [two_both[0]] + [swap(two_both[k], "ctx", k) for k in range(1, ctx)]
    out_in, middle_grad, gain_two = run(
        functools.partial(norm_two_back, shards, ctx),
        "norm_two_back",
        [((rows, width), low), ((rows, width), wide), ((shards, 1, r), wide)],
        [now, cotangent, *two_parts, middle_own, gains],
    )
    out_in_other = swap(out_in, "tensor")
    now = after(now, out_in_other)

    feed_got = swap(after(feed_other, now), "tensor")
    got = run(
        functools.partial(attend_back, ctx, heads),
        "attend_back",
        [((2 * rows, 2 * inner), low)] * ctx
        + [((inner // ctx, width), low)] * ctx
        + [((2 * rows, inner), low)],
        [now, out_in, out_in_other, soft, qkv, every, mixed],
        scratch=[pltpu.VMEM((2 * length, 2 * inner), low), pltpu.VMEM((2 * rows, inner), low)],
        cost=4,
        vmem=24,
    )
    kv_parts, for_out, q_grad = got[:ctx], got[ctx : 2 * ctx], got[2 * ctx]
    now = after(now, feed_got, q_grad)

    kv_parts = [kv_parts[0]] + [swap(after(kv_parts[k], now), "ctx", k) for k in range(1, ctx)]
    for_out = [for_out[0]] + [swap(after(for_out[k], now), "ctx", k) for k in range(1, ctx)]
    got = run(
        functools.partial(first_grad, ctx),
        "first_grad",
        [((rows, width), low)] * 2 + [((2 * rows, 3 * inner // ctx), low)] * ctx,
        [now, *kv_parts, q_grad, every],
        scratch=[pltpu.VMEM((2 * rows, 3 * inner), low)],
    )
    first_mine, first_other, pieces = got[0], got[1], got[2:]
    now = after(now, first_other)

    pieces = [pieces[0]] + [swap(after(pieces[k], now), "ctx", k) for k in range(1, ctx)]
    first_got = swap(after(first_other, now), "tensor")
    input_mine, gain_one = run(
        functools.partial(norm_one_back, shards),
        "norm_one_back",
        [((rows, width), low), ((shards, 1, r), wide)],
        [now, inputs, first_mine, first_got, middle_grad, gains],
    )
    feed_both = [add(after(feed_mine, now)[k], feed_got[k]) for k in range(ctx)]
    feed_parts = [feed_both[0]] + [swap(feed_both[k], "ctx", k) for k in range(1, ctx)]
    now = after(now, *pieces[1:], *for_out[1:], *feed_parts[1:], input_mine)
    (four,) = run(
        functools.partial(weight_grads, ctx, shards),
        "weight_grads",
        [((shards, inner + 16, r), low)],
        [now, normed_one, *pieces, *for_out, gain_one, gain_two],
        scratch=[
            pltpu.VMEM((2 * length, 3 * inner // ctx), low),
            pltpu.VMEM((2 * length, width), low),
            pltpu.SemaphoreType.DMA,
        ],
        far=1,
        cost=2,
        vmem=24,
    )
    now = after(now, four, input_mine)

    (produced_mine,) = run(
        functools.partial(produce, ctx),
        "produce",
        [((rows, width), low)],
        [*feed_parts, middle_own],
        scalars=0,
    )
    now = after(now, wide_own, produced_mine, input_mine)

    wide_own = after(wide_own, now)
    half_rows = wide_rows // 2
    pair = ctx == 4
    wide_all = [swap(wide_own, "ctx", k) for k in ((1, 2) if pair else range(1, ctx))]
    four_shard = [four[0]] + [step(after(four[d], now), "shard", d) for d in range(1, shards)]
    input_other = swap(after(input_mine, now), "tensor")
    produced_other = swap(after(produced_mine, now), "tensor")
    out_y, out_x = run(
        place_outputs,
        "place_outputs",
        [(inputs.shape, low)] * 2,
        [now, produced_mine, produced_other, input_mine, input_other],
    )
    four_shard = [four[0]] + [after(part, out_y) for part in four_shard[1:]]
    four_own = sum((part.astype(wide) for part in four_shard)).astype(low)
    four_all = [four_own] + [swap(after(four_own, now), "ctx", k) for k in range(1, ctx)]
    now = after(now, *wide_all, *four_all[1:])

    far_halves = []
    if pair:
        far_halves = [
            swap(after(wide_all[0], now)[:half_rows], "ctx", 2),
            swap(after(wide_all[1], now)[half_rows:], "ctx", 1),
        ]
    out_q, out_k, out_v, out_o, own_gain = run(
        functools.partial(finish_attention, ctx),
        "finish_attention",
        [((inner, r), wide)] * 4 + [((2, r), wide)],
        [now, *four_all],
    )
    own_gain = own_gain + swap(own_gain, "tensor")

    pairs = pair and period <= 2
    period = 2 if pairs else ctx

    def finish(now, groups, sources, span, before):
        return run(
            functools.partial(finish_wide, period, widths, groups),
            "finish_wide",
            [(w_gate.shape, wide)] * 3,
            [now, *sources, *before],
            scratch=[
                pltpu.VMEM((r, 3 * max(widths)), wide),
                pltpu.VMEM((len(groups), 3, r, span), wide),
                pltpu.SemaphoreType.DMA((3 * len(groups),)),
            ],
            far_out=True,
            into=len(before),
            cost=3,
            vmem=24,
        )

    if pairs:
        groups = [[(0, 1, "all"), (1, 1, "all")], [(2, 1, "full")]]
        outs = finish(now, groups, [wide_own, *wide_all], 2 * columns, [])
        now = after(now, *far_halves, outs[0], own_gain)
        groups = [[(2, 1, "rest"), (3, 2, "all")]]
        outs = finish(now, groups, [wide_all[1], *far_halves], 2 * columns, outs)
    else:
        groups = [[(k, 1, "all") for k in range(ctx)]]
        outs = finish(now, groups, [wide_own, *wide_all], ctx * columns, [])
    out_g, out_u, out_d = outs

    return (
        out_y,
        out_x,
        own_gain[0],
        out_q.T,
        out_k.T,
        out_v.T,
        out_o,
        own_gain[1],
        out_g,
        out_u,
        out_d.T,
    )


def solution(mesh):
    placed = (
        P(None, ("shard", "ctx"), None),
        P(None, ("shard", "ctx"), None),
        P("shard"),
        P("shard", "tensor"),
        P("shard", "tensor"),
        P("shard", "tensor"),
        P("tensor", "shard"),
        P("shard"),
        P("shard", "tensor"),
        P("shard", "tensor"),
        P("tensor", "shard"),
        P(),
    )
    return jax.shard_map(
        on_device, mesh=mesh, in_specs=placed, out_specs=placed[:2] + placed[2:11], check_vma=False
    )
```

```python
import functools

import jax
import jax.numpy as jnp
from jax import lax
from jax.experimental import pallas as pl
from jax.experimental.pallas import tpu as pltpu
from jax.sharding import PartitionSpec as P

DK = 64
norm_eps = 1e-06
distance_marks = (8, 12, 16, 23, 32, 46, 64, 91)
masked_score = -1e30
low = jnp.bfloat16
wide = jnp.float32
LANES = 128
COST = 1e8


def dot_nn(left, right):
    return lax.dot_general(left, right, (((1,), (0,)), ((), ())), preferred_element_type=wide)


def dot_nt(left, right):
    return lax.dot_general(left, right, (((1,), (1,)), ((), ())), preferred_element_type=wide)


def dot_tn(left, right):
    return lax.dot_general(left, right, (((0,), (0,)), ((), ())), preferred_element_type=wide)


def wrap(value, n):
    return lax.rem(value + 2 * n, n)


def run(body, name, outs, operands, scratch=(), scalars=1, cost=1, far=0, far_out=False, into=0, vmem=16):
    return pl.pallas_call(
        body,
        name=name,
        out_shape=[jax.ShapeDtypeStruct(s, d) for s, d in outs],
        in_specs=[pl.BlockSpec(memory_space=pltpu.SMEM)] * scalars
        + [pl.BlockSpec(memory_space=pltpu.HBM)] * far
        + [pl.BlockSpec(memory_space=pltpu.VMEM)] * (len(operands) - scalars - far - into)
        + [pl.BlockSpec(memory_space=pltpu.HBM)] * into,
        out_specs=[pl.BlockSpec(memory_space=pltpu.HBM if far_out else pltpu.VMEM)] * len(outs),
        scratch_shapes=list(scratch),
        input_output_aliases={len(operands) - into + i: i for i in range(into)},
        compiler_params=pltpu.CompilerParams(vmem_limit_bytes=vmem * 2**20),
        cost_estimate=pl.CostEstimate(flops=int(cost * COST), bytes_accessed=0, transcendentals=0),
    )(*operands)


def step(x, axis, k=1):
    n = lax.axis_size(axis)
    return lax.ppermute(x, axis, [(i, (i + k) % n) for i in range(n)])


def swap(x, axis, k=1):
    n = lax.axis_size(axis)
    return lax.ppermute(x, axis, [(i, i ^ k) for i in range(n)])


def after(x, *others):
    return lax.optimization_barrier((x, *others))[0]


def pack_attention(n_ctx, idx, w_q, w_k, w_v, w_o, gain, buf, held, sem):
    inner, r = w_o.shape
    for v, ref in enumerate((w_q, w_k, w_v, w_o)):

        @pl.when(idx[1] == v)
        def _(ref=ref):
            copy = pltpu.make_async_copy(ref, held, sem)
            copy.start()
            copy.wait()

    buf[0:inner, 0:r] = held[...]

    buf[inner : inner + 2, 0:r] = gain[...]


def wide_tiles(r, widths):
    rp = pl.cdiv(r, 16) * 16
    row, parts = 0, []
    for n in widths:
        full, left = divmod(3 * n, LANES)
        pieces = [(row + rp * q, r, 0, LANES * q, LANES, 0) for q in range(full)]
        row += rp * full
        if left:
            assert 2 * left == LANES
            pieces.append((row, r // 2, 0, LANES * full, left, 0))
            pieces.append((row, r // 2, r // 2, LANES * full, left, left))
            row += pl.cdiv(r // 2, 8) * 8
        parts.append(pieces)
    return parts, pl.cdiv(row, 32) * 32


def pack_wide(period, widths, window, w_g, w_u, w_d, buf, held, sems):
    c = lax.axis_index("ctx")
    r = w_g.shape[0]
    columns = sum(widths)
    parts, _ = wide_tiles(r, widths)
    for v in range(period):

        @pl.when(lax.rem(c, period) == v)
        def _(v=v):
            start = v * columns // LANES * LANES
            far = lax.div(c, period) * (period * columns) + start
            here = pl.ds(pl.multiple_of(far, LANES), window)
            copies = [
                pltpu.make_async_copy(ref.at[:, here], held.at[i], sems.at[i])
                for i, ref in enumerate((w_g, w_u, w_d))
            ]
            for copy in copies:
                copy.start()
            for copy in copies:
                copy.wait()
            at = v * columns - start
            for n, pieces in zip(widths, parts, strict=True):
                for row, size, top, lane, lanes, to in pieces:
                    while lanes:
                        which, inside = divmod(lane, n)
                        take = min(lanes, n - inside)
                        buf[row : row + size, to : to + take] = held[
                            which, top : top + size, at + inside : at + inside + take
                        ]
                        lane, to, lanes = lane + take, to + take, lanes - take
                at += n


def bias_body(rows, seg_len, marks, idx, table, out):
    c = idx[1]
    heads, length, _ = out.shape

    def info(position):
        block = sum(((position >= rows * b).astype(jnp.int32) for b in range(1, length // rows)))
        token = (block ^ c) * rows + position - block * rows
        seg = sum(((token >= q * seg_len).astype(jnp.int32) for q in range(8, 20)))
        parent = jnp.where(seg == 0, -1, jnp.where(seg <= 4, 0, (seg - 3) >> 1))
        shift = jnp.where(seg == 0, 0, jnp.where(seg <= 4, seg - 1, seg - 2))
        return seg, parent, token - shift * seg_len

    key_seg, _, key_place = info(lax.broadcasted_iota(jnp.int32, (16, length), 1))

    def rows_of(i, _):
        at = pl.multiple_of(i * 16, 16)
        seg, parent, place = info(lax.broadcasted_iota(jnp.int32, (16, length), 0) + at)
        allowed = (key_seg == 0) | (key_seg == seg) | (key_seg == parent)
        relative = key_place - place
        magnitude = jnp.abs(relative)
        marked = sum(((magnitude >= mark).astype(jnp.int32) for mark in marks))
        bucket = jnp.where(relative > 0, 16, 0) + jnp.where(magnitude < 8, magnitude, 7 + marked)
        looked = [jnp.full(bucket.shape, table[0, h], wide) for h in range(heads)]
        for b in range(1, table.shape[0]):
            hit = bucket == b
            looked = [jnp.where(hit, table[b, h], looked[h]) for h in range(heads)]
        for h in range(heads):
            out[h, pl.ds(at, 16), :] = jnp.where(allowed, looked[h], masked_score)
        return 0

    lax.fori_loop(0, length // 16, rows_of, 0)


def tree_blocks(n_ctx, half, own, mine, rest):
    for k in range(n_ctx):
        yield 0, k, own[half] if k == 0 else mine[k - 1][...]
    for k in range(n_ctx):
        yield 1, k, own[1 - half] if k == 0 else rest[k - 1]


def norm_one(n_ctx, n_shard, idx, x_in, *refs):
    s, half = idx[0], idx[2]
    mine, rest = refs[: n_ctx - 1], refs[n_ctx - 1]
    bufs = refs[n_ctx : n_ctx + n_shard]
    normed, gains, held = refs[n_ctx + n_shard :]
    r = held.shape[2]
    _, rows, width = x_in.shape
    for k, buf in enumerate(bufs):
        at = buf.shape[0] - 16
        held[wrap(s - k, n_shard), 0:2, :] = buf[at : at + 2, 0:r].astype(wide)
    for j in range(n_shard):
        gains[:, r * j : r * (j + 1)] = held[j, 0:2, :]
    for m, k, x in tree_blocks(n_ctx, half, x_in, mine, rest):
        x = x.astype(wide)
        y = x * lax.rsqrt(jnp.mean(x * x, axis=-1, keepdims=True) + norm_eps)
        at = (m * n_ctx + k) * rows
        normed[at : at + rows, :] = (y * gains[0:1, :]).astype(low)


def attend(n_ctx, n_shard, rows, heads, place, idx, normed, w_q, w_k, w_v, w_o, bias, *refs):
    s, c = idx[0], idx[1]
    groups = 1 + max((g for pieces in place.values() for g, _, _ in pieces))
    got = [refs[g * n_ctx : (g + 1) * n_ctx] for g in range(groups)]
    att_mine, att_other, soft, qkv, mixed, every, held = refs[groups * n_ctx :]
    inner, r = w_o.shape
    length = n_ctx * rows
    for i, ref in enumerate((w_q, w_k, w_v, w_o)):
        held[s, i * inner : (i + 1) * inner, :] = ref[...]
    for v in range(n_ctx):

        @pl.when(c == v)
        def _(v=v):
            for k in range(n_ctx):
                for z, pieces in place.items():
                    at, last = (v ^ k) * inner, ((v ^ k) + 1) * inner
                    for g, row, size in pieces:
                        size = min(size, last - at)
                        held[wrap(s - z, n_shard), at : at + size, :] = got[g][k][
                            row : row + size, 0:r
                        ]
                        at += size

    for j in range(n_shard):
        every[:, r * j : r * (j + 1)] = held[j]
    qkv[...] = dot_nt(normed[...], every[0 : 3 * inner, :]).astype(low)
    for m in (1, 0):
        low_row = m * length
        for h in range(heads):
            at = DK * h
            keys = qkv[low_row : low_row + length, inner + at : inner + at + DK]
            values = qkv[low_row : low_row + length, 2 * inner + at : 2 * inner + at + DK]
            for b in range(n_ctx):
                top = low_row + b * rows
                scores = dot_nt(qkv[top : top + rows, at : at + DK], keys)
                scores += bias[h, b * rows : (b + 1) * rows, :]
                raised = jnp.exp(scores - jnp.max(scores, axis=-1, keepdims=True))
                share = raised / jnp.sum(raised, axis=-1, keepdims=True)
                if b == 0:
                    soft[m, h] = share
                mixed[top : top + rows, at : at + DK] = dot_nn(share.astype(low), values).astype(low)
        out = att_mine if m == 0 else att_other
        out[...] = dot_nn(
            mixed[low_row : low_row + length, :], every[3 * inner : 4 * inner, :]
        ).astype(low)


def middle_norm(n_ctx, idx, x_in, *refs):
    mine, (att, got, gains, normed, middle_own) = refs[: n_ctx - 1], refs[n_ctx - 1 :]
    rows = x_in.shape[1]
    for k in range(n_ctx):
        at = slice(k * rows, (k + 1) * rows)
        x = x_in[idx[2]] if k == 0 else mine[k - 1][...]
        mid = x.astype(wide) + (att[at, :].astype(wide) + got[at, :].astype(wide))
        scale = lax.rsqrt(jnp.mean(mid * mid, axis=-1, keepdims=True) + norm_eps)
        normed[at, :] = (mid * scale * gains[1:2, :]).astype(low)
        if k == 0:
            middle_own[...] = mid


def unpack_wide(parts, r, buf, weights, j):
    for e, pieces in enumerate(parts):
        for row, size, top, lane, lanes, at in pieces:
            weights[e][r * j + top : r * j + top + size, lane : lane + lanes] = buf[
                j, row : row + size, at : at + lanes
            ]


def feed_forward(n_ctx, n_shard, widths, idx, buf_far, nt_mine, nt_other, cot_in, *refs):
    half = idx[2]
    n_parts = len(widths)
    mine, rest, refs = refs[: n_ctx - 1], refs[n_ctx - 1], refs[n_ctx:]
    sent, given, refs = refs[0], refs[1 : 1 + 2 * n_parts], refs[1 + 2 * n_parts :]
    buf, nt, cot, sems, sems_out = refs[:5]
    weights, hidden, pair = (refs[5 + i * n_parts : 5 + (i + 1) * n_parts] for i in range(3))
    length, _ = nt_mine.shape
    rows = length // n_ctx
    r = weights[0].shape[0] // n_shard

    def block(m, k):
        at = (m * n_ctx + k) * rows
        return slice(at, at + rows)

    begun = [pltpu.make_async_copy(buf_far.at[0], buf.at[0], sems.at[0])]
    moves = [
        (nt_mine, nt.at[0:length, :]),
        (nt_other, nt.at[length : 2 * length, :]),
        (cot_in.at[half], cot.at[block(0, 0), :]),
        (cot_in.at[1 - half], cot.at[block(1, 0), :]),
    ]
    moves += [(buf_far.at[j], buf.at[j]) for j in range(1, n_shard)]
    for k in range(1, n_ctx):
        moves.append((mine[k - 1], cot.at[block(0, k), :]))
        moves.append((rest.at[k - 1], cot.at[block(1, k), :]))
    begun += [pltpu.make_async_copy(x, y, sems.at[i + 1]) for i, (x, y) in enumerate(moves)]
    for copy in begun:
        copy.start()
    loads = [begun[0]] + begun[5 : 4 + n_shard]
    parts, _ = wide_tiles(r, widths)
    for j in range(n_shard):
        loads[j].wait()
        unpack_wide(parts, r, buf, weights, j)
    for copy in begun[1:5] + begun[4 + n_shard :]:
        copy.wait()
    c0, c1 = 0.7978845608028654, 0.044715
    out = []

    def write(source, target):
        copy = pltpu.make_async_copy(source, target, sems_out.at[len(out)])
        copy.start()
        out.append(copy)

    for m in (1, 0):
        at = slice(m * length, (m + 1) * length)
        for e, n in enumerate(widths):
            both = dot_nn(nt[at, :], weights[e][:, 0 : 2 * n])
            back = dot_nn(cot[at, :], weights[e][:, 2 * n : 3 * n])
            gate, up = both[:, :n], both[:, n:]
            square = gate * gate
            bent = jnp.tanh(c0 * (gate + c1 * gate * square))
            half_one = 0.5 * (1.0 + bent)
            active = gate * half_one
            slope = half_one + 0.5 * gate * (1.0 - bent * bent) * (c0 * (1.0 + 3.0 * c1 * square))
            hidden[e][at, :] = (active * up).astype(low)
            pair[e][at, 0:n] = (back * up * slope).astype(low)
            pair[e][at, n : 2 * n] = (back * active).astype(low)
    for source, target in zip((*hidden, *pair), given, strict=True):
        write(source, target)
    for e, n in enumerate(widths):
        for_in = dot_tn(nt[...], pair[e][...]).astype(low)
        for_down = dot_tn(cot[...], hidden[e][...]).astype(low)
        first, last = parts[e][0][0], parts[e][-1][0] + parts[e][-1][1]
        for j in range(n_shard):
            for row, size, top, lane, lanes, at in parts[e]:
                top = r * j + top
                inside = max(0, min(lanes, 2 * n - lane))
                if inside:
                    buf[j, row : row + size, at : at + inside] = for_in[
                        top : top + size, lane : lane + inside
                    ]
                if inside < lanes:
                    begin = lane + inside - 2 * n
                    buf[j, row : row + size, at + inside : at + lanes] = for_down[
                        top : top + size, begin : begin + lanes - inside
                    ]
            here = slice(first, last if e < n_parts - 1 else buf.shape[1])
            write(buf.at[j, here, :], sent.at[j, here, :])
    for copy in out:
        copy.wait()


def feed_out(n_ctx, n_shard, widths, idx, buf_far, *refs):
    n_parts = len(widths)
    far, refs = refs[: 2 * n_parts], refs[2 * n_parts :]
    feed, two, refs = refs[0:2], refs[2:4], refs[4:]
    buf, feed_held, two_held, sems, sems_out = refs[:5]
    weights, hidden, pair = (refs[5 + i * n_parts : 5 + (i + 1) * n_parts] for i in range(3))
    _, _, rows, _ = two_held.shape
    length = n_ctx * rows
    r = weights[0].shape[0] // n_shard
    parts, _ = wide_tiles(r, widths)
    moves = [(buf_far.at[j], buf.at[j]) for j in range(n_shard)]
    moves += list(zip(far, (*hidden, *pair), strict=True))
    begun = [pltpu.make_async_copy(x, y, sems.at[i]) for i, (x, y) in enumerate(moves)]
    for copy in begun:
        copy.start()
    for j in range(n_shard):
        begun[j].wait()
        unpack_wide(parts, r, buf, weights, j)
    for copy in begun[n_shard:]:
        copy.wait()
    out = []
    for held, given, lefts, first, last in (
        (two_held, two, pair, 0, 2),
        (feed_held, feed, hidden, 2, 3),
    ):
        for m in (1, 0):
            at = slice(m * length, (m + 1) * length)
            total = sum(
                (
                    dot_nt(lefts[e][at, :], weights[e][:, first * n : last * n])
                    for e, n in enumerate(widths)
                )
            )
            for i in range(n_ctx):
                held[m, i] = total[i * rows : (i + 1) * rows].astype(low)
            copy = pltpu.make_async_copy(held.at[m], given[m], sems_out.at[len(out)])
            copy.start()
            out.append(copy)
    for copy in out:
        copy.wait()


def norm_two_back(n_shard, n_parts, idx, cot_in, *refs):
    parts, refs = refs[:n_parts], refs[n_parts:]
    middle, gains, out_in, grad, gain_grad = refs
    r = gain_grad.shape[2]
    mid = middle[...]
    two = sum((p[...].astype(wide) for p in parts))
    scale = lax.rsqrt(jnp.mean(mid * mid, axis=-1, keepdims=True) + norm_eps)
    u = two * gains[1:2, :]
    inner = jnp.mean(u * mid, axis=-1, keepdims=True) * (scale * scale * scale)
    back = cot_in[idx[2]].astype(wide) + scale * u - mid * inner
    grad[...] = back
    out_in[...] = back.astype(low)
    total = jnp.sum(two * mid * scale, axis=0, keepdims=True)
    for j in range(n_shard):
        gain_grad[j] = total[:, r * j : r * (j + 1)]


def attend_back(n_ctx, heads, idx, o_mine, o_other, soft, qkv, every, mixed, *refs):
    kv, for_out, (q_grad, kv_all, mixed_grad) = refs[:n_ctx], refs[n_ctx : 2 * n_ctx], refs[2 * n_ctx :]
    rows = o_mine.shape[0]
    length = n_ctx * rows
    inner = heads * DK
    share_rows = for_out[0].shape[0]
    for m, o_in in ((0, o_mine), (1, o_other)):
        top, own = m * length, m * rows
        mixed_grad[own : own + rows, :] = dot_nt(o_in[...], every[3 * inner :, :]).astype(low)
        for h in range(heads):
            at = DK * h
            share = soft[m, h]
            grad = mixed_grad[own : own + rows, at : at + DK]
            keys = qkv[top : top + length, inner + at : inner + at + DK]
            values = qkv[top : top + length, 2 * inner + at : 2 * inner + at + DK]
            queries = qkv[top : top + rows, at : at + DK]
            weight = dot_nt(grad, values)
            ds = share * (weight - jnp.sum(weight * share, axis=-1, keepdims=True))
            ds = ds.astype(low)
            q_grad[own : own + rows, at : at + DK] = dot_nn(ds, keys).astype(low)
            kv_all[top : top + length, at : at + DK] = dot_tn(ds, queries).astype(low)
            kv_all[top : top + length, inner + at : inner + at + DK] = dot_tn(
                share.astype(low), grad
            ).astype(low)
        for k in range(n_ctx):
            kv[k][own : own + rows, :] = kv_all[top + k * rows : top + (k + 1) * rows, :]
    got = dot_tn(mixed[0:rows, :], o_mine[...])
    got += dot_tn(mixed[length : length + rows, :], o_other[...])
    got = got.astype(low)
    for v in range(n_ctx):

        @pl.when(idx[1] == v)
        def _(v=v):
            for k in range(n_ctx):
                for_out[k][...] = got[(v ^ k) * share_rows : ((v ^ k) + 1) * share_rows, :]


def first_grad(n_ctx, idx, *refs):
    parts, (q_grad, every, out_mine, out_other), pieces, three = (
        refs[:n_ctx],
        refs[n_ctx : n_ctx + 4],
        refs[n_ctx + 4 : 2 * n_ctx + 4],
        refs[2 * n_ctx + 4],
    )
    rows2, inner = q_grad.shape
    rows = rows2 // 2
    size = inner // n_ctx
    three[:, 0:inner] = q_grad[...]
    three[:, inner:] = sum((p[...].astype(wide) for p in parts)).astype(low)
    for v in range(n_ctx):

        @pl.when(idx[1] == v)
        def _(v=v):
            for k in range(n_ctx):
                for i in range(3):
                    at = i * inner + (v ^ k) * size
                    pieces[k][:, i * size : (i + 1) * size] = three[:, at : at + size]

    got = dot_nn(three[...], every[0 : 3 * inner, :]).astype(low)
    out_mine[...] = got[0:rows]
    out_other[...] = got[rows:]


def weight_grads(n_ctx, n_shard, idx, normed, *refs):
    pieces, for_out, refs = refs[:n_ctx], refs[n_ctx : 2 * n_ctx], refs[2 * n_ctx :]
    gain_one, gain_two, stack, grads, held, sem = refs
    s = idx[0]
    copy = pltpu.make_async_copy(normed, held, sem)
    copy.start()
    size, r = for_out[0].shape[0], stack.shape[2]
    rows = pieces[0].shape[0] // 2
    out_rows = sum((p[...].astype(wide) for p in for_out))
    for j in range(n_shard):
        d = wrap(j - s, n_shard)
        stack[d, 3 * size : 4 * size, :] = out_rows[:, r * j : r * (j + 1)].astype(low)
        stack[d, 4 * size : 4 * size + 1, :] = gain_one[j].astype(low)
        stack[d, 4 * size + 1 : 4 * size + 2, :] = gain_two[j].astype(low)
    for m in range(2):
        for k in range(n_ctx):
            at = (m * n_ctx + k) * rows
            grads[at : at + rows, :] = pieces[k][m * rows : (m + 1) * rows, :]
    copy.wait()
    got = dot_tn(grads[...], held[...])
    for j in range(n_shard):
        stack[wrap(j - s, n_shard), 0 : 3 * size, :] = got[:, r * j : r * (j + 1)].astype(low)


def place_outputs(idx, a_mine, a_other, b_mine, b_other, a, b):
    half = idx[2]
    a[half] = a_mine[...]
    a[1 - half] = a_other[...]
    b[half] = b_mine[...]
    b[1 - half] = b_other[...]


def norm_one_back(n_shard, idx, x_in, mine, got, grad, gains, out, gain_grad):
    r = gain_grad.shape[2]
    x = x_in[idx[2]].astype(wide)
    one = mine[...].astype(wide) + got[...].astype(wide)
    scale = lax.rsqrt(jnp.mean(x * x, axis=-1, keepdims=True) + norm_eps)
    u = one * gains[0:1, :]
    inner = jnp.mean(u * x, axis=-1, keepdims=True) * (scale * scale * scale)
    out[...] = (grad[...] + scale * u - x * inner).astype(low)
    total = jnp.sum(one * x * scale, axis=0, keepdims=True)
    for j in range(n_shard):
        gain_grad[j] = total[:, r * j : r * (j + 1)]


def produce(n_parts, *refs):
    parts, (middle, out) = refs[:n_parts], refs[n_parts:]
    out[...] = (middle[...] + sum((p[...].astype(wide) for p in parts))).astype(low)


def finish_wide(period, widths, groups, idx, *refs):
    flat = [item for group in groups for item in group]
    count = sum((pieces for _, pieces, _ in flat))
    sources, refs = refs[:count], refs[count:]
    n_outs = 3
    outs, (held, sems) = refs[-2 - n_outs : -2], refs[-2:]
    r = outs[0].shape[0]
    columns = sum(widths)
    parts, rows = wide_tiles(r, widths)
    c = idx[1]
    for v in range(period):

        @pl.when(lax.rem(c, period) == v)
        def _(v=v):
            first = 0
            copies = []
            for g, group in enumerate(groups):
                taken = []
                for k, pieces, lanes_kind in group:
                    begin = ((v ^ k) % period) * columns
                    tile_low = pl.cdiv(begin, LANES) * LANES - begin
                    tile_high = (begin + columns) // LANES * LANES - begin
                    if lanes_kind == "all":
                        low_lane, high_lane = 0, columns
                    elif lanes_kind == "full":
                        low_lane, high_lane = tile_low, tile_high
                    elif tile_low:
                        low_lane, high_lane = 0, tile_low
                    else:
                        low_lane, high_lane = tile_high, columns
                    taken.append((k, pieces, low_lane, high_lane, first))
                    first += pieces
                start = min((((v ^ k) % period) * columns + lo for k, _, lo, _, _ in taken))
                stop = max((((v ^ k) % period) * columns + hi for k, _, _, hi, _ in taken))
                far = (lax.div(c, period) ^ (group[0][0] // period)) * (period * columns) + start
                for k, pieces, low_lane, high_lane, at_source in taken:
                    size_each = rows // pieces
                    begin = ((v ^ k) % period) * columns - start
                    for i, n in enumerate(widths):
                        base = sum(widths[:i])
                        for row, size, top, lane, lanes, at in parts[i]:
                            while lanes:
                                j, inside = divmod(lane, n)
                                take = min(lanes, n - inside)
                                lo = max(low_lane, base + inside)
                                hi = min(high_lane, base + inside + take)
                                skip = lo - base - inside
                                done = 0 if lo < hi else size
                                while done < size:
                                    part, here = divmod(row + done, size_each)
                                    many = min(size - done, size_each - here)
                                    held[g, j, top + done : top + done + many, begin + lo : begin + hi] = (
                                        sources[at_source + part][
                                            here : here + many, at + skip : at + skip + hi - lo
                                        ].astype(wide)
                                    )
                                    done += many
                                lane, at, lanes = lane + take, at + take, lanes - take
                for j in range(3):
                    copy = pltpu.make_async_copy(
                        held.at[g, j, :, 0 : stop - start],
                        outs[j].at[:, pl.ds(pl.multiple_of(far, LANES), stop - start)],
                        sems.at[3 * g + j],
                    )
                    copy.start()
                    copies.append(copy)
            for copy in copies:
                copy.wait()


def finish_attention(n_ctx, idx, *refs):
    pieces, (outs, gains) = refs[:n_ctx], (refs[n_ctx:-1], refs[-1])
    inner, _ = outs[0].shape
    size = inner // n_ctx
    for v in range(n_ctx):

        @pl.when(idx[1] == v)
        def _(v=v):
            for k in range(n_ctx):
                at = (v ^ k) * size
                for i in range(4):
                    outs[i][at : at + size, :] = pieces[k][i * size : (i + 1) * size, :].astype(wide)

    gains[...] = sum((p[inner : inner + 2, :].astype(wide) for p in pieces))


def on_device(
    inputs,
    cotangent,
    norm1_gain,
    w_query,
    w_key,
    w_value,
    w_out,
    norm2_gain,
    w_gate,
    w_up,
    w_down,
    bias_table,
):
    _, rows, width = inputs.shape
    shards, ctx = lax.axis_size("shard"), lax.axis_size("ctx")
    inner, r = w_out.shape
    heads = inner // DK
    length = ctx * rows
    columns = w_gate.shape[1] // ctx
    first_width = pl.cdiv(columns, 2 * LANES) * LANES
    widths = (first_width, columns - first_width)
    lanes_r = pl.cdiv(r, LANES) * LANES
    s, c, half = lax.axis_index("shard"), lax.axis_index("ctx"), lax.axis_index("tensor")
    idx = jnp.stack([s, c, half]).astype(jnp.int32)
    attention_weights = (w_query.T, w_key.T, w_value.T, w_out)


    wide_rows = wide_tiles(r, widths)[1]
    period = next(p for p in range(1, ctx + 1) if p == ctx or p * columns % LANES == 0)
    window = max(
        pl.cdiv((v + 1) * columns, LANES) * LANES - v * columns // LANES * LANES
        for v in range(period)
    )
    (packed,) = run(
        functools.partial(pack_wide, period, widths, window),
        "pack_wide",
        [((wide_rows, LANES), low)],
        [w_gate, w_up, w_down.T],
        scalars=0,
        scratch=[
            pltpu.VMEM((3, r, window), low),
            pltpu.SemaphoreType.DMA((3,)),
        ],
        cost=2,
        far=3,
        vmem=60,
    )
    chunks = lax.all_gather(packed, "shard", axis=0, tiled=False)
    own_x = lax.dynamic_index_in_dim(inputs, half, 0, keepdims=False)
    (own_buf,) = run(
        functools.partial(pack_attention, ctx),
        "pack_attention",
        [((inner + 16, lanes_r), low)],
        [after(idx, packed), *attention_weights, jnp.stack([norm1_gain, norm2_gain])],
        scratch=[pltpu.VMEM((inner, r), low), pltpu.SemaphoreType.DMA],
        far=4,
        vmem=60,
    )
    if shards == 4:
        low_one, high_one = step(own_buf, "shard", 1), step(own_buf, "shard", -1)
        middle = own_buf.shape[0] // 2
        far = [step(low_one[:middle], "shard", 1), step(high_one[middle:], "shard", -1)]
        from_shard = [low_one, jnp.concatenate(far), high_one]
    else:
        from_shard = [step(own_buf, "shard", k) for k in range(1, shards)]
    table = lax.dynamic_slice_in_dim(bias_table, half * heads, heads, 1)
    (bias,) = run(
        functools.partial(bias_body, rows, rows // 5, distance_marks),
        "bias",
        [((heads, length, length), wide)],
        [after(idx, own_buf), table],
        scalars=2,
        cost=5,
    )
    mine_x = [swap(after(own_x, bias), "ctx", k) for k in range(1, ctx)]
    now = after(idx, *from_shard, *mine_x, bias)

    group = jnp.concatenate(from_shard)
    buf_rows = inner + 16
    place = {z: [(0, (z - 1) * buf_rows, inner)] for z in range(1, shards)}
    gathered = [group] + [swap(after(group, now), "ctx", k) for k in range(1, ctx)]
    rest_x = swap(after(jnp.stack(mine_x), now), "tensor")
    normed_one, gains = run(
        functools.partial(norm_one, ctx, shards),
        "norm_one",
        [((2 * length, width), low), ((2, width), wide)],
        [now, inputs, *mine_x, rest_x, own_buf, *from_shard],
        scratch=[pltpu.VMEM((shards, 8, r), wide)],
        cost=3,
    )
    now = after(now, *gathered[1:], normed_one)

    own_cot = lax.dynamic_index_in_dim(cotangent, half, 0, keepdims=False)
    mine_cot = [swap(after(own_cot, now), "ctx", k) for k in range(1, ctx)]
    att_mine, att_other, soft, qkv, mixed, every = run(
        functools.partial(attend, ctx, shards, rows, heads, place),
        "attend",
        [
            ((length, width), low),
            ((length, width), low),
            ((2, heads, rows, length), wide),
            ((2 * length, 3 * inner), low),
            ((2 * length, inner), low),
            ((4 * inner, width), low),
        ],
        [now, normed_one, *attention_weights, bias, *gathered],
        scratch=[pltpu.VMEM((shards, 4 * inner, r), low)],
        cost=14,
        vmem=24,
    )
    now = after(now, *mine_cot, att_other)

    att_got = swap(after(att_other, now), "tensor")
    rest_cot = swap(after(jnp.stack(mine_cot), now), "tensor")
    nt_mine, middle_own = run(
        functools.partial(middle_norm, ctx),
        "middle_norm",
        [((length, width), low), ((rows, width), wide)],
        [now, inputs, *mine_x, att_mine, att_got, gains],
    )
    nt_other = swap(nt_mine, "tensor")
    now = after(now, nt_other, rest_cot)

    def add(a, b):
        return (a.astype(wide) + b.astype(wide)).astype(low)

    tokens_out = ((ctx, rows, width), low)
    units = [((2 * length, n), low) for n in (*widths, *(2 * n for n in widths))]
    unit_scratch = [pltpu.VMEM(shape, kind) for shape, kind in units]
    weight_scratch = [pltpu.VMEM((width, 3 * n), low) for n in widths]
    wide_grads, *units = run(
        functools.partial(feed_forward, ctx, shards, widths),
        "feed_forward",
        [((shards, wide_rows, LANES), low), *units],
        [now, chunks, nt_mine, nt_other, cotangent, *mine_cot, rest_cot],
        scratch=[
            pltpu.VMEM((shards, wide_rows, LANES), low),
            pltpu.VMEM((2 * length, width), low),
            pltpu.VMEM((2 * length, width), low),
            pltpu.SemaphoreType.DMA((3 + shards + 2 * ctx,)),
            pltpu.SemaphoreType.DMA(((2 + shards) * len(widths),)),
            *weight_scratch,
            *unit_scratch,
        ],
        far=5 + ctx - 1,
        far_out=True,
        cost=14,
        vmem=60,
    )
    wide_own = lax.psum_scatter(wide_grads, "shard", scatter_dimension=0, tiled=False)
    feed_mine, feed_other, two_mine, two_other = run(
        functools.partial(feed_out, ctx, shards, widths),
        "feed_out",
        [tokens_out] * 4,
        [now, chunks, *units],
        scratch=[
            pltpu.VMEM((shards, wide_rows, LANES), low),
            pltpu.VMEM((2, ctx, rows, width), low),
            pltpu.VMEM((2, ctx, rows, width), low),
            pltpu.SemaphoreType.DMA((shards + 2 * len(widths),)),
            pltpu.SemaphoreType.DMA((4,)),
            *weight_scratch,
            *unit_scratch,
        ],
        far=1 + 2 * len(widths),
        far_out=True,
        cost=5,
        vmem=60,
    )
    now = after(now, two_other)

    two_got = swap(after(two_other, now), "tensor")
    two_both = [add(two_mine[k], two_got[k]) for k in range(ctx)]
    two_parts = [two_both[0]] + [swap(two_both[k], "ctx", k) for k in range(1, ctx)]
    out_in, middle_grad, gain_two = run(
        functools.partial(norm_two_back, shards, ctx),
        "norm_two_back",
        [((rows, width), low), ((rows, width), wide), ((shards, 1, r), wide)],
        [now, cotangent, *two_parts, middle_own, gains],
    )
    out_in_other = swap(out_in, "tensor")
    now = after(now, out_in_other)

    feed_got = swap(after(feed_other, now), "tensor")
    got = run(
        functools.partial(attend_back, ctx, heads),
        "attend_back",
        [((2 * rows, 2 * inner), low)] * ctx
        + [((inner // ctx, width), low)] * ctx
        + [((2 * rows, inner), low)],
        [now, out_in, out_in_other, soft, qkv, every, mixed],
        scratch=[pltpu.VMEM((2 * length, 2 * inner), low), pltpu.VMEM((2 * rows, inner), low)],
        cost=4,
        vmem=24,
    )
    kv_parts, for_out, q_grad = got[:ctx], got[ctx : 2 * ctx], got[2 * ctx]
    now = after(now, feed_got, q_grad)

    kv_parts = [kv_parts[0]] + [swap(after(kv_parts[k], now), "ctx", k) for k in range(1, ctx)]
    for_out = [for_out[0]] + [swap(after(for_out[k], now), "ctx", k) for k in range(1, ctx)]
    got = run(
        functools.partial(first_grad, ctx),
        "first_grad",
        [((rows, width), low)] * 2 + [((2 * rows, 3 * inner // ctx), low)] * ctx,
        [now, *kv_parts, q_grad, every],
        scratch=[pltpu.VMEM((2 * rows, 3 * inner), low)],
    )
    first_mine, first_other, pieces = got[0], got[1], got[2:]
    now = after(now, first_other)

    pieces = [pieces[0]] + [swap(after(pieces[k], now), "ctx", k) for k in range(1, ctx)]
    first_got = swap(after(first_other, now), "tensor")
    input_mine, gain_one = run(
        functools.partial(norm_one_back, shards),
        "norm_one_back",
        [((rows, width), low), ((shards, 1, r), wide)],
        [now, inputs, first_mine, first_got, middle_grad, gains],
    )
    feed_both = [add(after(feed_mine, now)[k], feed_got[k]) for k in range(ctx)]
    feed_parts = [feed_both[0]] + [swap(feed_both[k], "ctx", k) for k in range(1, ctx)]
    now = after(now, *pieces[1:], *for_out[1:], *feed_parts[1:], input_mine)
    (four,) = run(
        functools.partial(weight_grads, ctx, shards),
        "weight_grads",
        [((shards, inner + 16, r), low)],
        [now, normed_one, *pieces, *for_out, gain_one, gain_two],
        scratch=[
            pltpu.VMEM((2 * length, 3 * inner // ctx), low),
            pltpu.VMEM((2 * length, width), low),
            pltpu.SemaphoreType.DMA,
        ],
        far=1,
        cost=2,
        vmem=24,
    )
    now = after(now, four, input_mine)

    (produced_mine,) = run(
        functools.partial(produce, ctx),
        "produce",
        [((rows, width), low)],
        [*feed_parts, middle_own],
        scalars=0,
    )
    now = after(now, wide_own, produced_mine, input_mine)

    wide_own = after(wide_own, now)
    half_rows = wide_rows // 2
    pair = ctx == 4
    wide_all = [swap(wide_own, "ctx", k) for k in ((1, 2) if pair else range(1, ctx))]
    four_shard = [four[0]] + [step(after(four[d], now), "shard", d) for d in range(1, shards)]
    input_other = swap(after(input_mine, now), "tensor")
    produced_other = swap(after(produced_mine, now), "tensor")
    out_y, out_x = run(
        place_outputs,
        "place_outputs",
        [(inputs.shape, low)] * 2,
        [now, produced_mine, produced_other, input_mine, input_other],
    )
    four_shard = [four[0]] + [after(part, out_y) for part in four_shard[1:]]
    four_own = sum((part.astype(wide) for part in four_shard)).astype(low)
    four_all = [four_own] + [swap(after(four_own, now), "ctx", k) for k in range(1, ctx)]
    now = after(now, *wide_all, *four_all[1:])

    far_halves = []
    if pair:
        far_halves = [
            swap(after(wide_all[0], now)[:half_rows], "ctx", 2),
            swap(after(wide_all[1], now)[half_rows:], "ctx", 1),
        ]
    out_q, out_k, out_v, out_o, own_gain = run(
        functools.partial(finish_attention, ctx),
        "finish_attention",
        [((inner, r), wide)] * 4 + [((2, r), wide)],
        [now, *four_all],
    )
    own_gain = own_gain + swap(own_gain, "tensor")

    pairs = pair and period <= 2
    period = 2 if pairs else ctx

    def finish(now, groups, sources, span, before):
        return run(
            functools.partial(finish_wide, period, widths, groups),
            "finish_wide",
            [(w_gate.shape, wide)] * 3,
            [now, *sources, *before],
            scratch=[
                pltpu.VMEM((len(groups), 3, r, span), wide),
                pltpu.SemaphoreType.DMA((3 * len(groups),)),
            ],
            far_out=True,
            into=len(before),
            cost=3,
            vmem=24,
        )

    if pairs:
        groups = [[(0, 1, "all"), (1, 1, "all")], [(2, 1, "full")]]
        outs = finish(now, groups, [wide_own, *wide_all], 2 * columns, [])
        now = after(now, *far_halves, outs[0], own_gain)
        groups = [[(2, 1, "rest"), (3, 2, "all")]]
        outs = finish(now, groups, [wide_all[1], *far_halves], 2 * columns, outs)
    else:
        groups = [[(k, 1, "all") for k in range(ctx)]]
        outs = finish(now, groups, [wide_own, *wide_all], ctx * columns, [])
    out_g, out_u, out_d = outs

    return (
        out_y,
        out_x,
        own_gain[0],
        out_q.T,
        out_k.T,
        out_v.T,
        out_o,
        own_gain[1],
        out_g,
        out_u,
        out_d.T,
    )


def solution(mesh):
    placed = (
        P(None, ("shard", "ctx"), None),
        P(None, ("shard", "ctx"), None),
        P("shard"),
        P("shard", "tensor"),
        P("shard", "tensor"),
        P("shard", "tensor"),
        P("tensor", "shard"),
        P("shard"),
        P("shard", "tensor"),
        P("shard", "tensor"),
        P("tensor", "shard"),
        P(),
    )
    return jax.shard_map(
        on_device, mesh=mesh, in_specs=placed, out_specs=placed[:2] + placed[2:11], check_vma=False
    )
```
